32 devices in a mesh: dp: 8 (over z, y), mp: 4 (over x, core).
Axes of the slice: x: 2, y: 2, z: 4, core: 2. Of those that a mesh axis runs over, the one named last changes fastest.
Arguments:
- tokens: bfloat16 [32768, 512], P(('dp', 'mp')), may hold values from -6 to 6
- segment_ids: int32 [32, 1024], P('dp'), may hold values from 0 to 22, as said below
- cotangent: bfloat16 [32768, 512], P(('dp', 'mp')), may hold values from -6 to 6
- step_count: int32 [1], replicated, may hold values from 2 to 20
- mixer_weights: float32 [512, 4, 512], P('dp', None, 'mp')
- mixer_moment: float32 [512, 4, 512], P('dp', None, 'mp')
- mixer_second: float32 [512, 4, 512], P('dp', None, 'mp')
- feed_weights: float32 [512, 2, 2048], P('dp', None, 'mp')
- feed_moment: float32 [512, 2, 2048], P('dp', None, 'mp')
- feed_second: float32 [512, 2, 2048], P('dp', None, 'mp')
- sorter_weights: float32 [512, 256], P('dp', 'mp'), may hold values from -1.5 to 1.5
- sorter_moment: float32 [512, 256], P('dp', 'mp')
- sorter_second: float32 [512, 256], P('dp', 'mp')
- norm_gains: float32 [2, 512], P(None, ('dp', 'mp')), may hold values from 0.5 to 1.5
- gain_moment: float32 [2, 512], P(None, ('dp', 'mp'))
- gain_second: float32 [2, 512], P(None, ('dp', 'mp'))
Outputs:
- block_output: bfloat16 [32768, 512], P(('dp', 'mp'))
- token_grad: float32 [32768, 512], P(('dp', 'mp'))
- penalty: float32 [1], replicated
- mixer_momentum: float32 [512, 4, 512], P('dp', None, 'mp')
- mixer_variance: float32 [512, 4, 512], P('dp', None, 'mp')
- mixer_master: float32 [512, 4, 512], P('dp', None, 'mp')
- feed_momentum: float32 [512, 2, 2048], P('dp', None, 'mp')
- feed_variance: float32 [512, 2, 2048], P('dp', None, 'mp')
- feed_master: float32 [512, 2, 2048], P('dp', None, 'mp')
- sorter_momentum: float32 [512, 256], P('dp', 'mp')
- sorter_variance: float32 [512, 256], P('dp', 'mp')
- sorter_master: float32 [512, 256], P('dp', 'mp')
- gain_momentum: float32 [2, 512], P(None, ('dp', 'mp'))
- gain_variance: float32 [2, 512], P(None, ('dp', 'mp'))
- gain_master: float32 [2, 512], P(None, ('dp', 'mp'))
The draws below stay inside these ranges and needn't reach their ends.
Inputs may be any that keep to these rules, and one draw needn't show every extreme that they name: `segment_ids`: 0 marks padding, which only follows the sentences at the end of a sequence; nonzero ids never fall along a sequence.
All inputs are finite; a program needn't handle non-finite values.
Results may differ from the reference program's by a relative error of at most 0.028.
The reference program's roundings to bfloat16 on the way count: a program that leaves them out, or rounds other values in their place, can miss the bound.
Values may be sent and summed in bfloat16 or wider, within the bound.
A program may use at most 192 MiB of HBM per device.

```python
import math
import jax
import jax.numpy as jnp
from jax import lax

WIDTH = 512
HEADS = 8
HEAD_DIM = 64
HIDDEN_SIZE = 2048
BLOCK = 32
SINK_ITERS = 8
SEQ_LEN = 1024
SEQ_DEV = 4
SEQS = 32
TOKENS = 32768
BLOCKS = 32


first_share = 0.1 / 0.9


second_share = 0.05 / 0.95


def slot_factor(factors, array_rank, slot_axis):
    layout = [1] * array_rank
    layout[slot_axis] = len(factors)
    return jnp.asarray(factors, jnp.float32).reshape(tuple(layout))


def moment_draw(key, extent, factors, slot_axis):
    return jax.random.normal(key, extent, jnp.float32) * first_share * slot_factor(factors, len(extent), slot_axis)


def second_draw(key, extent, factors, slot_axis):
    spread = jnp.exp(jax.random.uniform(key, extent, jnp.float32, math.log(0.5), math.log(2.0)))
    scales = slot_factor(factors, len(extent), slot_axis)
    return 3.0 * second_share * spread * scales * scales


def block_root():
    return math.sqrt(BLOCK)


def mixer_scales():
    token_root = math.sqrt(TOKENS)
    return [6.0 / block_root() * token_root, 6.0 / block_root() * token_root, 4.0 / block_root() * token_root, 2.0 / block_root() * token_root]


def feed_scales():
    token_root = math.sqrt(TOKENS)
    return [0.7 * math.sqrt(WIDTH / HIDDEN_SIZE) * token_root, 0.7 * token_root]


def gain_scales():
    token_root = math.sqrt(TOKENS)
    return [12.0 / block_root() * token_root, 0.7 * token_root]


def sorter_scales():
    return [3.0 / BLOCK * math.sqrt(TOKENS)]


def draw_segment_ids(key, part):
    length_key, cut_key = jax.random.split(jax.random.fold_in(key, 11))
    lengths = jax.random.randint(length_key, (SEQS, SEQ_LEN), 8, 48)
    sentence_ends = jnp.cumsum(lengths, axis=1)
    positions = jnp.arange(SEQ_LEN, dtype=jnp.int32)
    sentence_ids = 1 + jax.vmap(lambda sentence_row: jnp.searchsorted(sentence_row, positions, side='right'))(sentence_ends)
    sentence_ids = jnp.minimum(sentence_ids, 1 + (SEQ_LEN - BLOCK) // 47)
    shortfall = jax.random.randint(cut_key, (SEQS, 1), 0, BLOCK)
    row_index = jnp.arange(SEQS, dtype=jnp.int32)[:, None]
    fill_length = SEQ_LEN // 4 + 3 * SEQ_LEN // 4 * row_index // max(SEQS - 1, 1) - shortfall
    return jnp.where(positions[None, :] < fill_length, sentence_ids, 0).astype(jnp.int32)


def draw_mixer_weights(key, part):
    factors = [(WIDTH / 2) ** (-0.5), (WIDTH / 2) ** (-0.5), WIDTH ** (-0.5), (WIDTH / 16) ** (-0.5)]
    return jax.random.normal(key, (WIDTH, 4, WIDTH), jnp.float32) * slot_factor(factors, 3, 1)


def draw_mixer_moment(key, part):
    return moment_draw(jax.random.fold_in(key, 21), (WIDTH, 4, WIDTH), mixer_scales(), 1)


def draw_mixer_second(key, part):
    return second_draw(jax.random.fold_in(key, 22), (WIDTH, 4, WIDTH), mixer_scales(), 1)


def draw_feed_weights(key, part):
    factors = [WIDTH ** (-0.5), HIDDEN_SIZE ** (-0.5)]
    return jax.random.normal(key, (WIDTH, 2, HIDDEN_SIZE), jnp.float32) * slot_factor(factors, 3, 1)


def draw_feed_moment(key, part):
    return moment_draw(jax.random.fold_in(key, 31), (WIDTH, 2, HIDDEN_SIZE), feed_scales(), 1)


def draw_feed_second(key, part):
    return second_draw(jax.random.fold_in(key, 32), (WIDTH, 2, HIDDEN_SIZE), feed_scales(), 1)


def draw_sorter_moment(key, part):
    return moment_draw(jax.random.fold_in(key, 51), (WIDTH, HEADS * BLOCKS), sorter_scales(), 0)


def draw_sorter_second(key, part):
    return second_draw(jax.random.fold_in(key, 52), (WIDTH, HEADS * BLOCKS), sorter_scales(), 0)


def draw_gain_moment(key, part):
    return moment_draw(jax.random.fold_in(key, 41), (2, WIDTH), gain_scales(), 0)


def draw_gain_second(key, part):
    return second_draw(jax.random.fold_in(key, 42), (2, WIDTH), gain_scales(), 0)


def block_scale(rng, dims, cuts, low, largest):
    level = 1.0
    for position, parts in cuts:
        heights = jax.random.uniform(jax.random.fold_in(jax.random.fold_in(rng, 6), position), (parts,), jnp.float32, low / len(cuts), largest / len(cuts))
        level = level * jnp.repeat(jnp.exp(heights), dims[position] // parts).reshape((-1,) + (1,) * (len(dims) - 1 - position))
    return level


def bell_draw(stream_key, shape, scale, limit, shards=(), kind=jnp.bfloat16):
    result = scale * jax.random.normal(stream_key, shape, jnp.float32)
    if shards:
        result = result * block_scale(stream_key, shape, shards, -0.22, 0.18)
    return jnp.clip(result, -limit, limit).astype(kind)


def setup_inputs(seed: int = 0) -> dict:
    streams_of = jax.random.split(jax.random.key(seed), 17)
    tokens = bell_draw(streams_of[0], (TOKENS, WIDTH), 1.0, 6.0, ((0, 32),))
    segment_ids = draw_segment_ids(jax.random.fold_in(streams_of[16], 71), 0)
    cotangent = bell_draw(streams_of[2], (TOKENS, WIDTH), 1.0, 6.0, ((0, 32),))
    step_count = jax.random.randint(streams_of[3], (1,), 2, 21).astype(jnp.int32)
    mixer_weights = draw_mixer_weights(jax.random.fold_in(streams_of[16], 71), 0)
    mixer_moment = draw_mixer_moment(jax.random.fold_in(streams_of[16], 71), 0)
    mixer_second = draw_mixer_second(jax.random.fold_in(streams_of[16], 71), 0)
    feed_weights = draw_feed_weights(jax.random.fold_in(streams_of[16], 71), 0)
    feed_moment = draw_feed_moment(jax.random.fold_in(streams_of[16], 71), 0)
    feed_second = draw_feed_second(jax.random.fold_in(streams_of[16], 71), 0)
    sorter_weights = bell_draw(streams_of[10], (WIDTH, HEADS * BLOCKS), (WIDTH // BLOCK) ** -0.5, 1.5, ((0, 8), (1, 4)), jnp.float32)
    sorter_moment = draw_sorter_moment(jax.random.fold_in(streams_of[16], 71), 0)
    sorter_second = draw_sorter_second(jax.random.fold_in(streams_of[16], 71), 0)
    norm_gains = jnp.clip(1.0 + 0.1 * jax.random.normal(streams_of[13], (2, WIDTH), jnp.float32), 0.5, 1.5)
    gain_moment = draw_gain_moment(jax.random.fold_in(streams_of[16], 71), 0)
    gain_second = draw_gain_second(jax.random.fold_in(streams_of[16], 71), 0)
    return dict(tokens=tokens, segment_ids=segment_ids, cotangent=cotangent, step_count=step_count, mixer_weights=mixer_weights, mixer_moment=mixer_moment, mixer_second=mixer_second, feed_weights=feed_weights, feed_moment=feed_moment, feed_second=feed_second, sorter_weights=sorter_weights, sorter_moment=sorter_moment, sorter_second=sorter_second, norm_gains=norm_gains, gain_moment=gain_moment, gain_second=gain_second)


norm_eps = 1e-05
softness_factor = 0.75
excluded_fill = -1000000000.0
penalty_weight = 0.1
beta_first = 0.9
beta_second = 0.95
adam_eps = 1e-08
weight_decay = 0.1
rate_mixer = 0.2
rate_feed = 0.1
rate_sorter = 0.6
rate_gains = 1.0
highest = lax.Precision.HIGHEST

@jax.custom_vjp
def low(v):
    return lax.optimization_barrier(v.astype(jnp.bfloat16)).astype(jnp.float32)

@jax.custom_vjp
def low_back(v):
    return v

def low_keep(v):
    return (low(v), None)

def low_pass(kept, grad):
    return (grad,)

def back_keep(v):
    return (v, None)

def back_low(kept, grad):
    return (low(grad),)
low.defvjp(low_keep, low_pass)
low_back.defvjp(back_keep, back_low)

def rounded(value):
    return low_back(low(value))

def layer_norm(block_rows, gain):
    centred = block_rows - lax.optimization_barrier(jnp.mean(block_rows, axis=-1, keepdims=True))
    variance = lax.optimization_barrier(jnp.mean(centred * centred, axis=-1, keepdims=True))
    return centred * lax.rsqrt(variance + norm_eps) * gain

def balancing_terms(logit_matrix, permitted_pairs, genuine_rows):
    present_iterate = jnp.where(permitted_pairs, logit_matrix / softness_factor, excluded_fill)
    for sweep in range(SINK_ITERS):
        present_iterate = present_iterate - jax.nn.logsumexp(present_iterate, axis=-1, keepdims=True)
        present_iterate = present_iterate - jax.nn.logsumexp(present_iterate, axis=-2, keepdims=True)
    weights = jnp.exp(present_iterate)
    sorting_entropy = -jnp.sum(jnp.where(genuine_rows, weights * present_iterate, 0.0))
    return (weights, sorting_entropy)

def block_masks(segments):
    real_blocks = segments[:, ::BLOCK] > 0
    diagonal = jnp.arange(BLOCKS)[:, None] == jnp.arange(BLOCKS)[None, :]
    permitted_pairs = real_blocks[:, None, :, None] & real_blocks[:, None, None, :] | diagonal
    return (real_blocks, permitted_pairs, real_blocks[:, None, :, None])

def token_masks(segments):
    groups = segments.shape[0]
    token_ids = segments.reshape(groups, BLOCKS, BLOCK)
    near_mask = token_ids[:, :, :, None] == token_ids[:, :, None, :]
    far_mask = jnp.broadcast_to(token_ids[:, :, :, None] > 0, near_mask.shape)
    return jnp.concatenate([near_mask, far_mask], axis=-1)[:, None]

def group_forward(params, block_rows, segments):
    mixer_low, feed_low, sorter_low, gain_rows = params
    groups = segments.shape[0]
    tile_size = BLOCK * HEAD_DIM

    def to_blocks(flat):
        return flat.reshape(groups, BLOCKS, BLOCK, HEADS, HEAD_DIM).transpose(0, 3, 1, 2, 4)
    first_in = low(layer_norm(block_rows, gain_rows[0]))
    queries = rounded(jnp.dot(first_in, mixer_low[:, 0, :], precision=highest))
    key_rows = rounded(jnp.dot(first_in, mixer_low[:, 1, :], precision=highest))
    value_rows = rounded(jnp.dot(first_in, mixer_low[:, 2, :], precision=highest))
    query_blocks = to_blocks(queries)
    key_blocks = to_blocks(key_rows)
    value_blocks = to_blocks(value_rows)
    block_means = low(lax.optimization_barrier(jnp.mean(first_in.reshape(groups, BLOCKS, BLOCK, WIDTH), axis=2)))
    sorting_logit_rows = low_back(jnp.einsum('gbd,dk->gbk', block_means, sorter_low, precision=highest))
    sorting_logit_rows = sorting_logit_rows.reshape(groups, BLOCKS, HEADS, BLOCKS).transpose(0, 2, 1, 3)
    real_blocks, permitted_pairs, genuine_rows = block_masks(segments)
    sorting_probabilities, sorting_entropy = balancing_terms(sorting_logit_rows, permitted_pairs, genuine_rows)
    probs_low = low(sorting_probabilities)
    sorted_keys = rounded(jnp.einsum('ghbc,ghcf->ghbf', probs_low, key_blocks.reshape(groups, HEADS, BLOCKS, tile_size), precision=highest))
    sorted_values = rounded(jnp.einsum('ghbc,ghcf->ghbf', probs_low, value_blocks.reshape(groups, HEADS, BLOCKS, tile_size), precision=highest))
    sorted_keys = sorted_keys.reshape(groups, HEADS, BLOCKS, BLOCK, HEAD_DIM)
    sorted_values = sorted_values.reshape(groups, HEADS, BLOCKS, BLOCK, HEAD_DIM)
    all_keys = jnp.concatenate([key_blocks, sorted_keys], axis=3)
    all_values = jnp.concatenate([value_blocks, sorted_values], axis=3)
    raw_scores = low_back(jnp.einsum('ghnie,ghnje->ghnij', query_blocks, all_keys, precision=highest))
    scores = jnp.where(token_masks(segments), raw_scores * HEAD_DIM ** (-0.5), excluded_fill)
    attention = jax.nn.softmax(scores, axis=-1)
    mixed_blocks = rounded(jnp.einsum('ghnij,ghnje->ghnie', low(attention), all_values, precision=highest))
    mixed_rows = mixed_blocks.transpose(0, 2, 3, 1, 4).reshape(groups * SEQ_LEN, WIDTH)
    branch = low_back(jnp.dot(mixed_rows, mixer_low[:, 3, :].T, precision=highest))
    middle = block_rows + branch
    second_in = low(layer_norm(middle, gain_rows[1]))
    pre_act = low_back(jnp.dot(second_in, feed_low[:, 0, :], precision=highest))
    activated = low(jax.nn.relu(pre_act))
    return (middle + jnp.dot(activated, feed_low[:, 1, :].T, precision=highest), sorting_entropy)

def forward(tokens_f, mixer, feed, sorter, gain_rows, segments, block_count):
    params = (low(mixer), low(feed), low(sorter), gain_rows)
    rows_all = tokens_f.reshape(SEQS // SEQ_DEV, SEQ_DEV * SEQ_LEN, WIDTH)
    segs_all = segments.reshape(SEQS // SEQ_DEV, SEQ_DEV, SEQ_LEN)
    group_step = jax.checkpoint(group_forward)

    def scan_step(running, inputs):
        outputs, sorting_entropy = group_step(params, inputs[0], inputs[1])
        return (running + sorting_entropy, outputs)
    running, outputs = lax.scan(scan_step, jnp.zeros((), jnp.float32), (rows_all, segs_all))
    return (outputs.reshape(TOKENS, WIDTH), running / (block_count * HEADS))

def adamw(master, moment, second, grad, rate, step_value):
    moment_new = beta_first * moment + (1.0 - beta_first) * grad
    second_new = beta_second * second + (1.0 - beta_second) * grad * grad
    first_hat = moment_new / (1.0 - beta_first ** step_value)
    second_hat = second_new / (1.0 - beta_second ** step_value)
    master_new = master - rate * (first_hat / (jnp.sqrt(second_hat) + adam_eps) + weight_decay * master)
    return (moment_new, second_new, master_new)

def reference(tokens, segment_ids, cotangent, step_count, mixer_weights, mixer_moment, mixer_second, feed_weights, feed_moment, feed_second, sorter_weights, sorter_moment, sorter_second, norm_gains, gain_moment, gain_second):
    block_count = jnp.sum((segment_ids[:, ::BLOCK] > 0).astype(jnp.float32))

    def objective(tokens_f, mixer, feed, sorter, gain_rows):
        return forward(tokens_f, mixer, feed, sorter, gain_rows, segment_ids, block_count)
    (outputs, penalty), pull = jax.vjp(objective, tokens.astype(jnp.float32), mixer_weights, feed_weights, sorter_weights, norm_gains)
    token_grad, mixer_grad, feed_grad, sorter_grad, gain_grad = pull((cotangent.astype(jnp.float32), jnp.asarray(penalty_weight * TOKENS, jnp.float32)))
    step_value = step_count[0].astype(jnp.float32)
    mixer_new = adamw(mixer_weights, mixer_moment, mixer_second, mixer_grad, rate_mixer, step_value)
    feed_new = adamw(feed_weights, feed_moment, feed_second, feed_grad, rate_feed, step_value)
    sorter_new = adamw(sorter_weights, sorter_moment, sorter_second, sorter_grad, rate_sorter, step_value)
    gain_new = adamw(norm_gains, gain_moment, gain_second, gain_grad, rate_gains, step_value)
    return (outputs.astype(jnp.bfloat16), token_grad, penalty.reshape(1), mixer_new[0], mixer_new[1], mixer_new[2], feed_new[0], feed_new[1], feed_new[2], sorter_new[0], sorter_new[1], sorter_new[2], gain_new[0], gain_new[1], gain_new[2])
```

```python
import functools
import jax
import jax.numpy as jnp
from jax import lax
from jax.sharding import PartitionSpec as P
from jax.experimental import pallas as pl
from jax.experimental.pallas import tpu as pltpu

WIDTH = 512
HEADS = 8
HEAD_DIM = 64
HIDDEN = 2048
BLOCK = 32
SINK_ITERS = 8
SEQ_LEN = 1024
BLOCKS = 32
LOGITS = HEADS * BLOCKS
ROWS = 256
TILES = SEQ_LEN // ROWS
PACK = 4
GROUPS = HEADS // PACK
LANES = PACK * HEAD_DIM
PAIRS = PACK * BLOCK

norm_eps = 1e-05
softness_factor = 0.75
excluded_fill = -1000000000.0
penalty_weight = 0.1
bf16 = jnp.bfloat16
f32 = jnp.float32


def mm(a, b, ca=1, cb=0):
    return lax.dot_general(a, b, (((ca,), (cb,)), ((), ())), preferred_element_type=f32)


def iota(shape, dim):
    return lax.broadcasted_iota(jnp.int32, shape, dim)


def normalize(rows):
    centred = rows - jnp.mean(rows, axis=-1, keepdims=True)
    inverse = lax.rsqrt(jnp.mean(centred * centred, axis=-1, keepdims=True) + norm_eps)
    return centred * inverse, inverse


def norm_back(grad_out, normed, inverse, gain):
    scaled = grad_out * gain
    return inverse * (
        scaled
        - jnp.mean(scaled, axis=-1, keepdims=True)
        - normed * jnp.mean(scaled * normed, axis=-1, keepdims=True)
    )


def three_parts(value):
    high = value.astype(bf16)
    rest = value - high.astype(f32)
    mid = rest.astype(bf16)
    low = (rest - mid.astype(f32)).astype(bf16)
    return high, mid, low


def group_matrix():
    return (iota((LOGITS, LOGITS), 0) // BLOCKS == iota((LOGITS, LOGITS), 1) // BLOCKS).astype(bf16)


def exact_dot(value, matrix):
    rows = value.shape[0]
    out = mm(jnp.concatenate(three_parts(value), axis=0), matrix)
    return out[:rows] + out[rows : 2 * rows] + out[2 * rows :]


def head_max(value):
    lane_head = iota(value.shape, 1) // BLOCKS
    out = jnp.zeros_like(value)
    for head in range(HEADS):
        here = lane_head == head
        top = jnp.max(jnp.where(here, value, -jnp.inf), axis=1, keepdims=True)
        out = jnp.where(here, top, out)
    return out


def permitted(real_col, real_row):
    col = iota((BLOCKS, LOGITS), 1) % BLOCKS
    return ((real_col * real_row) > 0) | (iota((BLOCKS, LOGITS), 0) == col)


def sinkhorn(logits, allowed, groups, store):
    logs = jnp.where(allowed, logits / softness_factor, excluded_fill)
    top = head_max(logs)
    logs = logs - (top + jnp.log(exact_dot(jnp.exp(logs - top), groups)))
    store(0, jnp.exp(logs))
    top = jnp.max(logs, axis=0, keepdims=True)
    logs = logs - (top + jnp.log(jnp.sum(jnp.exp(logs - top), axis=0, keepdims=True)))
    weights = jnp.exp(logs)
    store(1, weights)
    for sweep in range(1, SINK_ITERS):
        logs = logs - jnp.log(exact_dot(weights, groups))
        weights = jnp.exp(logs)
        store(2 * sweep, weights)
        logs = logs - jnp.log(jnp.sum(weights, axis=0, keepdims=True))
        weights = jnp.exp(logs)
        store(2 * sweep + 1, weights)
    return logs, weights


def sinkhorn_back(grad, groups, load):
    for sweep in reversed(range(SINK_ITERS)):
        grad = grad - load(2 * sweep + 1) * jnp.sum(grad, axis=0, keepdims=True)
        grad = grad - load(2 * sweep) * exact_dot(grad, groups)
    return grad


def by_head(tile):
    rows = jnp.concatenate([tile] * HEADS, axis=0)
    keep = iota((LOGITS, WIDTH), 0) // BLOCKS == iota((LOGITS, WIDTH), 1) // HEAD_DIM
    return jnp.where(keep, rows, jnp.zeros_like(rows))


def by_pack(tile):
    rows = jnp.concatenate([tile] * PACK, axis=0)
    keep = iota((PAIRS, LANES), 0) // BLOCK == iota((PAIRS, LANES), 1) // HEAD_DIM
    return jnp.where(keep, rows, jnp.zeros_like(rows))


def own_heads(product):
    lane_head = iota((BLOCK, LANES), 1) // HEAD_DIM
    out = product[:BLOCK]
    for head in range(1, PACK):
        out = jnp.where(lane_head == head, product[head * BLOCK : (head + 1) * BLOCK], out)
    return out


CHUNK = 128
CHUNKS = WIDTH // CHUNK


def take(ref, rows, low=0, count=CHUNKS):
    return jnp.concatenate([ref[part, rows, :] for part in range(low, low + count)], axis=1)


def put(ref, rows, value, low=0):
    for part in range(value.shape[1] // CHUNK):
        ref[low + part, rows, :] = value[:, part * CHUNK : (part + 1) * CHUNK]


MESH = pl.DeviceIdType.MESH


class Layout:
    def __init__(self, mesh_dp, mesh_mp):
        self.dp, self.mp = mesh_dp, mesh_mp
        self.C = 2 if mesh_mp % 2 == 0 else 1
        self.X = mesh_mp // self.C
        self.L = 2 if mesh_dp % 2 == 0 else 1
        self.H = mesh_dp // self.L

    def here(self):
        dp, mp = lax.axis_index("dp"), lax.axis_index("mp")
        return dp // self.L, dp % self.L, mp // self.C, mp % self.C


class Item:
    def __init__(self, lay, J, r, c):
        self.lay, self.J, self.r, self.c = lay, J, r, c
        self.direct = c % 128 == 0
        self.half = r // 2

    def shard(self):
        return (self.J, self.r, self.c)

    def dims(self, *lead, rows=None, wide=None):
        rows = self.r if rows is None else rows
        wide = self.lay.mp if wide is None else wide
        if self.direct:
            return (self.J, *lead, rows, wide * self.c)
        return (self.J, *lead, wide, rows, self.c)

    def full(self):
        return self.dims(self.lay.H, self.lay.L)

    def at(self, lead, m, rows=slice(None)):
        if self.direct:
            cols = slice(None) if m is None else pl.ds(pl.multiple_of(m * self.c, 128), self.c)
            return (slice(None), *lead, rows, cols)
        return (slice(None), *lead, slice(None) if m is None else m, rows, slice(None))

    def rows_a(self):
        return slice(0, self.half)

    def rows_b(self):
        return slice(self.half, self.r)


ALLR = slice(None)


class Sems:
    def __init__(self, send, recv):
        self.send, self.recv, self.used = send, recv, 0

    def copy(self, src, dst, device):
        index = self.used
        self.used += 1
        return pltpu.make_async_remote_copy(
            src_ref=src,
            dst_ref=dst,
            send_sem=self.send.at[index],
            recv_sem=self.recv.at[index],
            device_id=device,
            device_id_type=MESH,
        )


def begin(copies):
    for copy in copies:
        copy.start()
    return copies


def arrive(copies):
    for copy in copies:
        copy.wait_recv()


class Gather:
    def __init__(self, item, shard, full, sems):
        self.item, self.shard, self.full, self.sems = item, shard, full, sems
        self.sent = []

    def stage(self, number):
        item, lay, full = self.item, self.item.lay, self.full
        h, l, x, c = lay.here()
        mp = x * lay.C + c
        copies = []

        def to(hh, ll, xx, cc):
            return (hh * lay.L + ll, xx * lay.C + cc)

        def same(index, device):
            copies.append(self.sems.copy(full.at[index], full.at[index], device))

        if number == 0:
            for k in range(1, lay.H):
                copies.append(
                    self.sems.copy(self.shard, full.at[item.at((h, l), mp)], to((h + k) % lay.H, l, x, c))
                )
        if number == 1:
            for k in range(1, lay.L):
                same(item.at((ALLR, l), mp, item.rows_a()), to(h, (l + k) % lay.L, x, c))
            for k in range(1, lay.X):
                same(item.at((ALLR, l), mp, item.rows_b()), to(h, l, (x + k) % lay.X, c))
        if number == 2:
            for k in range(1, lay.X):
                same(item.at((ALLR, ALLR), mp, item.rows_a()), to(h, l, (x + k) % lay.X, c))
            for k in range(1, lay.L):
                for part in range(lay.X):
                    same(item.at((ALLR, l), part * lay.C + c, item.rows_b()), to(h, (l + k) % lay.L, x, c))
        if number == 3:
            for k in range(1, lay.C):
                for part in range(lay.X):
                    same(item.at((ALLR, ALLR), part * lay.C + c), to(h, l, x, (c + k) % lay.C))
        self.sent += begin(copies)
        self.flying = copies

    def place(self):
        h, l, x, c = self.item.lay.here()
        self.full[self.item.at((h, l), x * self.item.lay.C + c)] = self.shard[...]

    def landed(self):
        arrive(self.flying)

    def close(self):
        for copy in self.sent:
            copy.wait_send()

    @staticmethod
    def count(lay):
        return (lay.H - 1) + (lay.L - 1) + (lay.X - 1) * 2 + (lay.L - 1) * lay.X + (lay.C - 1) * lay.X


class Scatter:
    def __init__(self, item, full, buffers, out, sems):
        self.item, self.full, self.out, self.sems = item, full, out, sems
        self.core, self.one_a, self.one_b, self.two_a, self.two_b, self.top_a, self.top_b = buffers
        self.sent = []

    @staticmethod
    def buffers(item):
        lay = item.lay
        half = item.half
        return [
            pltpu.VMEM((lay.C - 1, *item.dims(lay.H, lay.L, wide=lay.X)), bf16),
            pltpu.VMEM((lay.X - 1, *item.dims(lay.H, lay.L, rows=half, wide=1)), bf16),
            pltpu.VMEM((lay.L - 1, *item.dims(lay.H, rows=half, wide=lay.X)), bf16),
            pltpu.VMEM((lay.L - 1, *item.dims(lay.H, rows=half, wide=1)), bf16),
            pltpu.VMEM((lay.X - 1, *item.dims(lay.H, rows=half, wide=1)), bf16),
            pltpu.VMEM((lay.H - 1, *item.dims(rows=half, wide=1)), bf16),
            pltpu.VMEM((lay.H - 1, *item.dims(rows=half, wide=1)), bf16),
        ]

    def stage(self, number):
        item, lay = self.item, self.item.lay
        h, l, x, c = lay.here()
        copies = []

        def to(hh, ll, xx, cc):
            return (hh * lay.L + ll, xx * lay.C + cc)

        def send(src, src_index, dst, dst_index, device):
            copies.append(self.sems.copy(src.at[src_index], dst.at[dst_index], device))

        if number == 0:
            for k in range(1, lay.C):
                cc = (c + k) % lay.C
                for part in range(lay.X):
                    send(
                        self.full, item.at((ALLR, ALLR), part * lay.C + cc),
                        self.core, (k - 1, *item.at((ALLR, ALLR), part)),
                        to(h, l, x, cc),
                    )
        if number == 1:
            for k in range(1, lay.X):
                xx = (x + k) % lay.X
                send(
                    self.core, (0, *item.at((ALLR, ALLR), xx, item.rows_a())),
                    self.one_a, (k - 1, *item.at((ALLR, ALLR), 0)),
                    to(h, l, xx, c),
                )
            for k in range(1, lay.L):
                ll = (l + k) % lay.L
                send(
                    self.core, (0, *item.at((ALLR, ll), None, item.rows_b())),
                    self.one_b, (k - 1, *item.at((ALLR,), None)),
                    to(h, ll, x, c),
                )
        if number == 2:
            for k in range(1, lay.L):
                ll = (l + k) % lay.L
                send(
                    self.one_a, (0, *item.at((ALLR, ll), 0)),
                    self.two_a, (k - 1, *item.at((ALLR,), 0)),
                    to(h, ll, x, c),
                )
            for k in range(1, lay.X):
                xx = (x + k) % lay.X
                send(
                    self.one_b, (0, *item.at((ALLR,), xx)),
                    self.two_b, (k - 1, *item.at((ALLR,), 0)),
                    to(h, l, xx, c),
                )
        if number == 3:
            for k in range(1, lay.H):
                hh = (h + k) % lay.H
                for src, dst in ((self.two_a, self.top_a), (self.two_b, self.top_b)):
                    send(src, (0, *item.at((hh,), 0)), dst, (k - 1, *item.at((), 0)), to(hh, l, x, c))
        self.sent += begin(copies)
        self.flying = copies

    def fold(self, number):
        item, lay = self.item, self.item.lay
        h, l, x, c = lay.here()
        arrive(self.flying)

        def over_high(body):
            def step(high, carry):
                body(high)
                return carry

            lax.fori_loop(0, lay.H, step, 0)

        def add(target, index, source, source_index, extra):
            total = source[source_index].astype(f32) + target[(0, *index)].astype(f32)
            for other in range(1, extra):
                total = total + target[(other, *index)].astype(f32)
            target[(0, *index)] = total.astype(bf16)

        if number == 0:

            def core(high):
                for low in range(lay.L):
                    for part in range(lay.X):
                        add(
                            self.core, item.at((high, low), part),
                            self.full, item.at((high, low), part * lay.C + c), lay.C - 1,
                        )

            over_high(core)
        if number == 1:

            def one(high):
                for low in range(lay.L):
                    add(
                        self.one_a, item.at((high, low), 0),
                        self.core, (0, *item.at((high, low), x, item.rows_a())), lay.X - 1,
                    )
                add(
                    self.one_b, item.at((high,), None),
                    self.core, (0, *item.at((high, l), None, item.rows_b())), lay.L - 1,
                )

            over_high(one)
        if number == 2:

            def two(high):
                add(self.two_a, item.at((high,), 0), self.one_a, (0, *item.at((high, l), 0)), lay.L - 1)
                add(self.two_b, item.at((high,), 0), self.one_b, (0, *item.at((high,), x)), lay.X - 1)

            over_high(two)
        if number == 3:
            for rows, mine, others in (
                (item.rows_a(), self.two_a, self.top_a), (item.rows_b(), self.two_b, self.top_b),
            ):
                total = mine[(0, *item.at((h,), 0))].astype(f32)
                for other in range(lay.H - 1):
                    total = total + others[(other, *item.at((), 0))].astype(f32)
                self.out[:, rows, :] = total

    def close(self):
        for copy in self.sent:
            copy.wait_send()

    @staticmethod
    def count(lay):
        return (lay.C - 1) * lay.X + (lay.X - 1) * 2 + (lay.L - 1) * 2 + (lay.H - 1) * 2


class Total:
    def __init__(self, lay, near, far, sems):
        self.lay, self.near, self.far, self.sems = lay, near, far, sems
        self.sent = []

    def over_mp(self, value):
        dp, mp = lax.axis_index("dp"), lax.axis_index("mp")
        self.near[mp] = value
        self.flying = begin([
            self.sems.copy(self.near.at[mp], self.near.at[mp], (dp, (mp + k) % self.lay.mp))
            for k in range(1, self.lay.mp)
        ])
        self.sent += self.flying

    def over_dp(self):
        dp, mp = lax.axis_index("dp"), lax.axis_index("mp")
        arrive(self.flying)
        total = self.near[0]
        for other in range(1, self.lay.mp):
            total = total + self.near[other]
        self.far[dp] = total
        self.flying = begin([
            self.sems.copy(self.far.at[dp], self.far.at[dp], ((dp + k) % self.lay.dp, mp))
            for k in range(1, self.lay.dp)
        ])
        self.sent += self.flying

    def result(self):
        arrive(self.flying)
        total = self.far[0]
        for other in range(1, self.lay.dp):
            total = total + self.far[other]
        return total

    def close(self):
        for copy in self.sent:
            copy.wait_send()

    @staticmethod
    def count(lay):
        return lay.mp - 1 + lay.dp - 1


def meet(lay):
    barrier = pltpu.get_barrier_semaphore()
    dp, mp = lax.axis_index("dp"), lax.axis_index("mp")
    for k in range(1, lay.mp):
        pl.semaphore_signal(barrier, inc=1, device_id=(dp, (mp + k) % lay.mp), device_id_type=MESH)
    for k in range(1, lay.dp):
        pl.semaphore_signal(barrier, inc=1, device_id=((dp + k) % lay.dp, mp), device_id_type=MESH)
    pl.semaphore_wait(barrier, lay.mp + lay.dp - 2)


def spread_rows(row):
    return jnp.concatenate([row[:, at : at + 128] for at in range(0, row.shape[1], 128)], axis=0)


def joined_row(rows):
    return jnp.concatenate([rows[at : at + 1] for at in range(rows.shape[0])], axis=1)


def diagonal_column(row, count):
    same = iota((count, count), 0) == iota((count, count), 1)
    return jnp.sum(jnp.where(same, jnp.broadcast_to(row, (count, count)), 0.0), axis=1, keepdims=True)


def step_kernel(
    lay, items, total_tokens,
    x_ref, cot_ref, seg_ref, small_ref, qkv_in, sorter_in, wo_in, feed_in,
    out_ref, grad_ref, qkv_out, sorter_out, wo_out, feed_out, small_out,
    *scratch,
):
    qkv_item, sorter_item, wo_item, feed_item = items
    scratch = list(scratch)
    (
        qkv_ref, sorter_blocks, wo_ref, feed_ref, dqkv_ref, dsorter_blocks, dwo_ref, dfeed_ref,
        sorter_ref, first_ref, q_ref, k_ref, v_ref, sk_ref, sv_ref, att_ref, mixed_ref, means_ref, sink_ref, logs_ref,
        segrow_ref, spread_ref, gain_grad_ref,
        near_a, far_a, near_b, far_b, send_sems, recv_sems,
    ) = scratch[:29]
    rest = scratch[29:]
    sems = Sems(send_sems, recv_sems)
    meet(lay)
    gather_qkv = Gather(qkv_item, qkv_in, qkv_ref, sems)
    gather_sorter = Gather(sorter_item, sorter_in, sorter_blocks, sems)
    gather_wo = Gather(wo_item, wo_in, wo_ref, sems)
    gather_feed = Gather(feed_item, feed_in, feed_ref, sems)
    early, late = (gather_qkv, gather_sorter), (gather_wo, gather_feed)
    scatters = []
    for item, full, out in (
        (qkv_item, dqkv_ref, qkv_out), (sorter_item, dsorter_blocks, sorter_out),
        (wo_item, dwo_ref, wo_out), (feed_item, dfeed_ref, feed_out),
    ):
        scatters.append(Scatter(item, full, rest[:7], out, sems))
        rest = rest[7:]
    scatter_qkv, scatter_sorter, scatter_wo, scatter_feed = scatters
    total_a = Total(lay, near_a, far_a, sems)
    total_b = Total(lay, near_b, far_b, sems)

    def each(group, name, *args):
        for member in group:
            getattr(member, name)(*args)

    seg = seg_ref[...].astype(f32)
    real_col = (seg[:, 0:1] > 0).astype(f32)
    lane_block = iota((BLOCKS, LOGITS), 1) % BLOCKS
    real_row = jnp.sum(jnp.where(iota((BLOCKS, LOGITS), 0) == lane_block, real_col, 0.0), axis=0, keepdims=True)
    count = jnp.broadcast_to(jnp.sum(real_col, axis=0, keepdims=True), (8, 128))
    total_a.over_mp(jnp.concatenate([small_ref[...], count], axis=0))
    each(early, "stage", 0)
    each(early + late, "place")
    segrow_ref[...] = jnp.concatenate([seg] * PACK, axis=1)
    total_a.over_dp()
    each(early, "landed")
    each(early, "stage", 1)
    each(late, "stage", 0)
    summed = total_a.result()
    gain_first = joined_row(summed[0:4])
    gain_second = joined_row(summed[4:8])
    entropy_weight = penalty_weight * total_tokens / (summed[8:9, 0:1] * HEADS)
    each(early, "landed")
    each(early, "stage", 2)
    each(early, "landed")
    each(early, "stage", 3)

    def norm_first(tile, carry):
        rows = pl.ds(pl.multiple_of(tile * ROWS, ROWS), ROWS)
        normed, _ = normalize(x_ref[rows, :].astype(f32))
        first_ref[rows, :] = (normed * gain_first).astype(bf16)
        return carry

    lax.fori_loop(0, TILES, norm_first, 0)
    member = (iota((BLOCKS, SEQ_LEN), 0) == iota((BLOCKS, SEQ_LEN), 1) // BLOCK).astype(bf16)
    means = (mm(member, first_ref[...]) / BLOCK).astype(bf16)
    means_ref[...] = means
    each(early, "landed")
    each(late, "landed")
    each(late, "stage", 1)

    def weight(ref, j, cols=slice(None)):
        if len(ref.shape) == 6:
            parts = [ref[j, :, :, part].reshape(WIDTH, ref.shape[-1]) for part in range(lay.mp)]
            return jnp.concatenate(parts, axis=1)
        tile = ref[j, :, :, :, cols]
        return tile.reshape(WIDTH, tile.shape[-1])

    def project(tile, carry):
        rows = pl.ds(pl.multiple_of(tile * ROWS, ROWS), ROWS)
        first = first_ref[rows, :]
        q_ref[rows, :] = mm(first, weight(qkv_ref, 0)).astype(bf16)
        put(k_ref, rows, mm(first, weight(qkv_ref, 1)).astype(bf16).astype(f32))
        put(v_ref, rows, mm(first, weight(qkv_ref, 2)).astype(bf16).astype(f32))
        return carry

    lax.fori_loop(0, TILES, project, 0)
    r, c = sorter_item.r, sorter_item.c
    for high in range(lay.H):
        for low in range(lay.L):
            for part in range(lay.mp):
                rows = slice((high * lay.L + low) * r, (high * lay.L + low + 1) * r)
                sorter_ref[rows, part * c : (part + 1) * c] = sorter_blocks[0, high, low, part]
    logits = mm(means, sorter_ref[...])
    allowed = permitted(real_col, real_row)
    each(late, "landed")
    each(late, "stage", 2)

    def store(index, value):
        sink_ref[index] = value

    logs, weights = sinkhorn(logits, allowed, group_matrix(), store)
    logs_ref[...] = logs
    probs = weights.astype(bf16)

    def sort(i, carry):
        rows = pl.ds(i, BLOCKS, stride=BLOCK)
        put(sk_ref, rows, mm(probs, by_head(take(k_ref, rows).astype(bf16))))
        put(sv_ref, rows, mm(probs, by_head(take(v_ref, rows).astype(bf16))))
        return carry

    lax.fori_loop(0, BLOCK, sort, 0)
    each(late, "landed")
    each(late, "stage", 3)

    def attend(block, carry):
        rows = pl.ds(pl.multiple_of(block * BLOCK, BLOCK), BLOCK)
        row = segrow_ref[pl.ds(block, 1), :]
        near = diagonal_column(row[:, :BLOCK], BLOCK) == row
        far = jnp.broadcast_to(row > 0, (BLOCK, PAIRS))
        mask = jnp.concatenate([near, far], axis=0)
        for group in range(GROUPS):
            lanes = slice(group * LANES, (group + 1) * LANES)
            low, count = group * LANES // CHUNK, LANES // CHUNK
            keys = jnp.concatenate([take(k_ref, rows, low, count), take(sk_ref, rows, low, count)], axis=0).astype(bf16)
            values = jnp.concatenate([take(v_ref, rows, low, count), take(sv_ref, rows, low, count)], axis=0).astype(bf16)
            queries = by_pack(q_ref[rows, lanes])
            scores = jnp.where(mask, mm(keys, queries, 1, 1) * (HEAD_DIM ** -0.5), excluded_fill)
            shifted = jnp.exp(scores - jnp.max(scores, axis=0, keepdims=True))
            attention = shifted * (1.0 / jnp.sum(shifted, axis=0, keepdims=True))
            att_ref[block, group] = attention
            mixed_ref[rows, lanes] = own_heads(mm(attention.astype(bf16), values, 0, 0)).astype(bf16)
        return carry

    lax.fori_loop(0, BLOCKS, attend, 0)
    each(late, "landed")
    gain_grad_ref[...] = jnp.zeros_like(gain_grad_ref)

    def keep(ref, j, cols, value):
        if len(ref.shape) == 6:
            for part in range(lay.mp):
                piece = value[:, part * ref.shape[-1] : (part + 1) * ref.shape[-1]]
                ref[j, :, :, part] = piece.astype(bf16).reshape(lay.H, lay.L, WIDTH // lay.dp, ref.shape[-1])
            return
        ref[j, :, :, :, cols] = value.astype(bf16).reshape(lay.H, lay.L, WIDTH // lay.dp, value.shape[1])

    def feed_phase(second_ref, act_ref, pre_ref):
        def feed(tile, carry):
            rows = pl.ds(pl.multiple_of(tile * ROWS, ROWS), ROWS)
            middle = x_ref[rows, :].astype(f32) + mm(mixed_ref[rows, :], weight(wo_ref, 0), 1, 1)
            normed, inverse = normalize(middle)
            second = (normed * gain_second).astype(bf16)
            second_ref[rows, :] = second
            cot = cot_ref[rows, :]
            total = middle
            second_grad = jnp.zeros((ROWS, WIDTH), f32)
            for part in range(HIDDEN // WIDTH):
                cols = slice(part * WIDTH, (part + 1) * WIDTH)
                up, down = weight(feed_ref, 0, cols), weight(feed_ref, 1, cols)
                pre = mm(second, up)
                act = jnp.maximum(pre, 0.0).astype(bf16)
                act_ref[rows, cols] = act
                total = total + mm(act, down, 1, 1)
                pre_grad = jnp.where(pre > 0, mm(cot, down), 0.0).astype(bf16)
                pre_ref[rows, cols] = pre_grad
                second_grad = second_grad + mm(pre_grad, up, 1, 1)
            out_ref[rows, :] = total.astype(bf16)
            grad_ref[rows, :] = cot.astype(f32) + norm_back(second_grad, normed, inverse, gain_second)
            gain_grad_ref[8:16, :] += jnp.sum((second_grad * normed).reshape(ROWS // 8, 8, WIDTH), axis=0)
            return carry

        lax.fori_loop(0, TILES, feed, 0)

        def feed_weights(part, carry):
            cols = pl.ds(pl.multiple_of(part * WIDTH, WIDTH), WIDTH)
            keep(dfeed_ref, 0, cols, mm(second_ref[...], pre_ref[:, cols], 0, 0))
            keep(dfeed_ref, 1, cols, mm(cot_ref[...], act_ref[:, cols], 0, 0))
            return carry

        lax.fori_loop(0, HIDDEN // WIDTH, feed_weights, 0)

    pl.run_scoped(
        feed_phase,
        pltpu.VMEM((SEQ_LEN, WIDTH), bf16),
        pltpu.VMEM((SEQ_LEN, HIDDEN), bf16),
        pltpu.VMEM((SEQ_LEN, HIDDEN), bf16),
    )
    scatter_feed.stage(0)
    keep(dwo_ref, 0, slice(None), mm(grad_ref[...].astype(bf16), mixed_ref[...], 0, 0))
    scatter_wo.stage(0)
    first_set = (scatter_feed, scatter_wo)

    def start(tile, carry):
        rows = pl.ds(pl.multiple_of(tile * ROWS, ROWS), ROWS)
        mixed_ref[rows, :] = mm(grad_ref[rows, :].astype(bf16), weight(wo_ref, 0)).astype(bf16)
        return carry

    lax.fori_loop(0, TILES, start, 0)
    each(first_set, "fold", 0)
    each(first_set, "stage", 1)

    def backward(dk_ref, dv_ref):
        def attend_back(block, carry):
            rows = pl.ds(pl.multiple_of(block * BLOCK, BLOCK), BLOCK)
            for group in range(GROUPS):
                lanes = slice(group * LANES, (group + 1) * LANES)
                low, count = group * LANES // CHUNK, LANES // CHUNK
                keys = jnp.concatenate([take(k_ref, rows, low, count), take(sk_ref, rows, low, count)], axis=0).astype(bf16)
                values = jnp.concatenate([take(v_ref, rows, low, count), take(sv_ref, rows, low, count)], axis=0).astype(bf16)
                queries = by_pack(q_ref[rows, lanes])
                mixed_grad = by_pack(mixed_ref[rows, lanes])
                attention = att_ref[block, group]
                prob_grad = mm(values, mixed_grad, 1, 1)
                inner = jnp.sum(attention * prob_grad, axis=0, keepdims=True)
                score_grad = (attention * (prob_grad - inner) * (HEAD_DIM ** -0.5)).astype(bf16)
                q_ref[rows, lanes] = own_heads(mm(score_grad, keys, 0, 0)).astype(bf16)
                key_grad = mm(score_grad, queries)
                value_grad = mm(attention.astype(bf16), mixed_grad)
                put(dk_ref, rows, key_grad[:BLOCK], low)
                put(dv_ref, rows, value_grad[:BLOCK], low)
                put(sk_ref, rows, key_grad[BLOCK:].astype(bf16).astype(f32), low)
                put(sv_ref, rows, value_grad[BLOCK:].astype(bf16).astype(f32), low)
            return carry

        lax.fori_loop(0, BLOCKS // 2, attend_back, 0)
        each(first_set, "fold", 1)
        each(first_set, "stage", 2)
        lax.fori_loop(BLOCKS // 2, BLOCKS, attend_back, 0)
        each(first_set, "fold", 2)
        each(first_set, "stage", 3)
        weights = sink_ref[2 * SINK_ITERS - 1]
        same_head = iota((LOGITS, LOGITS), 0) // BLOCKS == iota((LOGITS, LOGITS), 1) // BLOCKS
        turned = jnp.where(same_head, jnp.concatenate([weights] * HEADS, axis=0), 0.0).T
        probs_back = turned[:BLOCKS]
        for head in range(1, HEADS):
            probs_back = probs_back + turned[head * BLOCKS : (head + 1) * BLOCKS]
        probs_back = probs_back.astype(bf16)

        def sort_back(i, total):
            rows = pl.ds(i, BLOCKS, stride=BLOCK)
            key_part = by_head(take(sk_ref, rows).astype(bf16))
            value_part = by_head(take(sv_ref, rows).astype(bf16))
            put(dk_ref, rows, take(dk_ref, rows) + mm(probs_back, key_part))
            put(dv_ref, rows, take(dv_ref, rows) + mm(probs_back, value_part))
            total = total + mm(key_part, take(k_ref, rows).astype(bf16), 1, 1)
            return total + mm(value_part, take(v_ref, rows).astype(bf16), 1, 1)

        stacked = lax.fori_loop(0, BLOCK, sort_back, jnp.zeros((LOGITS, BLOCKS), f32))
        first = first_ref[...]
        keep(dqkv_ref, 0, slice(None), mm(first, q_ref[...], 0, 0))
        keep(dqkv_ref, 1, slice(None), mm(first, take(dk_ref, slice(None)).astype(bf16), 0, 0))
        keep(dqkv_ref, 2, slice(None), mm(first, take(dv_ref, slice(None)).astype(bf16), 0, 0))
        scatter_qkv.stage(0)
        each(first_set, "fold", 3)

        copies = (iota((BLOCKS, LOGITS), 0) == iota((BLOCKS, LOGITS), 1) % BLOCKS).astype(bf16)
        wide = jnp.where(same_head, exact_dot(stacked, copies), 0.0)
        probs_grad = wide[:BLOCKS]
        for head in range(1, HEADS):
            probs_grad = probs_grad + wide[head * BLOCKS : (head + 1) * BLOCKS]
        logs = logs_ref[...]
        pull = jnp.where(real_col > 0, entropy_weight * (logs + 1.0), 0.0)
        scatter_qkv.fold(0)
        scatter_qkv.stage(1)
        grad = sinkhorn_back(weights * (probs_grad - pull), group_matrix(), lambda index: sink_ref[index])
        logit_grad = jnp.where(allowed, grad / softness_factor, 0.0).astype(bf16)
        sorter_grad = mm(means_ref[...], logit_grad, 0, 0).astype(bf16)
        for high in range(lay.H):
            for low in range(lay.L):
                for part in range(lay.mp):
                    rows = slice((high * lay.L + low) * r, (high * lay.L + low + 1) * r)
                    dsorter_blocks[0, high, low, part] = sorter_grad[rows, part * c : (part + 1) * c]
        scatter_sorter.stage(0)
        spread_ref[...] = mm(logit_grad, sorter_ref[...], 1, 1) / BLOCK
        scatter_qkv.fold(1)
        scatter_qkv.stage(2)
        scatter_sorter.fold(0)
        scatter_sorter.stage(1)
        here = ROWS // BLOCK

        def finish(tile, carry):
            rows = pl.ds(pl.multiple_of(tile * ROWS, ROWS), ROWS)
            spread = spread_ref[pl.ds(pl.multiple_of(tile * here, here), here), :]
            spread = jnp.broadcast_to(spread[:, None, :], (here, BLOCK, WIDTH)).reshape(ROWS, WIDTH)
            first_grad = (
                mm(q_ref[rows, :], weight(qkv_ref, 0), 1, 1)
                + mm(take(dk_ref, rows).astype(bf16), weight(qkv_ref, 1), 1, 1)
                + mm(take(dv_ref, rows).astype(bf16), weight(qkv_ref, 2), 1, 1)
                + spread
            )
            normed, inverse = normalize(x_ref[rows, :].astype(f32))
            grad_ref[rows, :] += norm_back(first_grad, normed, inverse, gain_first)
            gain_grad_ref[0:8, :] += jnp.sum((first_grad * normed).reshape(ROWS // 8, 8, WIDTH), axis=0)
            return carry

        lax.fori_loop(0, TILES, finish, 0)
        entropy = -jnp.sum(jnp.where(real_col > 0, weights * logs, 0.0), axis=0, keepdims=True)
        entropy = jnp.broadcast_to(entropy[:, :128] + entropy[:, 128:], (8, 128))
        total_b.over_mp(jnp.concatenate([
            spread_rows(jnp.sum(gain_grad_ref[0:8, :], axis=0, keepdims=True)),
            spread_rows(jnp.sum(gain_grad_ref[8:16, :], axis=0, keepdims=True)),
            entropy,
        ], axis=0))
        scatter_qkv.fold(2)
        scatter_qkv.stage(3)
        scatter_sorter.fold(1)
        scatter_sorter.stage(2)
        total_b.over_dp()
        scatter_sorter.fold(2)
        scatter_sorter.stage(3)
        small_out[0:16, :] = total_b.result()
        small_out[16:24, :] = summed[8:16]
        scatter_qkv.fold(3)
        scatter_sorter.fold(3)
        each(early + late + tuple(scatters) + (total_a, total_b), "close")

    pl.run_scoped(
        backward,
        pltpu.VMEM((CHUNKS, SEQ_LEN, CHUNK), f32),
        pltpu.VMEM((CHUNKS, SEQ_LEN, CHUNK), f32),
    )


def shape(dims, dtype):
    return jax.ShapeDtypeStruct(dims, dtype)


LIMIT = 63 * 1024 * 1024
TOK = (SEQ_LEN, WIDTH)
SPLIT = (CHUNKS, SEQ_LEN, CHUNK)


def run_step(lay, total_tokens, tokens, cotangent, seg, small, qkv, sorter, wo, feed):
    items = tuple(Item(lay, *w.shape) for w in (qkv, sorter, wo, feed))
    vm = pltpu.VMEM
    count = 4 * (Gather.count(lay) + Scatter.count(lay)) + 2 * Total.count(lay)
    scratch = (
        [vm(item.full(), bf16) for item in items] * 2
        + [vm((WIDTH, LOGITS), bf16), vm(TOK, bf16), vm(TOK, bf16)]
        + [vm(SPLIT, f32)] * 4
        + [
            vm((BLOCKS, GROUPS, 2 * BLOCK, PAIRS), f32), vm(TOK, bf16), vm((BLOCKS, WIDTH), bf16),
            vm((2 * SINK_ITERS, BLOCKS, LOGITS), f32), vm((BLOCKS, LOGITS), f32),
            vm((BLOCKS, PAIRS), f32), vm((BLOCKS, WIDTH), f32), vm((16, WIDTH), f32),
        ]
        + [vm((lay.mp, 16, 128), f32), vm((lay.dp, 16, 128), f32)] * 2
        + [pltpu.SemaphoreType.DMA((count,))] * 2
    )
    for item in items:
        scratch += Scatter.buffers(item)
    return pl.pallas_call(
        functools.partial(step_kernel, lay, items, total_tokens),
        out_shape=[shape(TOK, bf16), shape(TOK, f32)]
        + [shape(item.shard(), f32) for item in items]
        + [shape((24, 128), f32)],
        in_specs=[pl.BlockSpec(memory_space=pltpu.VMEM)] * 8,
        out_specs=[pl.BlockSpec(memory_space=pltpu.VMEM)] * 7,
        scratch_shapes=scratch,
        compiler_params=pltpu.CompilerParams(collective_id=0, has_side_effects=True, vmem_limit_bytes=LIMIT),
        name="step",
    )(tokens, cotangent, seg, small, qkv, sorter, wo, feed)


rate_mixer = 0.2
rate_feed = 0.1
rate_sorter = 0.6
rate_gains = 1.0
beta_first = 0.9
beta_second = 0.95
adam_eps = 1e-08
weight_decay = 0.1


def adamw(master, moment, second, grad, rate, step_value):
    moment_new = beta_first * moment + (1.0 - beta_first) * grad
    second_new = beta_second * second + (1.0 - beta_second) * grad * grad
    first_hat = moment_new / (1.0 - beta_first**step_value)
    second_hat = second_new / (1.0 - beta_second**step_value)
    master_new = master - rate * (
        first_hat / (jnp.sqrt(second_hat) + adam_eps) + weight_decay * master
    )
    return (moment_new, second_new, master_new)


def local(
    lay,
    tokens,
    segment_ids,
    cotangent,
    step_count,
    mixer_weights,
    mixer_moment,
    mixer_second,
    feed_weights,
    feed_moment,
    feed_second,
    sorter_weights,
    sorter_moment,
    sorter_second,
    norm_gains,
    gain_moment,
    gain_second,
):
    dp, mp = lax.axis_index("dp"), lax.axis_index("mp")
    total_tokens = lay.dp * segment_ids.shape[0] * SEQ_LEN
    seg = lax.dynamic_slice_in_dim(segment_ids, mp, 1, axis=0).reshape(BLOCKS, BLOCK)
    mixer = mixer_weights.astype(bf16).transpose(1, 0, 2)
    feed = feed_weights.astype(bf16).transpose(1, 0, 2)
    sorter = sorter_weights.astype(bf16)[None]
    width = norm_gains.shape[1]
    at = (dp * lay.mp + mp) * width
    small = lax.dynamic_update_slice(jnp.zeros((2, WIDTH), f32), norm_gains, (0, at)).reshape(8, 128)
    block_output, token_grad, qkv_sum, sorter_sum, wo_sum, feed_sum, sums = run_step(
        lay, float(total_tokens), tokens, cotangent, seg, small, mixer[:3], sorter, mixer[3:], feed
    )
    block_count = sums[16, 0]
    penalty = jnp.sum(sums[8]) / (block_count * HEADS)
    gain_sum = lax.dynamic_slice(sums[:8].reshape(2, WIDTH), (0, at), (2, width))
    mixer_sum = jnp.concatenate([qkv_sum, wo_sum], axis=0).transpose(1, 0, 2)
    step_value = step_count[0].astype(f32)
    mixer_new = adamw(mixer_weights, mixer_moment, mixer_second, mixer_sum, rate_mixer, step_value)
    feed_new = adamw(feed_weights, feed_moment, feed_second, feed_sum.transpose(1, 0, 2), rate_feed, step_value)
    sorter_new = adamw(sorter_weights, sorter_moment, sorter_second, sorter_sum[0], rate_sorter, step_value)
    gain_new = adamw(norm_gains, gain_moment, gain_second, gain_sum, rate_gains, step_value)
    return (block_output, token_grad, penalty.reshape(1), *mixer_new, *feed_new, *sorter_new, *gain_new)


def solution(mesh):
    return jax.shard_map(
        functools.partial(local, Layout(mesh.shape["dp"], mesh.shape["mp"])),
        mesh=mesh,
        in_specs=(
            P(("dp", "mp"), None),
            P("dp", None),
            P(("dp", "mp"), None),
            P(),
            P("dp", None, "mp"),
            P("dp", None, "mp"),
            P("dp", None, "mp"),
            P("dp", None, "mp"),
            P("dp", None, "mp"),
            P("dp", None, "mp"),
            P("dp", "mp"),
            P("dp", "mp"),
            P("dp", "mp"),
            P(None, ("dp", "mp")),
            P(None, ("dp", "mp")),
            P(None, ("dp", "mp")),
        ),
        out_specs=(
            P(("dp", "mp"), None),
            P(("dp", "mp"), None),
            P(),
            P("dp", None, "mp"),
            P("dp", None, "mp"),
            P("dp", None, "mp"),
            P("dp", None, "mp"),
            P("dp", None, "mp"),
            P("dp", None, "mp"),
            P("dp", "mp"),
            P("dp", "mp"),
            P("dp", "mp"),
            P(None, ("dp", "mp")),
            P(None, ("dp", "mp")),
            P(None, ("dp", "mp")),
        ),
        check_vma=False,
    )
```

```python
import functools
import math
import jax
import jax.numpy as jnp
from jax import lax
from jax.sharding import PartitionSpec as P
from jax.experimental import pallas as pl
from jax.experimental.pallas import tpu as pltpu

WIDTH = 512
HEADS = 8
HEAD_DIM = 64
HIDDEN = 2048
BLOCK = 32
SINK_ITERS = 8
SEQ_LEN = 1024
BLOCKS = 32
LOGITS = HEADS * BLOCKS
ROWS = 256
TILES = SEQ_LEN // ROWS
PACK = 4
GROUPS = HEADS // PACK
LANES = PACK * HEAD_DIM
PAIRS = PACK * BLOCK
PAIR = 2 * HEAD_DIM
UNROLL = 4

norm_eps = 1e-05
softness_factor = 0.75
excluded_fill = -1000000000.0
penalty_weight = 0.1
bf16 = jnp.bfloat16
f32 = jnp.float32


def mm(a, b, ca=1, cb=0):
    return lax.dot_general(a, b, (((ca,), (cb,)), ((), ())), preferred_element_type=f32)


def iota(shape, dim):
    return lax.broadcasted_iota(jnp.int32, shape, dim)


def normalize(rows):
    centred = rows - jnp.mean(rows, axis=-1, keepdims=True)
    inverse = lax.rsqrt(jnp.mean(centred * centred, axis=-1, keepdims=True) + norm_eps)
    return centred * inverse, inverse


def norm_back(grad_out, normed, inverse, gain):
    scaled = grad_out * gain
    return inverse * (
        scaled
        - jnp.mean(scaled, axis=-1, keepdims=True)
        - normed * jnp.mean(scaled * normed, axis=-1, keepdims=True)
    )


def three_parts(value):
    high = value.astype(bf16)
    rest = value - high.astype(f32)
    mid = rest.astype(bf16)
    low = (rest - mid.astype(f32)).astype(bf16)
    return high, mid, low


def group_matrix():
    return (iota((LOGITS, LOGITS), 0) // BLOCKS == iota((LOGITS, LOGITS), 1) // BLOCKS).astype(bf16)


def exact_dot(value, matrix):
    rows = value.shape[0]
    out = mm(jnp.concatenate(three_parts(value), axis=0), matrix)
    return out[:rows] + out[rows : 2 * rows] + out[2 * rows :]


def head_max(value):
    lane_head = iota(value.shape, 1) // BLOCKS
    out = jnp.zeros_like(value)
    for head in range(HEADS):
        here = lane_head == head
        top = jnp.max(jnp.where(here, value, -jnp.inf), axis=1, keepdims=True)
        out = jnp.where(here, top, out)
    return out


def permitted(real_col, real_row):
    col = iota((BLOCKS, LOGITS), 1) % BLOCKS
    return ((real_col * real_row) > 0) | (iota((BLOCKS, LOGITS), 0) == col)


def sinkhorn(logits, allowed, groups, store):
    logs = jnp.where(allowed, logits / softness_factor, excluded_fill)
    top = head_max(logs)
    logs = logs - (top + jnp.log(exact_dot(jnp.exp(logs - top), groups)))
    store(0, jnp.exp(logs))
    top = jnp.max(logs, axis=0, keepdims=True)
    logs = logs - (top + jnp.log(jnp.sum(jnp.exp(logs - top), axis=0, keepdims=True)))
    weights = jnp.exp(logs)
    store(1, weights)
    for sweep in range(1, SINK_ITERS):
        logs = logs - jnp.log(exact_dot(weights, groups))
        weights = jnp.exp(logs)
        store(2 * sweep, weights)
        logs = logs - jnp.log(jnp.sum(weights, axis=0, keepdims=True))
        weights = jnp.exp(logs)
        store(2 * sweep + 1, weights)
    return logs, weights


def sinkhorn_back(grad, groups, load):
    for sweep in reversed(range(SINK_ITERS)):
        grad = grad - load(2 * sweep + 1) * jnp.sum(grad, axis=0, keepdims=True)
        grad = grad - load(2 * sweep) * exact_dot(grad, groups)
    return grad


def by_pack(tile):
    rows = jnp.concatenate([tile] * PACK, axis=0)
    keep = iota((PAIRS, LANES), 0) // BLOCK == iota((PAIRS, LANES), 1) // HEAD_DIM
    return jnp.where(keep, rows, jnp.zeros_like(rows))


def own_heads(product):
    lane_head = iota((BLOCK, LANES), 1) // HEAD_DIM
    out = product[:BLOCK]
    for head in range(1, PACK):
        out = jnp.where(lane_head == head, product[head * BLOCK : (head + 1) * BLOCK], out)
    return out


STACK = 8
SPAN = STACK * BLOCKS


def by_place(rows):
    lanes = rows.shape[1]
    return jnp.swapaxes(rows.reshape(BLOCKS, BLOCK, lanes), 0, 1).reshape(SEQ_LEN, lanes)


def repeated(matrix):
    wide = jnp.concatenate([matrix] * STACK, axis=1)
    wide = jnp.concatenate([wide] * STACK, axis=0)
    keep = iota((SPAN, SPAN), 0) // BLOCKS == iota((SPAN, SPAN), 1) // BLOCKS
    return jnp.where(keep, wide, jnp.zeros_like(wide))


MESH = pl.DeviceIdType.MESH


class Layout:
    def __init__(self, mesh_dp, mesh_mp):
        self.dp, self.mp = mesh_dp, mesh_mp
        self.C = 2 if mesh_mp % 2 == 0 else 1
        self.X = mesh_mp // self.C
        self.L = 2 if mesh_dp % 2 == 0 else 1
        self.H = mesh_dp // self.L

    def here(self):
        dp, mp = lax.axis_index("dp"), lax.axis_index("mp")
        return dp // self.L, dp % self.L, mp // self.C, mp % self.C


class Item:
    def __init__(self, lay, J, r, c):
        self.lay, self.J, self.r, self.c = lay, J, r, c
        self.direct = c % 128 == 0
        self.half = r // 2

    def shard(self):
        return (self.J, self.r, self.c)

    def dims(self, *lead, rows=None, wide=None):
        rows = self.r if rows is None else rows
        wide = self.lay.mp if wide is None else wide
        if self.direct:
            return (self.J, *lead, rows, wide * self.c)
        return (self.J, *lead, wide, rows, self.c)

    def full(self):
        return self.dims(self.lay.H, self.lay.L)

    def at(self, lead, m, rows=slice(None)):
        if self.direct:
            cols = slice(None) if m is None else pl.ds(pl.multiple_of(m * self.c, 128), self.c)
            return (slice(None), *lead, rows, cols)
        return (slice(None), *lead, slice(None) if m is None else m, rows, slice(None))

    def rows_a(self):
        return slice(0, self.half)

    def rows_b(self):
        return slice(self.half, self.r)


ALLR = slice(None)


class Sems:
    def __init__(self, send, recv):
        self.send, self.recv, self.used = send, recv, 0

    def copy(self, src, dst, device):
        index = self.used
        self.used += 1
        return pltpu.make_async_remote_copy(
            src_ref=src,
            dst_ref=dst,
            send_sem=self.send.at[index],
            recv_sem=self.recv.at[index],
            device_id=device,
            device_id_type=MESH,
        )


def begin(copies):
    for copy in copies:
        copy.start()
    return copies


def arrive(copies):
    for copy in copies:
        copy.wait_recv()


class Gather:
    def __init__(self, item, shard, full, sems):
        self.item, self.shard, self.full, self.sems = item, shard, full, sems
        self.sent = []

    def stage(self, number):
        item, lay, full = self.item, self.item.lay, self.full
        h, l, x, c = lay.here()
        mp = x * lay.C + c
        copies = []

        def to(hh, ll, xx, cc):
            return (hh * lay.L + ll, xx * lay.C + cc)

        def same(index, device):
            copies.append(self.sems.copy(full.at[index], full.at[index], device))

        if number == 0:
            for k in range(1, lay.H):
                copies.append(
                    self.sems.copy(self.shard, full.at[item.at((h, l), mp)], to((h + k) % lay.H, l, x, c))
                )
        if number == 1:
            for k in range(1, lay.L):
                same(item.at((ALLR, l), mp, item.rows_a()), to(h, (l + k) % lay.L, x, c))
            for k in range(1, lay.X):
                same(item.at((ALLR, l), mp, item.rows_b()), to(h, l, (x + k) % lay.X, c))
        if number == 2:
            for k in range(1, lay.X):
                same(item.at((ALLR, ALLR), mp, item.rows_a()), to(h, l, (x + k) % lay.X, c))
            for k in range(1, lay.L):
                for part in range(lay.X):
                    same(item.at((ALLR, l), part * lay.C + c, item.rows_b()), to(h, (l + k) % lay.L, x, c))
        if number == 3:
            for k in range(1, lay.C):
                for part in range(lay.X):
                    same(item.at((ALLR, ALLR), part * lay.C + c), to(h, l, x, (c + k) % lay.C))
        self.sent += begin(copies)
        self.flying = copies

    def place(self):
        h, l, x, c = self.item.lay.here()
        self.full[self.item.at((h, l), x * self.item.lay.C + c)] = self.shard[...]

    def landed(self):
        arrive(self.flying)

    def close(self):
        for copy in self.sent:
            copy.wait_send()

    @staticmethod
    def count(lay):
        return (lay.H - 1) + (lay.L - 1) + (lay.X - 1) * 2 + (lay.L - 1) * lay.X + (lay.C - 1) * lay.X


class Scatter:
    def __init__(self, item, full, buffers, out, sems):
        self.item, self.full, self.out, self.sems = item, full, out, sems
        self.core, self.one_a, self.one_b, self.two_a, self.two_b, self.top_a, self.top_b = buffers
        self.sent = []

    @staticmethod
    def buffers(item):
        lay = item.lay
        half = item.half
        return [
            pltpu.VMEM((lay.C - 1, *item.dims(lay.H, lay.L, wide=lay.X)), bf16),
            pltpu.VMEM((lay.X - 1, *item.dims(lay.H, lay.L, rows=half, wide=1)), bf16),
            pltpu.VMEM((lay.L - 1, *item.dims(lay.H, rows=half, wide=lay.X)), bf16),
            pltpu.VMEM((lay.L - 1, *item.dims(lay.H, rows=half, wide=1)), bf16),
            pltpu.VMEM((lay.X - 1, *item.dims(lay.H, rows=half, wide=1)), bf16),
            pltpu.VMEM((lay.H - 1, *item.dims(rows=half, wide=1)), bf16),
            pltpu.VMEM((lay.H - 1, *item.dims(rows=half, wide=1)), bf16),
        ]

    def stage(self, number):
        item, lay = self.item, self.item.lay
        h, l, x, c = lay.here()
        copies = []

        def to(hh, ll, xx, cc):
            return (hh * lay.L + ll, xx * lay.C + cc)

        def send(src, src_index, dst, dst_index, device):
            copies.append(self.sems.copy(src.at[src_index], dst.at[dst_index], device))

        if number == 0:
            for k in range(1, lay.C):
                cc = (c + k) % lay.C
                for part in range(lay.X):
                    send(
                        self.full, item.at((ALLR, ALLR), part * lay.C + cc),
                        self.core, (k - 1, *item.at((ALLR, ALLR), part)),
                        to(h, l, x, cc),
                    )
        if number == 1:
            for k in range(1, lay.X):
                xx = (x + k) % lay.X
                send(
                    self.core, (0, *item.at((ALLR, ALLR), xx, item.rows_a())),
                    self.one_a, (k - 1, *item.at((ALLR, ALLR), 0)),
                    to(h, l, xx, c),
                )
            for k in range(1, lay.L):
                ll = (l + k) % lay.L
                send(
                    self.core, (0, *item.at((ALLR, ll), None, item.rows_b())),
                    self.one_b, (k - 1, *item.at((ALLR,), None)),
                    to(h, ll, x, c),
                )
        if number == 2:
            for k in range(1, lay.L):
                ll = (l + k) % lay.L
                send(
                    self.one_a, (0, *item.at((ALLR, ll), 0)),
                    self.two_a, (k - 1, *item.at((ALLR,), 0)),
                    to(h, ll, x, c),
                )
            for k in range(1, lay.X):
                xx = (x + k) % lay.X
                send(
                    self.one_b, (0, *item.at((ALLR,), xx)),
                    self.two_b, (k - 1, *item.at((ALLR,), 0)),
                    to(h, l, xx, c),
                )
        if number == 3:
            for k in range(1, lay.H):
                hh = (h + k) % lay.H
                for src, dst in ((self.two_a, self.top_a), (self.two_b, self.top_b)):
                    send(src, (0, *item.at((hh,), 0)), dst, (k - 1, *item.at((), 0)), to(hh, l, x, c))
        self.sent += begin(copies)
        self.flying = copies

    def fold(self, number):
        item, lay = self.item, self.item.lay
        h, l, x, c = lay.here()
        arrive(self.flying)

        def over_high(body):
            def step(high, carry):
                body(high)
                return carry

            lax.fori_loop(0, lay.H, step, 0)

        def add(target, index, source, source_index, extra):
            total = source[source_index].astype(f32) + target[(0, *index)].astype(f32)
            for other in range(1, extra):
                total = total + target[(other, *index)].astype(f32)
            target[(0, *index)] = total.astype(bf16)

        if number == 0:

            def core(high):
                for low in range(lay.L):
                    for part in range(lay.X):
                        add(
                            self.core, item.at((high, low), part),
                            self.full, item.at((high, low), part * lay.C + c), lay.C - 1,
                        )

            over_high(core)
        if number == 1:

            def one(high):
                for low in range(lay.L):
                    add(
                        self.one_a, item.at((high, low), 0),
                        self.core, (0, *item.at((high, low), x, item.rows_a())), lay.X - 1,
                    )
                add(
                    self.one_b, item.at((high,), None),
                    self.core, (0, *item.at((high, l), None, item.rows_b())), lay.L - 1,
                )

            over_high(one)
        if number == 2:

            def two(high):
                add(self.two_a, item.at((high,), 0), self.one_a, (0, *item.at((high, l), 0)), lay.L - 1)
                add(self.two_b, item.at((high,), 0), self.one_b, (0, *item.at((high,), x)), lay.X - 1)

            over_high(two)
        if number == 3:
            for rows, mine, others in (
                (item.rows_a(), self.two_a, self.top_a), (item.rows_b(), self.two_b, self.top_b),
            ):
                total = mine[(0, *item.at((h,), 0))].astype(f32)
                for other in range(lay.H - 1):
                    total = total + others[(other, *item.at((), 0))].astype(f32)
                self.out[:, rows, :] = total

    def close(self):
        for copy in self.sent:
            copy.wait_send()

    @staticmethod
    def count(lay):
        return (lay.C - 1) * lay.X + (lay.X - 1) * 2 + (lay.L - 1) * 2 + (lay.H - 1) * 2


class Total:
    def __init__(self, lay, near, far, sems):
        self.lay, self.near, self.far, self.sems = lay, near, far, sems
        self.sent = []

    def over_mp(self, value):
        dp, mp = lax.axis_index("dp"), lax.axis_index("mp")
        self.near[mp] = value
        self.flying = begin([
            self.sems.copy(self.near.at[mp], self.near.at[mp], (dp, (mp + k) % self.lay.mp))
            for k in range(1, self.lay.mp)
        ])
        self.sent += self.flying

    def over_dp(self):
        dp, mp = lax.axis_index("dp"), lax.axis_index("mp")
        arrive(self.flying)
        total = self.near[0]
        for other in range(1, self.lay.mp):
            total = total + self.near[other]
        self.far[dp] = total
        self.flying = begin([
            self.sems.copy(self.far.at[dp], self.far.at[dp], ((dp + k) % self.lay.dp, mp))
            for k in range(1, self.lay.dp)
        ])
        self.sent += self.flying

    def result(self):
        arrive(self.flying)
        total = self.far[0]
        for other in range(1, self.lay.dp):
            total = total + self.far[other]
        return total

    def close(self):
        for copy in self.sent:
            copy.wait_send()

    @staticmethod
    def count(lay):
        return lay.mp - 1 + lay.dp - 1


def meet(lay):
    barrier = pltpu.get_barrier_semaphore()
    dp, mp = lax.axis_index("dp"), lax.axis_index("mp")
    for k in range(1, lay.mp):
        pl.semaphore_signal(barrier, inc=1, device_id=(dp, (mp + k) % lay.mp), device_id_type=MESH)
    for k in range(1, lay.dp):
        pl.semaphore_signal(barrier, inc=1, device_id=((dp + k) % lay.dp, mp), device_id_type=MESH)
    pl.semaphore_wait(barrier, lay.mp + lay.dp - 2)


def spread_rows(row):
    return jnp.concatenate([row[:, at : at + 128] for at in range(0, row.shape[1], 128)], axis=0)


def joined_row(rows):
    return jnp.concatenate([rows[at : at + 1] for at in range(rows.shape[0])], axis=1)


def diagonal_column(row, count):
    same = iota((count, count), 0) == iota((count, count), 1)
    return jnp.sum(jnp.where(same, jnp.broadcast_to(row, (count, count)), 0.0), axis=1, keepdims=True)


def spot(width):
    at = (lax.axis_index("dp") * lax.axis_size("mp") + lax.axis_index("mp")) * width
    return (iota((width, WIDTH), 1) == iota((width, WIDTH), 0) + at).astype(bf16)


def packing(r, c):
    return 128 // c if c < 128 and (r * c // 128) % 16 == 0 else 1


def step_kernel(
    lay, gathers, scatter_items, total_tokens,
    tokens_ref, cotangent_ref, segment_ref, gains_in, mixer_in, feed_in, sorter_in,
    out_hbm, grad_hbm, feed_a_out, feed_b_out, woq_out, kv_out, sorter_out, small_out,
    *scratch,
):
    scratch = list(scratch)

    def pop(count):
        taken = scratch[:count]
        del scratch[:count]
        return taken

    shards, weights_full, grads_full = pop(5), pop(5), pop(5)
    qkv_ref, sorter_full, wo_ref, feed_a_ref, feed_b_ref = weights_full
    dfeed_a_ref, dfeed_b_ref, dwoq_ref, dkv_ref, dsorter_full = grads_full
    x_ref, cot_ref, out_ref, grad_ref = pop(4)
    (
        sorter_ref, first_ref, q_ref, k_ref, v_ref, sk_ref, sv_ref, place_k_ref, place_v_ref,
        att_ref, mixed_ref, means_ref, sink_ref, logs_ref, segrow_ref, spread_ref, gain_grad_ref,
        second_ref, act_ref, pre_ref, total_ref, second_grad_ref, pair_k_ref, pair_v_ref,
    ) = pop(24)
    dk_ref, dv_ref = total_ref, second_grad_ref
    near_a, far_a, near_b, far_b, send_sems, recv_sems, copy_sems = pop(7)
    sems = Sems(send_sems, recv_sems)
    fetch_x = pltpu.make_async_copy(tokens_ref, x_ref, copy_sems.at[0])
    fetch_cot = pltpu.make_async_copy(cotangent_ref, cot_ref, copy_sems.at[1])
    fetch_x.start()
    fetch_cot.start()
    mp = lax.axis_index("mp")
    meet(lay)
    gather = [Gather(item, shard, full, sems) for item, shard, full in zip(gathers, shards, weights_full)]
    early, middle_set, late = tuple(gather[:2]), (gather[2], gather[3]), (gather[4],)
    scatters = []
    outs = (feed_a_out, feed_b_out, woq_out, kv_out, sorter_out)
    for item, full, out in zip(scatter_items, grads_full, outs):
        scatters.append(Scatter(item, full, pop(7), out, sems))
    scatter_a, scatter_b, scatter_woq, scatter_kv, scatter_sorter = scatters
    total_a = Total(lay, near_a, far_a, sems)
    total_b = Total(lay, near_b, far_b, sems)

    def each(group, name, *args):
        for member in group:
            getattr(member, name)(*args)

    width = gains_in.shape[1]
    lane = iota((BLOCKS, SEQ_LEN), 1)
    row = segment_ref[pl.ds(mp, 1), :].astype(f32)
    picked = jnp.where(lane // BLOCK == iota((BLOCKS, SEQ_LEN), 0), jnp.broadcast_to(row, (BLOCKS, SEQ_LEN)), 0.0)
    seg = picked[:, :PAIRS]
    for at in range(PAIRS, SEQ_LEN, PAIRS):
        seg = seg + picked[:, at : at + PAIRS]
    tiling = (iota((PAIRS, PAIRS), 0) % BLOCK == iota((PAIRS, PAIRS), 1) % BLOCK).astype(bf16)
    seg = exact_dot(seg, tiling)
    segrow_ref[...] = seg
    real_col = (seg[:, 0:1] > 0).astype(f32)
    count = jnp.broadcast_to(jnp.sum(real_col, axis=0, keepdims=True), (8, 128))
    placed = exact_dot(gains_in[...], spot(width))
    total_a.over_mp(jnp.concatenate([spread_rows(placed[0:1]), spread_rows(placed[1:2]), count], axis=0))
    for j in range(3):
        shards[0][j] = mixer_in[:, j, :].astype(bf16)
    pack = packing(*sorter_in.shape)
    deep = sorter_in.shape[0] // pack
    sorter_shard = sorter_in[...].astype(bf16)
    shards[1][0] = jnp.concatenate([sorter_shard[k * deep : (k + 1) * deep] for k in range(pack)], axis=1)
    each(early, "stage", 0)
    each(early, "place")
    shards[2][0] = mixer_in[:, 3, :].astype(bf16)
    half_width = feed_in.shape[2] // 2
    for j in range(2):
        shards[3][j] = feed_in[:, j, :half_width].astype(bf16)
        shards[4][j] = feed_in[:, j, half_width:].astype(bf16)
    each(middle_set + late, "place")
    lane_block = iota((BLOCKS, LOGITS), 1) % BLOCKS
    real_row = jnp.sum(jnp.where(iota((BLOCKS, LOGITS), 0) == lane_block, real_col, 0.0), axis=0, keepdims=True)
    allowed = permitted(real_col, real_row)
    total_a.over_dp()
    each(early, "landed")
    each(early, "stage", 1)
    each(middle_set, "stage", 0)
    summed = total_a.result()
    gain_first = joined_row(summed[0:4])
    gain_second = joined_row(summed[4:8])
    entropy_weight = penalty_weight * total_tokens / (summed[8:9, 0:1] * HEADS)
    each(early, "landed")
    each(early, "stage", 2)
    fetch_x.wait()

    def norm_first(tile, carry):
        rows = pl.ds(pl.multiple_of(tile * ROWS, ROWS), ROWS)
        normed, _ = normalize(x_ref[rows, :].astype(f32))
        first_ref[rows, :] = (normed * gain_first).astype(bf16)
        return carry

    lax.fori_loop(0, TILES, norm_first, 0)
    member = (iota((BLOCKS, SEQ_LEN), 0) == iota((BLOCKS, SEQ_LEN), 1) // BLOCK).astype(bf16)
    means = (mm(member, first_ref[...]) / BLOCK).astype(bf16)
    means_ref[...] = means
    each(early, "landed")
    each(early, "stage", 3)
    each(middle_set, "landed")
    each(middle_set, "stage", 1)
    each(late, "stage", 0)
    each(early, "landed")

    def weight(ref, j, cols=slice(None)):
        if len(ref.shape) == 6:
            parts = [ref[j, :, :, part].reshape(WIDTH, ref.shape[-1]) for part in range(lay.mp)]
            return jnp.concatenate(parts, axis=1)
        tile = ref[j, :, :, :, cols]
        return tile.reshape(WIDTH, tile.shape[-1])

    def project(tile, carry):
        rows = pl.ds(pl.multiple_of(tile * ROWS, ROWS), ROWS)
        first = first_ref[rows, :]
        q_ref[rows, :] = mm(first, weight(qkv_ref, 0)).astype(bf16)
        k_ref[rows, :] = mm(first, weight(qkv_ref, 1)).astype(bf16)
        v_ref[rows, :] = mm(first, weight(qkv_ref, 2)).astype(bf16)
        return carry

    lax.fori_loop(0, TILES, project, 0)
    r, c = sorter_in.shape

    def sorter_places():
        for high in range(lay.H):
            for low in range(lay.L):
                for part in range(lay.mp):
                    base = (high * lay.L + low) * r
                    if pack == 1:
                        index = (0, high, low, part)
                    else:
                        index = (0, high, low, slice(None), slice(part * 128, (part + 1) * 128))
                    rows = [slice(base + k * deep, base + (k + 1) * deep) for k in range(pack)]
                    yield index, rows, slice(part * c, (part + 1) * c)

    for index, rows, cols in sorter_places():
        tile = sorter_full[index]
        for k in range(pack):
            sorter_ref[rows[k], cols] = tile[:, k * c : (k + 1) * c]
    logits = mm(means, sorter_ref[...])
    each(middle_set, "landed")
    each(middle_set, "stage", 2)

    def store(index, value):
        sink_ref[index] = value

    logs, weights = sinkhorn(logits, allowed, group_matrix(), store)
    logs_ref[...] = logs
    probs = weights.astype(bf16)
    place_k_ref[...] = by_place(k_ref[...])
    place_v_ref[...] = by_place(v_ref[...])
    first_head = iota((SPAN, 2 * PAIR), 1) % PAIR < HEAD_DIM

    def rearrange(matrices, keys, values, keys_out, values_out):
        for pair in range(HEADS // 2):
            lanes = slice(pair * PAIR, (pair + 1) * PAIR)
            one, two = matrices(2 * pair), matrices(2 * pair + 1)
            for part in range(SEQ_LEN // SPAN):
                rows = slice(part * SPAN, (part + 1) * SPAN)
                both = jnp.concatenate([keys[rows, lanes], values[rows, lanes]], axis=1)
                out = jnp.where(first_head, mm(one, both), mm(two, both))
                keys_out[rows, lanes] = out[:, :PAIR].astype(keys_out.dtype)
                values_out[rows, lanes] = out[:, PAIR:].astype(values_out.dtype)

    def forth(head):
        return repeated(probs[:, head * BLOCKS : (head + 1) * BLOCKS])

    rearrange(forth, place_k_ref, place_v_ref, sk_ref, sv_ref)
    sk_ref[...] = by_place(sk_ref[...])
    sv_ref[...] = by_place(sv_ref[...])
    each(late, "landed")
    each(late, "stage", 1)

    def block_rows(block):
        return pl.ds(pl.multiple_of(block * BLOCK, BLOCK), BLOCK)

    def operands(block, group):
        rows = block_rows(block)
        lanes = slice(group * LANES, (group + 1) * LANES)
        keys = jnp.concatenate([k_ref[rows, lanes], sk_ref[rows, lanes]], axis=0)
        values = jnp.concatenate([v_ref[rows, lanes], sv_ref[rows, lanes]], axis=0)
        return keys, values, by_pack(q_ref[rows, lanes])

    def attend(step, carry):
        units = []
        for block in [step * UNROLL + k for k in range(UNROLL)]:
            row = segrow_ref[pl.ds(block, 1), :]
            near = diagonal_column(row[:, :BLOCK], BLOCK) == row
            far = jnp.broadcast_to(row > 0, (BLOCK, PAIRS))
            mask = jnp.concatenate([near, far], axis=0)
            units += [(block, group, mask, *operands(block, group)) for group in range(GROUPS)]
        results = []
        for block, group, mask, keys, values, queries in units:
            scores = jnp.where(mask, mm(keys, queries, 1, 1) * (HEAD_DIM ** -0.5), excluded_fill)
            shifted = jnp.exp(scores - jnp.max(scores, axis=0, keepdims=True))
            attention = shifted * (1.0 / jnp.sum(shifted, axis=0, keepdims=True))
            results.append((attention, own_heads(mm(attention.astype(bf16), values, 0, 0)).astype(bf16)))
        for (block, group, *_), (attention, mixed) in zip(units, results):
            att_ref[block, group] = attention
            mixed_ref[block_rows(block), group * LANES : (group + 1) * LANES] = mixed
        return carry

    half = BLOCKS // UNROLL // 2
    lax.fori_loop(0, half, attend, 0)
    each(middle_set, "landed")
    each(middle_set, "stage", 3)
    each(late, "landed")
    each(late, "stage", 2)
    lax.fori_loop(half, 2 * half, attend, 0)
    fetch_cot.wait()
    gain_grad_ref[...] = jnp.zeros_like(gain_grad_ref)
    each(middle_set, "landed")

    def keep(ref, j, cols, value):
        if len(ref.shape) == 6:
            for part in range(lay.mp):
                piece = value[:, part * ref.shape[-1] : (part + 1) * ref.shape[-1]]
                ref[j, :, :, part] = piece.astype(bf16).reshape(lay.H, lay.L, WIDTH // lay.dp, ref.shape[-1])
            return
        ref[j, :, :, :, cols] = value.astype(bf16).reshape(lay.H, lay.L, WIDTH // lay.dp, value.shape[1])

    def open_rows(tile, carry):
        rows = pl.ds(pl.multiple_of(tile * ROWS, ROWS), ROWS)
        middle = x_ref[rows, :].astype(f32) + mm(mixed_ref[rows, :], weight(wo_ref, 0), 1, 1)
        grad_ref[rows, :] = middle
        normed, _ = normalize(middle)
        second_ref[rows, :] = (normed * gain_second).astype(bf16)
        return carry

    def feed_rows(feed_ref, rows, total, second_grad):
        second, cot = second_ref[rows, :], cot_ref[rows, :]
        for part in range(feed_ref.shape[-1] // WIDTH):
            cols = slice(part * WIDTH, (part + 1) * WIDTH)
            up, down = weight(feed_ref, 0, cols), weight(feed_ref, 1, cols)
            pre = mm(second, up)
            act = jnp.maximum(pre, 0.0).astype(bf16)
            act_ref[rows, cols] = act
            total = total + mm(act, down, 1, 1)
            pre_grad = jnp.where(pre > 0, mm(cot, down), 0.0).astype(bf16)
            pre_ref[rows, cols] = pre_grad
            partial = mm(pre_grad, up, 1, 1)
            second_grad = partial if second_grad is None else second_grad + partial
        return total, second_grad

    def feed_a(tile, carry):
        rows = pl.ds(pl.multiple_of(tile * ROWS, ROWS), ROWS)
        total, second_grad = feed_rows(feed_a_ref, rows, grad_ref[rows, :], None)
        total_ref[rows, :] = total
        second_grad_ref[rows, :] = second_grad
        return carry

    def feed_b(tile, carry):
        rows = pl.ds(pl.multiple_of(tile * ROWS, ROWS), ROWS)
        total, second_grad = feed_rows(feed_b_ref, rows, total_ref[rows, :], second_grad_ref[rows, :])
        out_ref[rows, :] = total.astype(bf16)
        normed, inverse = normalize(grad_ref[rows, :])
        grad_ref[rows, :] = cot_ref[rows, :].astype(f32) + norm_back(second_grad, normed, inverse, gain_second)
        gain_grad_ref[8:16, :] += jnp.sum((second_grad * normed).reshape(ROWS // 8, 8, WIDTH), axis=0)
        return carry

    def feed_weights(dfeed_ref):
        def run(part, carry):
            cols = pl.ds(pl.multiple_of(part * WIDTH, WIDTH), WIDTH)
            keep(dfeed_ref, 0, cols, mm(second_ref[...], pre_ref[:, cols], 0, 0))
            keep(dfeed_ref, 1, cols, mm(cot_ref[...], act_ref[:, cols], 0, 0))
            return carry

        lax.fori_loop(0, dfeed_ref.shape[-1] // WIDTH, run, 0)

    lax.fori_loop(0, TILES, open_rows, 0)
    lax.fori_loop(0, TILES // 2, feed_a, 0)
    each(late, "landed")
    each(late, "stage", 3)
    lax.fori_loop(TILES // 2, TILES, feed_a, 0)
    feed_weights(dfeed_a_ref)
    scatter_a.stage(0)
    each(late, "landed")
    lax.fori_loop(0, TILES // 2, feed_b, 0)
    scatter_a.fold(0)
    scatter_a.stage(1)
    lax.fori_loop(TILES // 2, TILES, feed_b, 0)
    write_out = pltpu.make_async_copy(out_ref, out_hbm, copy_sems.at[2])
    write_out.start()
    scatter_a.fold(1)
    scatter_a.stage(2)
    feed_weights(dfeed_b_ref)
    scatter_b.stage(0)
    scatter_a.fold(2)
    scatter_a.stage(3)
    keep(dwoq_ref, 0, slice(None), mm(grad_ref[...].astype(bf16), mixed_ref[...], 0, 0))

    def start(tile, carry):
        rows = pl.ds(pl.multiple_of(tile * ROWS, ROWS), ROWS)
        mixed_ref[rows, :] = mm(grad_ref[rows, :].astype(bf16), weight(wo_ref, 0)).astype(bf16)
        return carry

    lax.fori_loop(0, TILES, start, 0)
    scatter_b.fold(0)
    scatter_b.stage(1)

    def attend_back(step, carry):
        units = []
        for block in [step * UNROLL + k for k in range(UNROLL)]:
            for group in range(GROUPS):
                mixed_grad = by_pack(mixed_ref[block_rows(block), group * LANES : (group + 1) * LANES])
                units.append((block, group, mixed_grad, att_ref[block, group], *operands(block, group)))
        results = []
        for block, group, mixed_grad, attention, keys, values, queries in units:
            prob_grad = mm(values, mixed_grad, 1, 1)
            inner = jnp.sum(attention * prob_grad, axis=0, keepdims=True)
            score_grad = (attention * (prob_grad - inner) * (HEAD_DIM ** -0.5)).astype(bf16)
            results.append((
                own_heads(mm(score_grad, keys, 0, 0)).astype(bf16),
                mm(score_grad, queries),
                mm(attention.astype(bf16), mixed_grad),
            ))
        for (block, group, *_), (query_grad, key_grad, value_grad) in zip(units, results):
            rows = block_rows(block)
            lanes = slice(group * LANES, (group + 1) * LANES)
            q_ref[rows, lanes] = query_grad
            dk_ref[rows, lanes] = key_grad[:BLOCK]
            dv_ref[rows, lanes] = value_grad[:BLOCK]
            sk_ref[rows, lanes] = key_grad[BLOCK:].astype(bf16)
            sv_ref[rows, lanes] = value_grad[BLOCK:].astype(bf16)
        return carry

    lax.fori_loop(0, half, attend_back, 0)
    scatter_a.fold(3)
    scatter_b.fold(1)
    scatter_b.stage(2)
    lax.fori_loop(half, 2 * half, attend_back, 0)
    first = first_ref[...]
    keep(dwoq_ref, 1, slice(None), mm(first, q_ref[...], 0, 0))
    scatter_woq.stage(0)
    scatter_b.fold(2)
    scatter_b.stage(3)
    weights = sink_ref[2 * SINK_ITERS - 1]
    same_head = iota((LOGITS, LOGITS), 0) // BLOCKS == iota((LOGITS, LOGITS), 1) // BLOCKS
    turned = jnp.where(same_head, jnp.concatenate([weights] * HEADS, axis=0), 0.0).T

    def back(head):
        rows = slice(head * BLOCKS, (head + 1) * BLOCKS)
        return repeated(turned[rows, rows].astype(bf16))

    sk_ref[...] = by_place(sk_ref[...])
    sv_ref[...] = by_place(sv_ref[...])
    rearrange(back, sk_ref, sv_ref, pair_k_ref, pair_v_ref)
    key_grad = (dk_ref[...] + by_place(pair_k_ref[...])).astype(bf16)
    value_grad = (dv_ref[...] + by_place(pair_v_ref[...])).astype(bf16)
    k_ref[...] = key_grad
    v_ref[...] = value_grad
    keep(dkv_ref, 0, slice(None), mm(first, key_grad, 0, 0))
    keep(dkv_ref, 1, slice(None), mm(first, value_grad, 0, 0))
    scatter_kv.stage(0)
    scatter_woq.fold(0)
    scatter_woq.stage(1)
    scatter_b.fold(3)
    lane_head = iota((SPAN, PAIR), 1) // HEAD_DIM
    diagonal = iota((SPAN, SPAN), 0) // BLOCKS == iota((SPAN, SPAN), 1) // BLOCKS
    folded = []
    for pair in range(HEADS // 2):
        lanes = slice(pair * PAIR, (pair + 1) * PAIR)
        parts = [slice(part * SPAN, (part + 1) * SPAN) for part in range(SEQ_LEN // SPAN)]
        right = [ref[rows, lanes] for rows in parts for ref in (place_k_ref, place_v_ref)]
        left = [ref[rows, lanes] for rows in parts for ref in (sk_ref, sv_ref)]
        for head in range(2):
            mine = [jnp.where(lane_head == head, tile, jnp.zeros_like(tile)) for tile in left]
            square = mm(jnp.concatenate(mine, axis=1), jnp.concatenate(right, axis=1), 1, 1)
            square = jnp.where(diagonal, square, 0.0)
            total = square[:BLOCKS]
            for place in range(1, STACK):
                total = total + square[place * BLOCKS : (place + 1) * BLOCKS]
            folded.append(total)
    copies = (iota((BLOCKS, LOGITS), 0) == iota((BLOCKS, LOGITS), 1) % BLOCKS).astype(bf16)
    stacked = exact_dot(jnp.concatenate(folded, axis=0), copies.T)
    wide = jnp.where(same_head, exact_dot(stacked, copies), 0.0)
    probs_grad = wide[:BLOCKS]
    for head in range(1, HEADS):
        probs_grad = probs_grad + wide[head * BLOCKS : (head + 1) * BLOCKS]
    logs = logs_ref[...]
    pull = jnp.where(real_col > 0, entropy_weight * (logs + 1.0), 0.0)
    scatter_kv.fold(0)
    scatter_kv.stage(1)
    grad = sinkhorn_back(weights * (probs_grad - pull), group_matrix(), lambda index: sink_ref[index])
    logit_grad = jnp.where(allowed, grad / softness_factor, 0.0).astype(bf16)
    sorter_grad = mm(means_ref[...], logit_grad, 0, 0).astype(bf16)
    for index, rows, cols in sorter_places():
        pieces = [sorter_grad[rows[k], cols] for k in range(pack)]
        dsorter_full[index] = jnp.concatenate(pieces, axis=1) if pack > 1 else pieces[0]
    scatter_sorter.stage(0)
    spread_ref[...] = mm(logit_grad, sorter_ref[...], 1, 1) / BLOCK
    scatter_woq.fold(1)
    scatter_woq.stage(2)
    scatter_kv.fold(1)
    scatter_kv.stage(2)
    scatter_sorter.fold(0)
    scatter_sorter.stage(1)
    here = ROWS // BLOCK

    def finish(tile, carry):
        rows = pl.ds(pl.multiple_of(tile * ROWS, ROWS), ROWS)
        spread = spread_ref[pl.ds(pl.multiple_of(tile * here, here), here), :]
        spread = jnp.broadcast_to(spread[:, None, :], (here, BLOCK, WIDTH)).reshape(ROWS, WIDTH)
        first_grad = (
            mm(q_ref[rows, :], weight(qkv_ref, 0), 1, 1)
            + mm(k_ref[rows, :], weight(qkv_ref, 1), 1, 1)
            + mm(v_ref[rows, :], weight(qkv_ref, 2), 1, 1)
            + spread
        )
        normed, inverse = normalize(x_ref[rows, :].astype(f32))
        grad_ref[rows, :] += norm_back(first_grad, normed, inverse, gain_first)
        gain_grad_ref[0:8, :] += jnp.sum((first_grad * normed).reshape(ROWS // 8, 8, WIDTH), axis=0)
        return carry

    writes = []

    def write_rows(part):
        rows = slice(part * SEQ_LEN // 2, (part + 1) * SEQ_LEN // 2)
        copy = pltpu.make_async_copy(grad_ref.at[rows], grad_hbm.at[rows], copy_sems.at[3 + part])
        copy.start()
        writes.append(copy)

    lax.fori_loop(0, TILES // 2, finish, 0)
    write_rows(0)
    scatter_woq.fold(2)
    scatter_woq.stage(3)
    scatter_kv.fold(2)
    scatter_kv.stage(3)
    scatter_sorter.fold(1)
    scatter_sorter.stage(2)
    lax.fori_loop(TILES // 2, TILES, finish, 0)
    write_rows(1)
    entropy = -jnp.sum(jnp.where(real_col > 0, weights * logs, 0.0), axis=0, keepdims=True)
    entropy = jnp.broadcast_to(entropy[:, :128] + entropy[:, 128:], (8, 128))
    total_b.over_mp(jnp.concatenate([
        spread_rows(jnp.sum(gain_grad_ref[0:8, :], axis=0, keepdims=True)),
        spread_rows(jnp.sum(gain_grad_ref[8:16, :], axis=0, keepdims=True)),
        entropy,
    ], axis=0))
    scatter_sorter.fold(2)
    scatter_sorter.stage(3)
    total_b.over_dp()
    scatter_woq.fold(3)
    scatter_kv.fold(3)
    scatter_sorter.fold(3)
    small_out[0:16, :] = total_b.result()
    small_out[16:24, :] = summed[8:16]
    write_out.wait()
    for copy in writes:
        copy.wait()
    each(tuple(gather) + tuple(scatters) + (total_a, total_b), "close")


def update_kernel(
    lay, step_ref, out_in, grad_in, feed_a, feed_b, woq, kv, sorter, sums, *refs
):
    masters, results = refs[:12], refs[12:27]
    out_rows, grad_rows, sem = refs[27:]
    block_out, token_out, penalty_out = results[:3]
    moves = []
    for part in range(2):
        rows = slice(part * SEQ_LEN // 2, (part + 1) * SEQ_LEN // 2)
        for which, (source, middle, target) in enumerate(
            ((out_in, out_rows, block_out), (grad_in, grad_rows, token_out))
        ):
            moves.append((
                pltpu.make_async_copy(source.at[rows], middle.at[rows], sem.at[part, which, 0]),
                pltpu.make_async_copy(middle.at[rows], target.at[rows], sem.at[part, which, 1]),
            ))
    for bring, _ in moves:
        bring.start()
    step_value = jnp.full((1, 128), step_ref[0], jnp.int32).astype(f32)
    scale_first = 1.0 / (1.0 - jnp.exp(step_value * math.log(beta_first)))[:, 0:1]
    scale_second = 1.0 / (1.0 - jnp.exp(step_value * math.log(beta_second)))[:, 0:1]

    def adamw(which, index, grad, rate):
        master, moment, second = [ref[index] for ref in masters[3 * which : 3 * which + 3]]
        moment_new = beta_first * moment + (1.0 - beta_first) * grad
        second_new = beta_second * second + (1.0 - beta_second) * grad * grad
        change = (moment_new * scale_first) / (jnp.sqrt(second_new * scale_second) + adam_eps)
        outs = results[3 + 3 * which : 6 + 3 * which]
        outs[0][index] = moment_new
        outs[1][index] = second_new
        outs[2][index] = master - rate * (change + weight_decay * master)

    for j, grad in enumerate((woq[1], kv[0], kv[1], woq[0])):
        adamw(0, (ALLR, j, ALLR), grad, rate_mixer)
    for bring, send in moves:
        bring.wait()
        send.start()
    half = feed_a.shape[2]
    for j in range(2):
        adamw(1, (ALLR, j, slice(0, half)), feed_a[j], rate_feed)
        adamw(1, (ALLR, j, slice(half, 2 * half)), feed_b[j], rate_feed)
    r, c = masters[6].shape
    pack = packing(r, c)
    deep = r // pack
    grad = jnp.concatenate([sorter[0][:, k * c : (k + 1) * c] for k in range(pack)], axis=0) if pack > 1 else sorter[0]
    adamw(2, (ALLR, ALLR), grad, rate_sorter)
    rows = jnp.concatenate([joined_row(sums[0:4, :]), joined_row(sums[4:8, :])], axis=0)
    own = spot(masters[9].shape[1])
    grad = sum(mm(part, own, 1, 1) for part in three_parts(rows))
    adamw(3, (ALLR, ALLR), grad, rate_gains)
    entropy = jnp.sum(sums[8:9, :], axis=1, keepdims=True)
    penalty_out[...] = jnp.broadcast_to(entropy / (sums[16:17, 0:1] * HEADS), (1, 128))
    for _, send in moves:
        send.wait()


def shape(dims, dtype):
    return jax.ShapeDtypeStruct(dims, dtype)


LIMIT = 63 * 1024 * 1024
TOK = (SEQ_LEN, WIDTH)


def run_step(lay, total_tokens, tokens, cotangent, segment_ids, gains, mixer, feed, sorter):
    r, c, half = mixer.shape[0], mixer.shape[2], feed.shape[2] // 2
    pack = packing(*sorter.shape)
    sorter_item = Item(lay, 1, sorter.shape[0] // pack, sorter.shape[1] * pack)
    feed_item, pair_item = Item(lay, 2, r, half), Item(lay, 2, r, c)
    gathers = (Item(lay, 3, r, c), sorter_item, Item(lay, 1, r, c), feed_item, feed_item)
    scatters = (feed_item, feed_item, pair_item, pair_item, sorter_item)
    vm = pltpu.VMEM
    count = 5 * (Gather.count(lay) + Scatter.count(lay)) + 2 * Total.count(lay)
    scratch = (
        [vm(item.shard(), bf16) for item in gathers]
        + [vm(item.full(), bf16) for item in gathers + scatters]
        + [vm(TOK, bf16), vm(TOK, bf16), vm(TOK, bf16), vm(TOK, f32)]
        + [vm((WIDTH, LOGITS), bf16)]
        + [vm(TOK, bf16)] * 8
        + [
            vm((BLOCKS, GROUPS, 2 * BLOCK, PAIRS), f32), vm(TOK, bf16), vm((BLOCKS, WIDTH), bf16),
            vm((2 * SINK_ITERS, BLOCKS, LOGITS), f32), vm((BLOCKS, LOGITS), f32),
            vm((BLOCKS, PAIRS), f32), vm((BLOCKS, WIDTH), f32), vm((16, WIDTH), f32),
            vm(TOK, bf16), vm((SEQ_LEN, HIDDEN // 2), bf16), vm((SEQ_LEN, HIDDEN // 2), bf16),
        ]
        + [vm(TOK, f32)] * 4
        + [vm((lay.mp, 16, 128), f32), vm((lay.dp, 16, 128), f32)] * 2
        + [pltpu.SemaphoreType.DMA((count,))] * 2
        + [pltpu.SemaphoreType.DMA((5,))]
    )
    for item in scatters:
        scratch += Scatter.buffers(item)
    inside = pl.BlockSpec(memory_space=pltpu.VMEM)
    outside = pl.BlockSpec(memory_space=pl.ANY)
    return pl.pallas_call(
        functools.partial(step_kernel, lay, gathers, scatters, total_tokens),
        out_shape=[shape(TOK, bf16), shape(TOK, f32)]
        + [shape(item.shard(), f32) for item in scatters]
        + [shape((24, 128), f32)],
        in_specs=[outside] * 2 + [inside] * 5,
        out_specs=[outside] * 2 + [inside] * 6,
        scratch_shapes=scratch,
        compiler_params=pltpu.CompilerParams(collective_id=0, has_side_effects=True, vmem_limit_bytes=LIMIT),
        name="step",
    )(tokens, cotangent, segment_ids, gains, mixer, feed, sorter)


def run_update(lay, step_count, block_output, token_grad, sums, states):
    inside = pl.BlockSpec(memory_space=pltpu.VMEM)
    outside = pl.BlockSpec(memory_space=pl.ANY)
    outs = [shape(TOK, bf16), shape(TOK, f32), shape((1, 128), f32)] + [shape(state.shape, f32) for state in states]
    return pl.pallas_call(
        functools.partial(update_kernel, lay),
        out_shape=outs,
        in_specs=[pl.BlockSpec(memory_space=pltpu.SMEM)] + [outside] * 2 + [inside] * 18,
        out_specs=[outside] * 2 + [inside] * 13,
        scratch_shapes=[pltpu.VMEM(TOK, bf16), pltpu.VMEM(TOK, f32), pltpu.SemaphoreType.DMA((2, 2, 2))],
        compiler_params=pltpu.CompilerParams(vmem_limit_bytes=LIMIT),
        name="update",
    )(step_count, block_output, token_grad, *sums, *states)


rate_mixer = 0.2
rate_feed = 0.1
rate_sorter = 0.6
rate_gains = 1.0
beta_first = 0.9
beta_second = 0.95
adam_eps = 1e-08
weight_decay = 0.1


def local(
    lay,
    tokens,
    segment_ids,
    cotangent,
    step_count,
    mixer_weights,
    mixer_moment,
    mixer_second,
    feed_weights,
    feed_moment,
    feed_second,
    sorter_weights,
    sorter_moment,
    sorter_second,
    norm_gains,
    gain_moment,
    gain_second,
):
    total_tokens = float(lay.dp * segment_ids.shape[0] * SEQ_LEN)
    block_output, token_grad, *sums = run_step(
        lay, total_tokens, tokens, cotangent, segment_ids, norm_gains, mixer_weights, feed_weights, sorter_weights
    )
    states = (
        mixer_weights, mixer_moment, mixer_second, feed_weights, feed_moment, feed_second,
        sorter_weights, sorter_moment, sorter_second, norm_gains, gain_moment, gain_second,
    )
    block_output, token_grad, penalty, *states = run_update(lay, step_count, block_output, token_grad, sums, states)
    return (block_output, token_grad, penalty[0, :1], *states)


def solution(mesh):
    return jax.shard_map(
        functools.partial(local, Layout(mesh.shape["dp"], mesh.shape["mp"])),
        mesh=mesh,
        in_specs=(
            P(("dp", "mp"), None),
            P("dp", None),
            P(("dp", "mp"), None),
            P(),
            P("dp", None, "mp"),
            P("dp", None, "mp"),
            P("dp", None, "mp"),
            P("dp", None, "mp"),
            P("dp", None, "mp"),
            P("dp", None, "mp"),
            P("dp", "mp"),
            P("dp", "mp"),
            P("dp", "mp"),
            P(None, ("dp", "mp")),
            P(None, ("dp", "mp")),
            P(None, ("dp", "mp")),
        ),
        out_specs=(
            P(("dp", "mp"), None),
            P(("dp", "mp"), None),
            P(),
            P("dp", None, "mp"),
            P("dp", None, "mp"),
            P("dp", None, "mp"),
            P("dp", None, "mp"),
            P("dp", None, "mp"),
            P("dp", None, "mp"),
            P("dp", "mp"),
            P("dp", "mp"),
            P("dp", "mp"),
            P(None, ("dp", "mp")),
            P(None, ("dp", "mp")),
            P(None, ("dp", "mp")),
        ),
        check_vma=False,
    )
```

```python
import functools
import math
import jax
import jax.numpy as jnp
from jax import lax
from jax.sharding import PartitionSpec as P
from jax.experimental import pallas as pl
from jax.experimental.pallas import tpu as pltpu

WIDTH = 512
HEADS = 8
HEAD_DIM = 64
HIDDEN = 2048
BLOCK = 32
SINK_ITERS = 8
SEQ_LEN = 1024
BLOCKS = 32
LOGITS = HEADS * BLOCKS
ROWS = 512
TILES = SEQ_LEN // ROWS
PACK = 4
GROUPS = HEADS // PACK
LANES = PACK * HEAD_DIM
PAIRS = PACK * BLOCK
PAIR = 2 * HEAD_DIM
UNROLL = 8

norm_eps = 1e-05
softness_factor = 0.75
excluded_fill = -1000000000.0
penalty_weight = 0.1
bf16 = jnp.bfloat16
f32 = jnp.float32


def mm(a, b, ca=1, cb=0):
    return lax.dot_general(a, b, (((ca,), (cb,)), ((), ())), preferred_element_type=f32)


def iota(shape, dim):
    return lax.broadcasted_iota(jnp.int32, shape, dim)


def normalize(rows):
    centred = rows - jnp.mean(rows, axis=-1, keepdims=True)
    inverse = lax.rsqrt(jnp.mean(centred * centred, axis=-1, keepdims=True) + norm_eps)
    return centred * inverse, inverse


def norm_back(grad_out, normed, inverse, gain):
    scaled = grad_out * gain
    return inverse * (
        scaled
        - jnp.mean(scaled, axis=-1, keepdims=True)
        - normed * jnp.mean(scaled * normed, axis=-1, keepdims=True)
    )


def three_parts(value):
    high = value.astype(bf16)
    rest = value - high.astype(f32)
    mid = rest.astype(bf16)
    low = (rest - mid.astype(f32)).astype(bf16)
    return high, mid, low


def group_matrix():
    return (iota((LOGITS, LOGITS), 0) // BLOCKS == iota((LOGITS, LOGITS), 1) // BLOCKS).astype(bf16)


def exact_dot(value, matrix):
    rows = value.shape[0]
    out = mm(jnp.concatenate(three_parts(value), axis=0), matrix)
    return out[:rows] + out[rows : 2 * rows] + out[2 * rows :]


def head_max(value):
    lane_head = iota(value.shape, 1) // BLOCKS
    out = jnp.zeros_like(value)
    for head in range(HEADS):
        here = lane_head == head
        top = jnp.max(jnp.where(here, value, -jnp.inf), axis=1, keepdims=True)
        out = jnp.where(here, top, out)
    return out


def permitted(real_col, real_row):
    col = iota((BLOCKS, LOGITS), 1) % BLOCKS
    return ((real_col * real_row) > 0) | (iota((BLOCKS, LOGITS), 0) == col)


def sinkhorn(logits, allowed, groups, store):
    logs = jnp.where(allowed, logits / softness_factor, excluded_fill)
    top = head_max(logs)
    logs = logs - (top + jnp.log(exact_dot(jnp.exp(logs - top), groups)))
    store(0, jnp.exp(logs))
    top = jnp.max(logs, axis=0, keepdims=True)
    logs = logs - (top + jnp.log(jnp.sum(jnp.exp(logs - top), axis=0, keepdims=True)))
    weights = jnp.exp(logs)
    store(1, weights)
    for sweep in range(1, SINK_ITERS):
        logs = logs - jnp.log(exact_dot(weights, groups))
        weights = jnp.exp(logs)
        store(2 * sweep, weights)
        logs = logs - jnp.log(jnp.sum(weights, axis=0, keepdims=True))
        weights = jnp.exp(logs)
        store(2 * sweep + 1, weights)
    return logs, weights


def sinkhorn_back(grad, groups, load):
    for sweep in reversed(range(SINK_ITERS)):
        grad = grad - load(2 * sweep + 1) * jnp.sum(grad, axis=0, keepdims=True)
        grad = grad - load(2 * sweep) * exact_dot(grad, groups)
    return grad


def by_pack(tile):
    rows = jnp.concatenate([tile] * PACK, axis=0)
    keep = iota((PAIRS, LANES), 0) // BLOCK == iota((PAIRS, LANES), 1) // HEAD_DIM
    return jnp.where(keep, rows, jnp.zeros_like(rows))


def own_heads(product):
    lane_head = iota((BLOCK, LANES), 1) // HEAD_DIM
    out = product[:BLOCK]
    for head in range(1, PACK):
        out = jnp.where(lane_head == head, product[head * BLOCK : (head + 1) * BLOCK], out)
    return out


STACK = 8
SPAN = STACK * BLOCKS


def by_place(rows):
    lanes = rows.shape[1]
    return jnp.swapaxes(rows.reshape(BLOCKS, BLOCK, lanes), 0, 1).reshape(SEQ_LEN, lanes)


def repeated(matrix):
    wide = jnp.concatenate([matrix] * STACK, axis=1)
    wide = jnp.concatenate([wide] * STACK, axis=0)
    keep = iota((SPAN, SPAN), 0) // BLOCKS == iota((SPAN, SPAN), 1) // BLOCKS
    return jnp.where(keep, wide, jnp.zeros_like(wide))


MESH = pl.DeviceIdType.MESH


class Layout:
    def __init__(self, mesh_dp, mesh_mp):
        self.dp, self.mp = mesh_dp, mesh_mp
        self.C = 2 if mesh_mp % 2 == 0 else 1
        self.X = mesh_mp // self.C
        self.L = 2 if mesh_dp % 2 == 0 else 1
        self.H = mesh_dp // self.L

    def here(self):
        dp, mp = lax.axis_index("dp"), lax.axis_index("mp")
        return dp // self.L, dp % self.L, mp // self.C, mp % self.C


class Item:
    def __init__(self, lay, J, r, c):
        self.lay, self.J, self.r, self.c = lay, J, r, c
        self.direct = c % 128 == 0
        self.half = r // 2

    def shard(self):
        return (self.J, self.r, self.c)

    def dims(self, *lead, rows=None, wide=None):
        rows = self.r if rows is None else rows
        wide = self.lay.mp if wide is None else wide
        if self.direct:
            return (self.J, *lead, rows, wide * self.c)
        return (self.J, *lead, wide, rows, self.c)

    def full(self):
        return self.dims(self.lay.H, self.lay.L)

    def at(self, lead, m, rows=slice(None)):
        if self.direct:
            cols = slice(None) if m is None else pl.ds(pl.multiple_of(m * self.c, 128), self.c)
            return (slice(None), *lead, rows, cols)
        return (slice(None), *lead, slice(None) if m is None else m, rows, slice(None))

    def rows_a(self):
        return slice(0, self.half)

    def rows_b(self):
        return slice(self.half, self.r)


ALLR = slice(None)


class Sems:
    def __init__(self, send, recv):
        self.send, self.recv, self.used = send, recv, 0

    def copy(self, src, dst, device):
        index = self.used
        self.used += 1
        return pltpu.make_async_remote_copy(
            src_ref=src,
            dst_ref=dst,
            send_sem=self.send.at[index],
            recv_sem=self.recv.at[index],
            device_id=device,
            device_id_type=MESH,
        )


def begin(copies):
    for copy in copies:
        copy.start()
    return copies


def arrive(copies):
    for copy in copies:
        copy.wait_recv()


class Gather:
    def __init__(self, item, shard, full, sems):
        self.item, self.shard, self.full, self.sems = item, shard, full, sems
        self.sent = []

    def stage(self, number):
        item, lay, full = self.item, self.item.lay, self.full
        h, l, x, c = lay.here()
        mp = x * lay.C + c
        copies = []

        def to(hh, ll, xx, cc):
            return (hh * lay.L + ll, xx * lay.C + cc)

        def same(index, device):
            copies.append(self.sems.copy(full.at[index], full.at[index], device))

        if number == 0:
            for k in range(1, lay.H):
                copies.append(
                    self.sems.copy(self.shard, full.at[item.at((h, l), mp)], to((h + k) % lay.H, l, x, c))
                )
        if number == 1:
            for k in range(1, lay.L):
                same(item.at((ALLR, l), mp, item.rows_a()), to(h, (l + k) % lay.L, x, c))
            for k in range(1, lay.X):
                same(item.at((ALLR, l), mp, item.rows_b()), to(h, l, (x + k) % lay.X, c))
        if number == 2:
            for k in range(1, lay.X):
                same(item.at((ALLR, ALLR), mp, item.rows_a()), to(h, l, (x + k) % lay.X, c))
            for k in range(1, lay.L):
                for part in range(lay.X):
                    same(item.at((ALLR, l), part * lay.C + c, item.rows_b()), to(h, (l + k) % lay.L, x, c))
        if number == 3:
            for k in range(1, lay.C):
                for part in range(lay.X):
                    same(item.at((ALLR, ALLR), part * lay.C + c), to(h, l, x, (c + k) % lay.C))
        self.sent += begin(copies)
        self.flying = copies

    def place(self):
        h, l, x, c = self.item.lay.here()
        self.full[self.item.at((h, l), x * self.item.lay.C + c)] = self.shard[...]

    def landed(self):
        arrive(self.flying)

    def close(self):
        for copy in self.sent:
            copy.wait_send()

    @staticmethod
    def count(lay):
        return (lay.H - 1) + (lay.L - 1) + (lay.X - 1) * 2 + (lay.L - 1) * lay.X + (lay.C - 1) * lay.X


class Scatter:
    def __init__(self, item, full, buffers, out, sems):
        self.item, self.full, self.out, self.sems = item, full, out, sems
        self.core, self.one_a, self.one_b, self.two_a, self.two_b, self.top_a, self.top_b = buffers
        self.sent = []

    @staticmethod
    def buffers(item):
        lay = item.lay
        half = item.half
        return [
            pltpu.VMEM((lay.C - 1, *item.dims(lay.H, lay.L, wide=lay.X)), bf16),
            pltpu.VMEM((lay.X - 1, *item.dims(lay.H, lay.L, rows=half, wide=1)), bf16),
            pltpu.VMEM((lay.L - 1, *item.dims(lay.H, rows=half, wide=lay.X)), bf16),
            pltpu.VMEM((lay.L - 1, *item.dims(lay.H, rows=half, wide=1)), bf16),
            pltpu.VMEM((lay.X - 1, *item.dims(lay.H, rows=half, wide=1)), bf16),
            pltpu.VMEM((lay.H - 1, *item.dims(rows=half, wide=1)), bf16),
            pltpu.VMEM((lay.H - 1, *item.dims(rows=half, wide=1)), bf16),
        ]

    def stage(self, number):
        item, lay = self.item, self.item.lay
        h, l, x, c = lay.here()
        copies = []

        def to(hh, ll, xx, cc):
            return (hh * lay.L + ll, xx * lay.C + cc)

        def send(src, src_index, dst, dst_index, device):
            copies.append(self.sems.copy(src.at[src_index], dst.at[dst_index], device))

        if number == 0:
            for k in range(1, lay.C):
                cc = (c + k) % lay.C
                for part in range(lay.X):
                    send(
                        self.full, item.at((ALLR, ALLR), part * lay.C + cc),
                        self.core, (k - 1, *item.at((ALLR, ALLR), part)),
                        to(h, l, x, cc),
                    )
        if number == 1:
            for k in range(1, lay.X):
                xx = (x + k) % lay.X
                send(
                    self.core, (0, *item.at((ALLR, ALLR), xx, item.rows_a())),
                    self.one_a, (k - 1, *item.at((ALLR, ALLR), 0)),
                    to(h, l, xx, c),
                )
            for k in range(1, lay.L):
                ll = (l + k) % lay.L
                send(
                    self.core, (0, *item.at((ALLR, ll), None, item.rows_b())),
                    self.one_b, (k - 1, *item.at((ALLR,), None)),
                    to(h, ll, x, c),
                )
        if number == 2:
            for k in range(1, lay.L):
                ll = (l + k) % lay.L
                send(
                    self.one_a, (0, *item.at((ALLR, ll), 0)),
                    self.two_a, (k - 1, *item.at((ALLR,), 0)),
                    to(h, ll, x, c),
                )
            for k in range(1, lay.X):
                xx = (x + k) % lay.X
                send(
                    self.one_b, (0, *item.at((ALLR,), xx)),
                    self.two_b, (k - 1, *item.at((ALLR,), 0)),
                    to(h, l, xx, c),
                )
        if number == 3:
            for k in range(1, lay.H):
                hh = (h + k) % lay.H
                for src, dst in ((self.two_a, self.top_a), (self.two_b, self.top_b)):
                    send(src, (0, *item.at((hh,), 0)), dst, (k - 1, *item.at((), 0)), to(hh, l, x, c))
        self.sent += begin(copies)
        self.flying = copies

    def fold(self, number):
        item, lay = self.item, self.item.lay
        h, l, x, c = lay.here()
        arrive(self.flying)

        def over_high(body):
            def step(high, carry):
                body(high)
                return carry

            lax.fori_loop(0, lay.H, step, 0)

        def add(target, index, source, source_index, extra):
            total = source[source_index].astype(f32) + target[(0, *index)].astype(f32)
            for other in range(1, extra):
                total = total + target[(other, *index)].astype(f32)
            target[(0, *index)] = total.astype(bf16)

        if number == 0:

            def core(high):
                for low in range(lay.L):
                    for part in range(lay.X):
                        add(
                            self.core, item.at((high, low), part),
                            self.full, item.at((high, low), part * lay.C + c), lay.C - 1,
                        )

            over_high(core)
        if number == 1:

            def one(high):
                for low in range(lay.L):
                    add(
                        self.one_a, item.at((high, low), 0),
                        self.core, (0, *item.at((high, low), x, item.rows_a())), lay.X - 1,
                    )
                add(
                    self.one_b, item.at((high,), None),
                    self.core, (0, *item.at((high, l), None, item.rows_b())), lay.L - 1,
                )

            over_high(one)
        if number == 2:

            def two(high):
                add(self.two_a, item.at((high,), 0), self.one_a, (0, *item.at((high, l), 0)), lay.L - 1)
                add(self.two_b, item.at((high,), 0), self.one_b, (0, *item.at((high,), x)), lay.X - 1)

            over_high(two)
        if number == 3:
            for rows, mine, others in (
                (item.rows_a(), self.two_a, self.top_a), (item.rows_b(), self.two_b, self.top_b),
            ):
                total = mine[(0, *item.at((h,), 0))].astype(f32)
                for other in range(lay.H - 1):
                    total = total + others[(other, *item.at((), 0))].astype(f32)
                self.out[:, rows, :] = total

    def close(self):
        for copy in self.sent:
            copy.wait_send()

    @staticmethod
    def count(lay):
        return (lay.C - 1) * lay.X + (lay.X - 1) * 2 + (lay.L - 1) * 2 + (lay.H - 1) * 2


class Total:
    def __init__(self, lay, near, far, sems):
        self.lay, self.near, self.far, self.sems = lay, near, far, sems
        self.sent = []

    def over_mp(self, value):
        dp, mp = lax.axis_index("dp"), lax.axis_index("mp")
        self.near[mp] = value
        self.flying = begin([
            self.sems.copy(self.near.at[mp], self.near.at[mp], (dp, (mp + k) % self.lay.mp))
            for k in range(1, self.lay.mp)
        ])
        self.sent += self.flying

    def over_dp(self):
        dp, mp = lax.axis_index("dp"), lax.axis_index("mp")
        arrive(self.flying)
        total = self.near[0]
        for other in range(1, self.lay.mp):
            total = total + self.near[other]
        self.far[dp] = total
        self.flying = begin([
            self.sems.copy(self.far.at[dp], self.far.at[dp], ((dp + k) % self.lay.dp, mp))
            for k in range(1, self.lay.dp)
        ])
        self.sent += self.flying

    def result(self):
        arrive(self.flying)
        total = self.far[0]
        for other in range(1, self.lay.dp):
            total = total + self.far[other]
        return total

    def close(self):
        for copy in self.sent:
            copy.wait_send()

    @staticmethod
    def count(lay):
        return lay.mp - 1 + lay.dp - 1


def greet(lay):
    barrier = pltpu.get_barrier_semaphore()
    dp, mp = lax.axis_index("dp"), lax.axis_index("mp")
    for k in range(1, lay.mp):
        pl.semaphore_signal(barrier, inc=1, device_id=(dp, (mp + k) % lay.mp), device_id_type=MESH)
    for k in range(1, lay.dp):
        pl.semaphore_signal(barrier, inc=1, device_id=((dp + k) % lay.dp, mp), device_id_type=MESH)


def await_all(lay):
    pl.semaphore_wait(pltpu.get_barrier_semaphore(), lay.mp + lay.dp - 2)


def spread_rows(row):
    return jnp.concatenate([row[:, at : at + 128] for at in range(0, row.shape[1], 128)], axis=0)


def joined_row(rows):
    return jnp.concatenate([rows[at : at + 1] for at in range(rows.shape[0])], axis=1)


def diagonal_column(row, count):
    same = iota((count, count), 0) == iota((count, count), 1)
    return jnp.sum(jnp.where(same, jnp.broadcast_to(row, (count, count)), 0.0), axis=1, keepdims=True)


def spot(width):
    at = (lax.axis_index("dp") * lax.axis_size("mp") + lax.axis_index("mp")) * width
    return (iota((width, WIDTH), 1) == iota((width, WIDTH), 0) + at).astype(bf16)


def packing(r, c):
    return 128 // c if c < 128 and (r * c // 128) % 16 == 0 else 1


def step_kernel(
    lay, gathers, scatter_items, total_tokens,
    tokens_ref, cotangent_ref, segment_ref, gains_in, mixer_hbm, feed_hbm, sorter_hbm,
    out_hbm, grad_hbm, *refs,
):
    sums_hbm, scratch = refs[:6], list(refs[6:])

    def pop(count):
        taken = scratch[:count]
        del scratch[:count]
        return taken

    shards, weights_full, grads_full = pop(5), pop(5), pop(5)
    kv_ref, sorter_full, woq_ref, feed_a_ref, feed_b_ref = weights_full
    dfeed_a_ref, dfeed_b_ref, dwoq_ref, dkv_ref, dsorter_full = grads_full
    x_ref, cot_ref, out_ref, grad_ref = pop(4)
    (
        sorter_ref, first_ref, q_ref, k_ref, v_ref, sk_ref, sv_ref, place_k_ref, place_v_ref,
        att_ref, mixed_ref, means_ref, sink_ref, logs_ref, segrow_ref, spread_ref, gain_grad_ref,
        second_ref, act_ref, pre_ref, total_ref, second_grad_ref,
    ) = pop(22)
    dk_ref, dv_ref = total_ref, second_grad_ref
    near_a, far_a, near_b, far_b, send_sems, recv_sems, copy_sems = pop(7)
    sems = Sems(send_sems, recv_sems)
    fetch_x = pltpu.make_async_copy(tokens_ref, x_ref, copy_sems.at[0])
    fetch_cot = pltpu.make_async_copy(cotangent_ref, cot_ref, copy_sems.at[1])
    mixer_in, feed_in, sorter_in = pop(3)
    fetches = [
        pltpu.make_async_copy(source, target, copy_sems.at[5 + k])
        for k, (source, target) in enumerate(
            ((mixer_hbm, mixer_in), (sorter_hbm, sorter_in), (feed_hbm, feed_in))
        )
    ]
    begin(fetches)
    fetch_x.start()
    fetch_cot.start()
    mp = lax.axis_index("mp")
    greet(lay)
    gather = [Gather(item, shard, full, sems) for item, shard, full in zip(gathers, shards, weights_full)]
    early = tuple(gather[:2])
    gather_woq, gather_a, gather_b = gather[2:]
    scatters = []
    *outs, small_out = sums = pop(6)
    for item, full, out in zip(scatter_items, grads_full, outs):
        scatters.append(Scatter(item, full, pop(7), out, sems))
    write_sums = [
        pltpu.make_async_copy(buffer, target, copy_sems.at[8 + k])
        for k, (buffer, target) in enumerate(zip(sums, sums_hbm))
    ]
    scatter_a, scatter_b, scatter_woq, scatter_kv, scatter_sorter = scatters
    total_a = Total(lay, near_a, far_a, sems)
    total_b = Total(lay, near_b, far_b, sems)

    def each(group, name, *args):
        for member in group:
            getattr(member, name)(*args)

    width = gains_in.shape[1]
    lane = iota((BLOCKS, SEQ_LEN), 1)
    row = segment_ref[pl.ds(mp, 1), :].astype(f32)
    picked = jnp.where(lane // BLOCK == iota((BLOCKS, SEQ_LEN), 0), jnp.broadcast_to(row, (BLOCKS, SEQ_LEN)), 0.0)
    seg = picked[:, :PAIRS]
    for at in range(PAIRS, SEQ_LEN, PAIRS):
        seg = seg + picked[:, at : at + PAIRS]
    tiling = (iota((PAIRS, PAIRS), 0) % BLOCK == iota((PAIRS, PAIRS), 1) % BLOCK).astype(bf16)
    seg = exact_dot(seg, tiling)
    segrow_ref[...] = seg
    real_col = (seg[:, 0:1] > 0).astype(f32)
    count = jnp.broadcast_to(jnp.sum(real_col, axis=0, keepdims=True), (8, 128))
    placed = exact_dot(gains_in[...], spot(width))
    small = jnp.concatenate([spread_rows(placed[0:1]), spread_rows(placed[1:2]), count], axis=0)
    for fetch in fetches:
        fetch.wait()
    for j, source in enumerate((1, 2)):
        shards[0][j] = mixer_in[:, source, :].astype(bf16)
    pack = packing(*sorter_in.shape)
    deep = sorter_in.shape[0] // pack
    sorter_shard = sorter_in[...].astype(bf16)
    shards[1][0] = jnp.concatenate([sorter_shard[k * deep : (k + 1) * deep] for k in range(pack)], axis=1)
    for j, source in enumerate((3, 0)):
        shards[2][j] = mixer_in[:, source, :].astype(bf16)
    half_width = feed_in.shape[2] // 2
    for j in range(2):
        shards[3][j] = feed_in[:, j, :half_width].astype(bf16)
        shards[4][j] = feed_in[:, j, half_width:].astype(bf16)
    each(gather, "place")
    lane_block = iota((BLOCKS, LOGITS), 1) % BLOCKS
    real_row = jnp.sum(jnp.where(iota((BLOCKS, LOGITS), 0) == lane_block, real_col, 0.0), axis=0, keepdims=True)
    allowed = permitted(real_col, real_row)
    await_all(lay)
    each(early, "stage", 0)
    total_a.over_mp(small)
    gather_woq.stage(0)
    fetch_x.wait()

    def norm_rows(tile, carry):
        rows = pl.ds(pl.multiple_of(tile * ROWS, ROWS), ROWS)
        total_ref[rows, :] = normalize(x_ref[rows, :].astype(f32))[0]
        return carry

    lax.fori_loop(0, TILES, norm_rows, 0)
    total_a.over_dp()
    each(early, "landed")
    each(early, "stage", 1)
    gather_a.stage(0)
    each(early, "landed")
    each(early, "stage", 2)
    gather_woq.landed()
    gather_woq.stage(1)
    summed = total_a.result()
    gain_first = joined_row(summed[0:4])
    gain_second = joined_row(summed[4:8])
    entropy_weight = penalty_weight * total_tokens / (summed[8:9, 0:1] * HEADS)

    def norm_first(tile, carry):
        rows = pl.ds(pl.multiple_of(tile * ROWS, ROWS), ROWS)
        first_ref[rows, :] = (total_ref[rows, :] * gain_first).astype(bf16)
        return carry

    lax.fori_loop(0, TILES, norm_first, 0)
    member = (iota((BLOCKS, SEQ_LEN), 0) == iota((BLOCKS, SEQ_LEN), 1) // BLOCK).astype(bf16)
    means = (mm(member, first_ref[...]) / BLOCK).astype(bf16)
    means_ref[...] = means
    gather_b.stage(0)
    each(early, "landed")
    each(early, "stage", 3)
    gather_a.landed()
    gather_a.stage(1)
    gather_woq.landed()
    gather_woq.stage(2)
    each(early, "landed")

    def weight(ref, j, cols=slice(None)):
        if len(ref.shape) == 6:
            parts = [ref[j, :, :, part].reshape(WIDTH, ref.shape[-1]) for part in range(lay.mp)]
            return jnp.concatenate(parts, axis=1)
        tile = ref[j, :, :, :, cols]
        return tile.reshape(WIDTH, tile.shape[-1])

    r, c = sorter_in.shape

    def sorter_places():
        for high in range(lay.H):
            for low in range(lay.L):
                for part in range(lay.mp):
                    base = (high * lay.L + low) * r
                    if pack == 1:
                        index = (0, high, low, part)
                    else:
                        index = (0, high, low, slice(None), slice(part * 128, (part + 1) * 128))
                    rows = [slice(base + k * deep, base + (k + 1) * deep) for k in range(pack)]
                    yield index, rows, slice(part * c, (part + 1) * c)

    for index, rows, cols in sorter_places():
        tile = sorter_full[index]
        for k in range(pack):
            sorter_ref[rows[k], cols] = tile[:, k * c : (k + 1) * c]
    logits = mm(means, sorter_ref[...])
    for tile in range(TILES):
        rows = slice(tile * ROWS, (tile + 1) * ROWS)
        k_ref[rows, :] = mm(first_ref[rows, :], weight(kv_ref, 0)).astype(bf16)
        v_ref[rows, :] = mm(first_ref[rows, :], weight(kv_ref, 1)).astype(bf16)

    def store(index, value):
        sink_ref[index] = value

    logs, weights = sinkhorn(logits, allowed, group_matrix(), store)
    logs_ref[...] = logs
    probs = weights.astype(bf16)
    gather_a.landed()
    gather_a.stage(2)
    gather_woq.landed()
    gather_woq.stage(3)
    gather_b.landed()
    gather_b.stage(1)
    place_k_ref[...] = by_place(k_ref[...])
    place_v_ref[...] = by_place(v_ref[...])
    first_head = iota((SPAN, 2 * PAIR), 1) % PAIR < HEAD_DIM

    def rearrange(matrices, keys, values, finish_pair):
        for pair in range(HEADS // 2):
            lanes = slice(pair * PAIR, (pair + 1) * PAIR)
            one, two = matrices(2 * pair), matrices(2 * pair + 1)
            outs = []
            for part in range(SEQ_LEN // SPAN):
                rows = slice(part * SPAN, (part + 1) * SPAN)
                both = jnp.concatenate([keys[rows, lanes], values[rows, lanes]], axis=1)
                outs.append(jnp.where(first_head, mm(one, both), mm(two, both)))
            out = jnp.concatenate(outs, axis=0)
            finish_pair(lanes, out[:, :PAIR], out[:, PAIR:])

    def forth(head):
        return repeated(probs[:, head * BLOCKS : (head + 1) * BLOCKS])

    def keep_sorted(lanes, keys, values):
        sk_ref[:, lanes] = by_place(keys.astype(bf16))
        sv_ref[:, lanes] = by_place(values.astype(bf16))

    rearrange(forth, place_k_ref, place_v_ref, keep_sorted)
    gather_woq.landed()

    def project_queries(tile, carry):
        rows = pl.ds(pl.multiple_of(tile * ROWS, ROWS), ROWS)
        q_ref[rows, :] = mm(first_ref[rows, :], weight(woq_ref, 1)).astype(bf16)
        return carry

    lax.fori_loop(0, TILES, project_queries, 0)

    def block_rows(block):
        return pl.ds(pl.multiple_of(block * BLOCK, BLOCK), BLOCK)

    def operands(block, group):
        rows = block_rows(block)
        lanes = slice(group * LANES, (group + 1) * LANES)
        keys = jnp.concatenate([k_ref[rows, lanes], sk_ref[rows, lanes]], axis=0)
        values = jnp.concatenate([v_ref[rows, lanes], sv_ref[rows, lanes]], axis=0)
        return keys, values

    def attend(step, carry):
        for block in [step * UNROLL + k for k in range(UNROLL)]:
            rows = block_rows(block)
            row = segrow_ref[pl.ds(block, 1), :]
            near = diagonal_column(row[:, :BLOCK], BLOCK) == row
            far = jnp.broadcast_to(row > 0, (BLOCK, PAIRS))
            mask = jnp.concatenate([near, far], axis=0)
            for group in range(GROUPS):
                lanes = slice(group * LANES, (group + 1) * LANES)
                keys, values = operands(block, group)
                scores = mm(keys, by_pack(q_ref[rows, lanes]), 1, 1) * (HEAD_DIM ** -0.5)
                scores = jnp.where(mask, scores, excluded_fill)
                shifted = jnp.exp(scores - jnp.max(scores, axis=0, keepdims=True))
                attention = shifted * (1.0 / jnp.sum(shifted, axis=0, keepdims=True))
                att_ref[block, group] = attention
                mixed_ref[rows, lanes] = own_heads(mm(attention.astype(bf16), values, 0, 0)).astype(bf16)
        return carry

    half = BLOCKS // UNROLL // 2
    lax.fori_loop(0, 2 * half, attend, 0)
    gather_a.landed()
    gather_a.stage(3)
    gather_b.landed()
    gather_b.stage(2)
    fetch_cot.wait()
    gain_grad_ref[...] = jnp.zeros_like(gain_grad_ref)

    def keep(ref, j, cols, value):
        if len(ref.shape) == 6:
            for part in range(lay.mp):
                piece = value[:, part * ref.shape[-1] : (part + 1) * ref.shape[-1]]
                ref[j, :, :, part] = piece.astype(bf16).reshape(lay.H, lay.L, WIDTH // lay.dp, ref.shape[-1])
            return
        ref[j, :, :, :, cols] = value.astype(bf16).reshape(lay.H, lay.L, WIDTH // lay.dp, value.shape[1])

    def open_rows(tile, carry):
        rows = pl.ds(pl.multiple_of(tile * ROWS, ROWS), ROWS)
        middle = x_ref[rows, :].astype(f32) + mm(mixed_ref[rows, :], weight(woq_ref, 0), 1, 1)
        grad_ref[rows, :] = middle
        normed, _ = normalize(middle)
        second_ref[rows, :] = (normed * gain_second).astype(bf16)
        return carry

    def feed_rows(feed_ref, rows, total, second_grad):
        second, cot = second_ref[rows, :], cot_ref[rows, :]
        for part in range(feed_ref.shape[-1] // WIDTH):
            cols = slice(part * WIDTH, (part + 1) * WIDTH)
            up, down = weight(feed_ref, 0, cols), weight(feed_ref, 1, cols)
            pre = mm(second, up)
            act = jnp.maximum(pre, 0.0).astype(bf16)
            act_ref[rows, cols] = act
            total = total + mm(act, down, 1, 1)
            pre_grad = jnp.where(pre > 0, mm(cot, down), 0.0).astype(bf16)
            pre_ref[rows, cols] = pre_grad
            partial = mm(pre_grad, up, 1, 1)
            second_grad = partial if second_grad is None else second_grad + partial
        return total, second_grad

    def feed_a(tile, carry):
        rows = pl.ds(pl.multiple_of(tile * ROWS, ROWS), ROWS)
        total, second_grad = feed_rows(feed_a_ref, rows, grad_ref[rows, :], None)
        total_ref[rows, :] = total
        second_grad_ref[rows, :] = second_grad
        return carry

    def feed_b(tile, carry):
        rows = pl.ds(pl.multiple_of(tile * ROWS, ROWS), ROWS)
        total, second_grad = feed_rows(feed_b_ref, rows, total_ref[rows, :], second_grad_ref[rows, :])
        out_ref[rows, :] = total.astype(bf16)
        normed, inverse = normalize(grad_ref[rows, :])
        grad_ref[rows, :] = cot_ref[rows, :].astype(f32) + norm_back(second_grad, normed, inverse, gain_second)
        gain_grad_ref[8:16, :] += jnp.sum((second_grad * normed).reshape(ROWS // 8, 8, WIDTH), axis=0)
        return carry

    def feed_weights(dfeed_ref):
        def run(part, carry):
            cols = pl.ds(pl.multiple_of(part * WIDTH, WIDTH), WIDTH)
            keep(dfeed_ref, 0, cols, mm(second_ref[...], pre_ref[:, cols], 0, 0))
            keep(dfeed_ref, 1, cols, mm(cot_ref[...], act_ref[:, cols], 0, 0))
            return carry

        lax.fori_loop(0, dfeed_ref.shape[-1] // WIDTH, run, 0)

    lax.fori_loop(0, TILES, open_rows, 0)
    gather_a.landed()
    lax.fori_loop(0, TILES, feed_a, 0)
    gather_b.landed()
    gather_b.stage(3)
    feed_weights(dfeed_a_ref)
    scatter_a.stage(0)
    gather_b.landed()
    lax.fori_loop(0, TILES // 2, feed_b, 0)
    scatter_a.fold(0)
    scatter_a.stage(1)
    lax.fori_loop(TILES // 2, TILES, feed_b, 0)
    write_out = pltpu.make_async_copy(out_ref, out_hbm, copy_sems.at[2])
    write_out.start()
    feed_weights(dfeed_b_ref)
    scatter_b.stage(0)
    keep(dwoq_ref, 0, slice(None), mm(grad_ref[...].astype(bf16), mixed_ref[...], 0, 0))

    def start(tile, carry):
        rows = pl.ds(pl.multiple_of(tile * ROWS, ROWS), ROWS)
        mixed_ref[rows, :] = mm(grad_ref[rows, :].astype(bf16), weight(woq_ref, 0)).astype(bf16)
        return carry

    lax.fori_loop(0, TILES, start, 0)
    scatter_a.fold(1)
    scatter_a.stage(2)
    scatter_b.fold(0)
    scatter_b.stage(1)

    def attend_back(step, carry):
        units = [(step * UNROLL + k, group) for k in range(UNROLL) for group in range(GROUPS)]

        def mixed_pack(block, group):
            return by_pack(mixed_ref[block_rows(block), group * LANES : (group + 1) * LANES])

        for block, group in units:
            rows, at = block_rows(block), group * LANES
            keys, values = operands(block, group)
            attention = att_ref[block, group]
            prob_grad = mm(values, mixed_pack(block, group), 1, 1)
            inner = jnp.sum(attention * prob_grad, axis=0, keepdims=True)
            score_grad = (attention * (prob_grad - inner) * (HEAD_DIM ** -0.5)).astype(bf16)
            pre_ref[rows, WIDTH + at : WIDTH + at + PAIRS] = score_grad[:BLOCK]
            pre_ref[rows, WIDTH + at + PAIRS : WIDTH + at + 2 * PAIRS] = score_grad[BLOCK:]
            pre_ref[rows, at : at + LANES] = own_heads(mm(score_grad, keys, 0, 0)).astype(bf16)
        for block, group in units:
            rows, at = block_rows(block), group * LANES
            lanes = slice(at, at + LANES)
            score_grad = jnp.concatenate(
                [pre_ref[rows, WIDTH + at : WIDTH + at + PAIRS], pre_ref[rows, WIDTH + at + PAIRS : WIDTH + at + 2 * PAIRS]],
                axis=0,
            )
            key_grad = mm(score_grad, by_pack(q_ref[rows, lanes]))
            value_grad = mm(att_ref[block, group].astype(bf16), mixed_pack(block, group))
            dk_ref[rows, lanes] = key_grad[:BLOCK]
            dv_ref[rows, lanes] = value_grad[:BLOCK]
            act_ref[rows, lanes] = key_grad[BLOCK:].astype(bf16)
            act_ref[rows, WIDTH + at : WIDTH + at + LANES] = value_grad[BLOCK:].astype(bf16)
        return carry

    lax.fori_loop(0, 2 * half, attend_back, 0)
    scatter_a.fold(2)
    scatter_a.stage(3)
    first = first_ref[...]
    q_ref[...] = pre_ref[:, :WIDTH]
    keep(dwoq_ref, 1, slice(None), mm(first, q_ref[...], 0, 0))
    scatter_woq.stage(0)
    weights = sink_ref[2 * SINK_ITERS - 1]
    same_head = iota((LOGITS, LOGITS), 0) // BLOCKS == iota((LOGITS, LOGITS), 1) // BLOCKS
    turned = jnp.where(same_head, jnp.concatenate([weights] * HEADS, axis=0), 0.0).T

    def back(head):
        rows = slice(head * BLOCKS, (head + 1) * BLOCKS)
        return repeated(turned[rows, rows].astype(bf16))

    sk_ref[...] = by_place(act_ref[:, :WIDTH])
    sv_ref[...] = by_place(act_ref[:, WIDTH:])

    def add_pair(lanes, keys, values):
        k_ref[:, lanes] = (dk_ref[:, lanes] + by_place(keys)).astype(bf16)
        v_ref[:, lanes] = (dv_ref[:, lanes] + by_place(values)).astype(bf16)

    rearrange(back, sk_ref, sv_ref, add_pair)
    scatter_b.fold(1)
    scatter_b.stage(2)
    scatter_woq.fold(0)
    scatter_woq.stage(1)
    keep(dkv_ref, 0, slice(None), mm(first, k_ref[...], 0, 0))
    keep(dkv_ref, 1, slice(None), mm(first, v_ref[...], 0, 0))
    scatter_kv.stage(0)
    lane_head = iota((SPAN, PAIR), 1) // HEAD_DIM
    diagonal = iota((SPAN, SPAN), 0) // BLOCKS == iota((SPAN, SPAN), 1) // BLOCKS
    folded = []
    for pair in range(HEADS // 2):
        lanes = slice(pair * PAIR, (pair + 1) * PAIR)
        parts = [slice(part * SPAN, (part + 1) * SPAN) for part in range(SEQ_LEN // SPAN)]
        right = [ref[rows, lanes] for rows in parts for ref in (place_k_ref, place_v_ref)]
        left = [ref[rows, lanes] for rows in parts for ref in (sk_ref, sv_ref)]
        for head in range(2):
            mine = [jnp.where(lane_head == head, tile, jnp.zeros_like(tile)) for tile in left]
            square = mm(jnp.concatenate(mine, axis=1), jnp.concatenate(right, axis=1), 1, 1)
            square = jnp.where(diagonal, square, 0.0)
            total = square[:BLOCKS]
            for place in range(1, STACK):
                total = total + square[place * BLOCKS : (place + 1) * BLOCKS]
            folded.append(total)
    copies = (iota((BLOCKS, LOGITS), 0) == iota((BLOCKS, LOGITS), 1) % BLOCKS).astype(bf16)
    stacked = exact_dot(jnp.concatenate(folded, axis=0), copies.T)
    wide = jnp.where(same_head, exact_dot(stacked, copies), 0.0)
    probs_grad = wide[:BLOCKS]
    for head in range(1, HEADS):
        probs_grad = probs_grad + wide[head * BLOCKS : (head + 1) * BLOCKS]
    logs = logs_ref[...]
    pull = jnp.where(real_col > 0, entropy_weight * (logs + 1.0), 0.0)
    scatter_kv.fold(0)
    scatter_kv.stage(1)
    grad = sinkhorn_back(weights * (probs_grad - pull), group_matrix(), lambda index: sink_ref[index])
    logit_grad = jnp.where(allowed, grad / softness_factor, 0.0).astype(bf16)
    sorter_grad = mm(means_ref[...], logit_grad, 0, 0).astype(bf16)
    for index, rows, cols in sorter_places():
        pieces = [sorter_grad[rows[k], cols] for k in range(pack)]
        dsorter_full[index] = jnp.concatenate(pieces, axis=1) if pack > 1 else pieces[0]
    scatter_sorter.stage(0)
    scatter_b.fold(2)
    scatter_b.stage(3)
    spread_ref[...] = mm(logit_grad, sorter_ref[...], 1, 1) / BLOCK
    here = ROWS // BLOCK

    def finish(tile, carry):
        rows = pl.ds(pl.multiple_of(tile * ROWS, ROWS), ROWS)
        spread = spread_ref[pl.ds(pl.multiple_of(tile * here, here), here), :]
        spread = jnp.broadcast_to(spread[:, None, :], (here, BLOCK, WIDTH)).reshape(ROWS, WIDTH)
        first_grad = (
            mm(q_ref[rows, :], weight(woq_ref, 1), 1, 1)
            + mm(k_ref[rows, :], weight(kv_ref, 0), 1, 1)
            + mm(v_ref[rows, :], weight(kv_ref, 1), 1, 1)
            + spread
        )
        normed, inverse = normalize(x_ref[rows, :].astype(f32))
        grad_ref[rows, :] += norm_back(first_grad, normed, inverse, gain_first)
        gain_grad_ref[0:8, :] += jnp.sum((first_grad * normed).reshape(ROWS // 8, 8, WIDTH), axis=0)
        return carry

    writes = []

    def write_rows(part):
        rows = slice(part * SEQ_LEN // 2, (part + 1) * SEQ_LEN // 2)
        copy = pltpu.make_async_copy(grad_ref.at[rows], grad_hbm.at[rows], copy_sems.at[3 + part])
        copy.start()
        writes.append(copy)

    lax.fori_loop(0, TILES // 2, finish, 0)
    write_rows(0)
    scatter_woq.fold(1)
    scatter_woq.stage(2)
    scatter_sorter.fold(0)
    scatter_sorter.stage(1)
    lax.fori_loop(TILES // 2, TILES, finish, 0)
    write_rows(1)
    entropy = -jnp.sum(jnp.where(real_col > 0, weights * logs, 0.0), axis=0, keepdims=True)
    entropy = jnp.broadcast_to(entropy[:, :128] + entropy[:, 128:], (8, 128))
    total_b.over_mp(jnp.concatenate([
        spread_rows(jnp.sum(gain_grad_ref[0:8, :], axis=0, keepdims=True)),
        spread_rows(jnp.sum(gain_grad_ref[8:16, :], axis=0, keepdims=True)),
        entropy,
    ], axis=0))
    scatter_kv.fold(1)
    scatter_kv.stage(2)
    scatter_woq.fold(2)
    scatter_woq.stage(3)
    scatter_sorter.fold(1)
    scatter_sorter.stage(2)
    total_b.over_dp()
    scatter_kv.fold(2)
    scatter_kv.stage(3)
    scatter_sorter.fold(2)
    scatter_sorter.stage(3)
    scatter_a.fold(3)
    write_sums[0].start()
    scatter_b.fold(3)
    write_sums[1].start()
    small_out[0:16, :] = total_b.result()
    small_out[16:24, :] = summed[8:16]
    write_sums[5].start()
    scatter_woq.fold(3)
    write_sums[2].start()
    write_out.wait()
    for copy in writes:
        copy.wait()
    each(tuple(gather) + (scatter_a, scatter_b, total_a, total_b), "close")
    scatter_kv.fold(3)
    write_sums[3].start()
    scatter_sorter.fold(3)
    write_sums[4].start()
    each((scatter_woq, scatter_kv, scatter_sorter), "close")
    for copy in write_sums:
        copy.wait()


def update_kernel(lay, step_ref, *refs):
    sources, targets, penalty_out, inputs, results = refs[:20], refs[20:34], refs[34], refs[35:55], refs[55:67]
    in_sems, out_sems = refs[67:]
    bring = [pltpu.make_async_copy(source, inputs[k], in_sems.at[k]) for k, source in enumerate(sources)]
    begin(bring[2:] + bring[:2])
    send = [
        pltpu.make_async_copy(buffer, targets[k], out_sems.at[k])
        for k, buffer in enumerate(tuple(inputs[:2]) + tuple(results))
    ]
    feed_a, feed_b, woq, kv, sorter, sums = inputs[2:8]
    masters = inputs[8:]
    step_value = jnp.full((1, 128), step_ref[0], jnp.int32).astype(f32)
    scale_first = 1.0 / (1.0 - jnp.exp(step_value * math.log(beta_first)))[:, 0:1]
    scale_second = 1.0 / (1.0 - jnp.exp(step_value * math.log(beta_second)))[:, 0:1]

    def adamw(which, index, grad, rate):
        master, moment, second = [ref[index] for ref in masters[3 * which : 3 * which + 3]]
        moment_new = beta_first * moment + (1.0 - beta_first) * grad
        second_new = beta_second * second + (1.0 - beta_second) * grad * grad
        change = (moment_new * scale_first) / (jnp.sqrt(second_new * scale_second) + adam_eps)
        outs = results[3 * which : 3 * which + 3]
        outs[0][index] = moment_new
        outs[1][index] = second_new
        outs[2][index] = master - rate * (change + weight_decay * master)

    for copy in bring[2:]:
        copy.wait()
    half = feed_a.shape[2]
    for j in range(2):
        adamw(1, (ALLR, j, slice(0, half)), feed_a[j], rate_feed)
        adamw(1, (ALLR, j, slice(half, 2 * half)), feed_b[j], rate_feed)
    begin(send[5:8])
    for copy in bring[:2]:
        copy.wait()
    begin(send[:2])
    for j, grad in enumerate((woq[1], kv[0], kv[1], woq[0])):
        adamw(0, (ALLR, j, ALLR), grad, rate_mixer)
    begin(send[2:5])
    r, c = masters[6].shape
    pack = packing(r, c)
    deep = r // pack
    grad = jnp.concatenate([sorter[0][:, k * c : (k + 1) * c] for k in range(pack)], axis=0) if pack > 1 else sorter[0]
    adamw(2, (ALLR, ALLR), grad, rate_sorter)
    begin(send[8:11])
    rows = jnp.concatenate([joined_row(sums[0:4, :]), joined_row(sums[4:8, :])], axis=0)
    own = spot(masters[9].shape[1])
    grad = sum(mm(part, own, 1, 1) for part in three_parts(rows))
    adamw(3, (ALLR, ALLR), grad, rate_gains)
    begin(send[11:14])
    entropy = jnp.sum(sums[8:9, :], axis=1, keepdims=True)
    penalty_out[...] = jnp.broadcast_to(entropy / (sums[16:17, 0:1] * HEADS), (1, 128))
    for copy in send:
        copy.wait()


def shape(dims, dtype):
    return jax.ShapeDtypeStruct(dims, dtype)


LIMIT = 63 * 1024 * 1024
TOK = (SEQ_LEN, WIDTH)


def run_step(lay, total_tokens, tokens, cotangent, segment_ids, gains, mixer, feed, sorter):
    r, c, half = mixer.shape[0], mixer.shape[2], feed.shape[2] // 2
    pack = packing(*sorter.shape)
    sorter_item = Item(lay, 1, sorter.shape[0] // pack, sorter.shape[1] * pack)
    feed_item, pair_item = Item(lay, 2, r, half), Item(lay, 2, r, c)
    gathers = (pair_item, sorter_item, pair_item, feed_item, feed_item)
    scatters = (feed_item, feed_item, pair_item, pair_item, sorter_item)
    vm = pltpu.VMEM
    count = 5 * (Gather.count(lay) + Scatter.count(lay)) + 2 * Total.count(lay)
    scratch = (
        [vm(item.shard(), bf16) for item in gathers]
        + [vm(item.full(), bf16) for item in gathers + scatters]
        + [vm(TOK, bf16), vm(TOK, bf16), vm(TOK, bf16), vm(TOK, f32)]
        + [vm((WIDTH, LOGITS), bf16)]
        + [vm(TOK, bf16)] * 8
        + [
            vm((BLOCKS, GROUPS, 2 * BLOCK, PAIRS), f32), vm(TOK, bf16), vm((BLOCKS, WIDTH), bf16),
            vm((2 * SINK_ITERS, BLOCKS, LOGITS), f32), vm((BLOCKS, LOGITS), f32),
            vm((BLOCKS, PAIRS), f32), vm((BLOCKS, WIDTH), f32), vm((16, WIDTH), f32),
            vm(TOK, bf16), vm((SEQ_LEN, HIDDEN // 2), bf16), vm((SEQ_LEN, HIDDEN // 2), bf16),
        ]
        + [vm(TOK, f32)] * 2
        + [vm((lay.mp, 16, 128), f32), vm((lay.dp, 16, 128), f32)] * 2
        + [pltpu.SemaphoreType.DMA((count,))] * 2
        + [pltpu.SemaphoreType.DMA((14,))]
        + [vm(mixer.shape, f32), vm(feed.shape, f32), vm(sorter.shape, f32)]
        + [vm(item.shard(), f32) for item in scatters]
        + [vm((24, 128), f32)]
    )
    for item in scatters:
        scratch += Scatter.buffers(item)
    inside = pl.BlockSpec(memory_space=pltpu.VMEM)
    outside = pl.BlockSpec(memory_space=pl.ANY)
    return pl.pallas_call(
        functools.partial(step_kernel, lay, gathers, scatters, total_tokens),
        out_shape=[shape(TOK, bf16), shape(TOK, f32)]
        + [shape(item.shard(), f32) for item in scatters]
        + [shape((24, 128), f32)],
        in_specs=[outside] * 2 + [inside] * 2 + [outside] * 3,
        out_specs=[outside] * 8,
        scratch_shapes=scratch,
        compiler_params=pltpu.CompilerParams(collective_id=0, has_side_effects=True, vmem_limit_bytes=LIMIT),
        name="step",
    )(tokens, cotangent, segment_ids, gains, mixer, feed, sorter)


def run_update(lay, step_count, block_output, token_grad, sums, states):
    outside = pl.BlockSpec(memory_space=pl.ANY)
    arrays = (block_output, token_grad, *sums, *states)
    moved = [shape(array.shape, array.dtype) for array in (block_output, token_grad, *states)]
    *moved, penalty = pl.pallas_call(
        functools.partial(update_kernel, lay),
        out_shape=moved + [shape((1, 128), f32)],
        in_specs=[pl.BlockSpec(memory_space=pltpu.SMEM)] + [outside] * len(arrays),
        out_specs=[outside] * len(moved) + [pl.BlockSpec(memory_space=pltpu.VMEM)],
        scratch_shapes=[pltpu.VMEM(array.shape, array.dtype) for array in arrays]
        + [pltpu.VMEM(state.shape, f32) for state in states]
        + [pltpu.SemaphoreType.DMA((len(arrays),)), pltpu.SemaphoreType.DMA((len(moved),))],
        compiler_params=pltpu.CompilerParams(vmem_limit_bytes=LIMIT),
        name="update",
    )(step_count, *arrays)
    return moved[0], moved[1], penalty, moved[2:]


rate_mixer = 0.2
rate_feed = 0.1
rate_sorter = 0.6
rate_gains = 1.0
beta_first = 0.9
beta_second = 0.95
adam_eps = 1e-08
weight_decay = 0.1


def local(
    lay,
    tokens,
    segment_ids,
    cotangent,
    step_count,
    mixer_weights,
    mixer_moment,
    mixer_second,
    feed_weights,
    feed_moment,
    feed_second,
    sorter_weights,
    sorter_moment,
    sorter_second,
    norm_gains,
    gain_moment,
    gain_second,
):
    total_tokens = float(lay.dp * segment_ids.shape[0] * SEQ_LEN)
    block_output, token_grad, *sums = run_step(
        lay, total_tokens, tokens, cotangent, segment_ids, norm_gains, mixer_weights, feed_weights, sorter_weights
    )
    states = (
        mixer_weights, mixer_moment, mixer_second, feed_weights, feed_moment, feed_second,
        sorter_weights, sorter_moment, sorter_second, norm_gains, gain_moment, gain_second,
    )
    block_output, token_grad, penalty, states = run_update(lay, step_count, block_output, token_grad, sums, states)
    return (block_output, token_grad, penalty[0, :1], *states)


def solution(mesh):
    return jax.shard_map(
        functools.partial(local, Layout(mesh.shape["dp"], mesh.shape["mp"])),
        mesh=mesh,
        in_specs=(
            P(("dp", "mp"), None),
            P("dp", None),
            P(("dp", "mp"), None),
            P(),
            P("dp", None, "mp"),
            P("dp", None, "mp"),
            P("dp", None, "mp"),
            P("dp", None, "mp"),
            P("dp", None, "mp"),
            P("dp", None, "mp"),
            P("dp", "mp"),
            P("dp", "mp"),
            P("dp", "mp"),
            P(None, ("dp", "mp")),
            P(None, ("dp", "mp")),
            P(None, ("dp", "mp")),
        ),
        out_specs=(
            P(("dp", "mp"), None),
            P(("dp", "mp"), None),
            P(),
            P("dp", None, "mp"),
            P("dp", None, "mp"),
            P("dp", None, "mp"),
            P("dp", None, "mp"),
            P("dp", None, "mp"),
            P("dp", None, "mp"),
            P("dp", "mp"),
            P("dp", "mp"),
            P("dp", "mp"),
            P(None, ("dp", "mp")),
            P(None, ("dp", "mp")),
            P(None, ("dp", "mp")),
        ),
        check_vma=False,
    )
```

```python
import functools
import math
import jax
import jax.numpy as jnp
from jax import lax
from jax.sharding import PartitionSpec as P
from jax.experimental import pallas as pl
from jax.experimental.pallas import tpu as pltpu

WIDTH = 512
HEADS = 8
HEAD_DIM = 64
HIDDEN = 2048
BLOCK = 32
SINK_ITERS = 8
SEQ_LEN = 1024
BLOCKS = 32
LOGITS = HEADS * BLOCKS
ROWS = 512
TILES = SEQ_LEN // ROWS
PACK = 4
GROUPS = HEADS // PACK
LANES = PACK * HEAD_DIM
PAIRS = PACK * BLOCK
PAIR = 2 * HEAD_DIM
UNROLL = 32
ROW_PARTS = 2

norm_eps = 1e-05
softness_factor = 0.75
excluded_fill = -1000000000.0
penalty_weight = 0.1
bf16 = jnp.bfloat16
f32 = jnp.float32


def mm(a, b, ca=1, cb=0):
    return lax.dot_general(a, b, (((ca,), (cb,)), ((), ())), preferred_element_type=f32)


def iota(shape, dim):
    return lax.broadcasted_iota(jnp.int32, shape, dim)


def normalize(rows):
    centred = rows - jnp.mean(rows, axis=-1, keepdims=True)
    inverse = lax.rsqrt(jnp.mean(centred * centred, axis=-1, keepdims=True) + norm_eps)
    return centred * inverse, inverse


def norm_back(grad_out, normed, inverse, gain):
    scaled = grad_out * gain
    return inverse * (
        scaled
        - jnp.mean(scaled, axis=-1, keepdims=True)
        - normed * jnp.mean(scaled * normed, axis=-1, keepdims=True)
    )


def three_parts(value):
    high = value.astype(bf16)
    rest = value - high.astype(f32)
    mid = rest.astype(bf16)
    low = (rest - mid.astype(f32)).astype(bf16)
    return high, mid, low


def group_matrix():
    return (iota((LOGITS, LOGITS), 0) // BLOCKS == iota((LOGITS, LOGITS), 1) // BLOCKS).astype(bf16)


def exact_dot(value, matrix):
    rows = value.shape[0]
    out = mm(jnp.concatenate(three_parts(value), axis=0), matrix)
    return out[:rows] + out[rows : 2 * rows] + out[2 * rows :]


def head_max(value):
    lane_head = iota(value.shape, 1) // BLOCKS
    out = jnp.zeros_like(value)
    for head in range(HEADS):
        here = lane_head == head
        top = jnp.max(jnp.where(here, value, -jnp.inf), axis=1, keepdims=True)
        out = jnp.where(here, top, out)
    return out


def permitted(real_col, real_row):
    col = iota((BLOCKS, LOGITS), 1) % BLOCKS
    return ((real_col * real_row) > 0) | (iota((BLOCKS, LOGITS), 0) == col)


def sinkhorn(logits, allowed, groups, store):
    logs = jnp.where(allowed, logits / softness_factor, excluded_fill)
    top = head_max(logs)
    logs = logs - (top + jnp.log(exact_dot(jnp.exp(logs - top), groups)))
    store(0, jnp.exp(logs))
    top = jnp.max(logs, axis=0, keepdims=True)
    logs = logs - (top + jnp.log(jnp.sum(jnp.exp(logs - top), axis=0, keepdims=True)))
    weights = jnp.exp(logs)
    store(1, weights)
    for sweep in range(1, SINK_ITERS):
        logs = logs - jnp.log(exact_dot(weights, groups))
        weights = jnp.exp(logs)
        store(2 * sweep, weights)
        logs = logs - jnp.log(jnp.sum(weights, axis=0, keepdims=True))
        weights = jnp.exp(logs)
        store(2 * sweep + 1, weights)
    return logs, weights


def sinkhorn_back(grad, groups, load):
    for sweep in reversed(range(SINK_ITERS)):
        grad = grad - load(2 * sweep + 1) * jnp.sum(grad, axis=0, keepdims=True)
        grad = grad - load(2 * sweep) * exact_dot(grad, groups)
    return grad


def by_pack(tile):
    rows = jnp.concatenate([tile] * PACK, axis=0)
    keep = iota((PAIRS, LANES), 0) // BLOCK == iota((PAIRS, LANES), 1) // HEAD_DIM
    return jnp.where(keep, rows, jnp.zeros_like(rows))


def own_heads(product):
    lane_head = iota((BLOCK, LANES), 1) // HEAD_DIM
    out = product[:BLOCK]
    for head in range(1, PACK):
        out = jnp.where(lane_head == head, product[head * BLOCK : (head + 1) * BLOCK], out)
    return out


STACK = 8
SPAN = STACK * BLOCKS


def by_place(rows):
    lanes = rows.shape[1]
    return jnp.swapaxes(rows.reshape(BLOCKS, BLOCK, lanes), 0, 1).reshape(SEQ_LEN, lanes)


def repeated(matrix):
    wide = jnp.concatenate([matrix] * STACK, axis=1)
    wide = jnp.concatenate([wide] * STACK, axis=0)
    keep = iota((SPAN, SPAN), 0) // BLOCKS == iota((SPAN, SPAN), 1) // BLOCKS
    return jnp.where(keep, wide, jnp.zeros_like(wide))


MESH = pl.DeviceIdType.MESH


class Layout:
    def __init__(self, mesh_dp, mesh_mp):
        self.dp, self.mp = mesh_dp, mesh_mp
        self.C = 2 if mesh_mp % 2 == 0 else 1
        self.X = mesh_mp // self.C
        self.L = 2 if mesh_dp % 2 == 0 else 1
        self.H = mesh_dp // self.L

    def here(self):
        dp, mp = lax.axis_index("dp"), lax.axis_index("mp")
        return dp // self.L, dp % self.L, mp // self.C, mp % self.C


class Item:
    def __init__(self, lay, J, r, c):
        self.lay, self.J, self.r, self.c = lay, J, r, c
        self.direct = c % 128 == 0
        self.half = r // 2

    def shard(self):
        return (self.J, self.r, self.c)

    def dims(self, *lead, rows=None, wide=None):
        rows = self.r if rows is None else rows
        wide = self.lay.mp if wide is None else wide
        if self.direct:
            return (self.J, *lead, rows, wide * self.c)
        return (self.J, *lead, wide, rows, self.c)

    def full(self):
        return self.dims(self.lay.H, self.lay.L)

    def at(self, lead, first, count=1, rows=slice(None)):
        if self.direct:
            start = first * self.c if isinstance(first, int) else pl.multiple_of(first * self.c, 128)
            return (slice(None), *lead, rows, pl.ds(start, count * self.c))
        return (slice(None), *lead, first if count == 1 else pl.ds(first, count), rows, slice(None))

    def rows_a(self):
        return slice(0, self.half)

    def rows_b(self):
        return slice(self.half, self.r)


ALLR = slice(None)


class Sems:
    def __init__(self, send, recv):
        self.send, self.recv = send, recv
        self.sends, self.recvs = 0, 0

    def lane(self, count):
        return Lane(self, count)


class Lane:
    def __init__(self, sems, count):
        self.sems, self.first, self.waiting = sems, sems.sends, []
        sems.sends += count

    def send(self, copies):
        self.close()
        for k, (src, dst, device) in enumerate(copies):
            self.waiting.append(
                pltpu.make_async_remote_copy(
                    src_ref=src,
                    dst_ref=dst,
                    send_sem=self.sems.send.at[self.first + k],
                    recv_sem=self.sems.recv.at[self.sems.recvs + k],
                    device_id=device,
                    device_id_type=MESH,
                )
            )
        self.sems.recvs += len(copies)
        return begin(list(self.waiting))

    def close(self):
        for copy in self.waiting:
            copy.wait_send()
        self.waiting = []


def begin(copies):
    for copy in copies:
        copy.start()
    return copies


def arrive(copies):
    for copy in copies:
        copy.wait_recv()


class Gather:
    def __init__(self, item, shard, full, sems, high_first=True):
        self.item, self.shard, self.full, self.high_first = item, shard, full, high_first
        self.lane = sems.lane(self.sends(item.lay))

    def stage(self, number):
        item, lay, full = self.item, self.item.lay, self.full
        h, l, x, c = lay.here()
        copies = []

        def to(hh, ll, xx, cc):
            return (hh * lay.L + ll, xx * lay.C + cc)

        def same(index, device):
            copies.append((full.at[index], full.at[index], device))

        mine = c * lay.X + x
        if number == 0 and not self.high_first:
            for rows, index, devices in (
                (item.rows_a(), item.at((h, l), mine, 1, item.rows_a()), [to(h, (l + k) % lay.L, x, c) for k in range(1, lay.L)]),
                (item.rows_b(), item.at((h, l), mine, 1, item.rows_b()), [to(h, l, (x + k) % lay.X, c) for k in range(1, lay.X)]),
            ):
                copies += [(self.shard.at[:, rows], full.at[index], device) for device in devices]
        if number == 1 and not self.high_first:
            for k in range(1, lay.H):
                device = to((h + k) % lay.H, l, x, c)
                same(item.at((h, ALLR), mine, 1, item.rows_a()), device)
                same(item.at((h, l), c * lay.X, lay.X, item.rows_b()), device)
        if number == 0 and self.high_first:
            for k in range(1, lay.H):
                copies.append((self.shard, full.at[item.at((h, l), mine)], to((h + k) % lay.H, l, x, c)))
        if number == 1 and self.high_first:
            for k in range(1, lay.L):
                same(item.at((ALLR, l), mine, 1, item.rows_a()), to(h, (l + k) % lay.L, x, c))
            for k in range(1, lay.X):
                same(item.at((ALLR, l), mine, 1, item.rows_b()), to(h, l, (x + k) % lay.X, c))
        if number == 2:
            for k in range(1, lay.X):
                same(item.at((ALLR, ALLR), mine, 1, item.rows_a()), to(h, l, (x + k) % lay.X, c))
            for k in range(1, lay.L):
                same(item.at((ALLR, l), c * lay.X, lay.X, item.rows_b()), to(h, (l + k) % lay.L, x, c))
        if number == 3:
            for k in range(1, lay.C):
                same(item.at((ALLR, ALLR), c * lay.X, lay.X), to(h, l, x, (c + k) % lay.C))
        self.flying = self.lane.send(copies)

    def place(self):
        h, l, x, c = self.item.lay.here()
        self.full[self.item.at((h, l), c * self.item.lay.X + x)] = self.shard[...]

    def landed(self):
        arrive(self.flying)

    def close(self):
        self.lane.close()

    @staticmethod
    def sends(lay):
        return max(2 * (lay.H - 1), lay.L + lay.X - 2, lay.C - 1)

    @staticmethod
    def count(lay):
        return 2 * (lay.H - 1) + 2 * (lay.L + lay.X - 2) + (lay.C - 1)


class Scatter:
    def __init__(self, item, full, buffers, write, sems):
        self.item, self.full, self.write = item, full, write
        self.lane = sems.lane(self.sends(item.lay))
        self.core, self.one_a, self.one_b, self.two_a, self.two_b, self.top_a, self.top_b = buffers

    @staticmethod
    def buffers(item):
        lay = item.lay
        half = item.half
        return [
            pltpu.VMEM((lay.C - 1, *item.dims(lay.H, lay.L, wide=lay.X)), bf16),
            pltpu.VMEM((lay.X - 1, *item.dims(lay.H, lay.L, rows=half, wide=1)), bf16),
            pltpu.VMEM((lay.L - 1, *item.dims(lay.H, rows=half, wide=lay.X)), bf16),
            pltpu.VMEM((lay.L - 1, *item.dims(lay.H, rows=half, wide=1)), bf16),
            pltpu.VMEM((lay.X - 1, *item.dims(lay.H, rows=half, wide=1)), bf16),
            pltpu.VMEM((lay.H - 1, *item.dims(rows=half, wide=1)), bf16),
            pltpu.VMEM((lay.H - 1, *item.dims(rows=half, wide=1)), bf16),
        ]

    def stage(self, number):
        item, lay = self.item, self.item.lay
        h, l, x, c = lay.here()
        copies = []

        def to(hh, ll, xx, cc):
            return (hh * lay.L + ll, xx * lay.C + cc)

        def send(src, src_index, dst, dst_index, device):
            copies.append((src.at[src_index], dst.at[dst_index], device))

        if number == 0:
            for k in range(1, lay.C):
                cc = (c + k) % lay.C
                send(
                    self.full, item.at((ALLR, ALLR), cc * lay.X, lay.X),
                    self.core, (k - 1, *item.at((ALLR, ALLR), 0, lay.X)),
                    to(h, l, x, cc),
                )
        if number == 1:
            for k in range(1, lay.X):
                xx = (x + k) % lay.X
                send(
                    self.core, (0, *item.at((ALLR, ALLR), xx, 1, item.rows_a())),
                    self.one_a, (k - 1, *item.at((ALLR, ALLR), 0)),
                    to(h, l, xx, c),
                )
            for k in range(1, lay.L):
                ll = (l + k) % lay.L
                send(
                    self.core, (0, *item.at((ALLR, ll), 0, lay.X, item.rows_b())),
                    self.one_b, (k - 1, *item.at((ALLR,), 0, lay.X)),
                    to(h, ll, x, c),
                )
        if number == 2:
            for k in range(1, lay.L):
                ll = (l + k) % lay.L
                send(
                    self.one_a, (0, *item.at((ALLR, ll), 0)),
                    self.two_a, (k - 1, *item.at((ALLR,), 0)),
                    to(h, ll, x, c),
                )
            for k in range(1, lay.X):
                xx = (x + k) % lay.X
                send(
                    self.one_b, (0, *item.at((ALLR,), xx)),
                    self.two_b, (k - 1, *item.at((ALLR,), 0)),
                    to(h, l, xx, c),
                )
        if number == 3:
            for k in range(1, lay.H):
                hh = (h + k) % lay.H
                for src, dst in ((self.two_a, self.top_a), (self.two_b, self.top_b)):
                    send(src, (0, *item.at((hh,), 0)), dst, (k - 1, *item.at((), 0)), to(hh, l, x, c))
        self.flying = self.lane.send(copies)

    def fold(self, number):
        item, lay = self.item, self.item.lay
        h, l, x, c = lay.here()
        arrive(self.flying)

        def over_high(body):
            def step(high, carry):
                body(high)
                return carry

            lax.fori_loop(0, lay.H, step, 0)

        def add(target, index, source, source_index, extra):
            total = source[source_index].astype(f32) + target[(0, *index)].astype(f32)
            for other in range(1, extra):
                total = total + target[(other, *index)].astype(f32)
            target[(0, *index)] = total.astype(bf16)

        if number == 0:

            def core(high):
                for low in range(lay.L):
                    add(
                        self.core, item.at((high, low), 0, lay.X),
                        self.full, item.at((high, low), c * lay.X, lay.X), lay.C - 1,
                    )

            over_high(core)
        if number == 1:

            def one(high):
                for low in range(lay.L):
                    add(
                        self.one_a, item.at((high, low), 0),
                        self.core, (0, *item.at((high, low), x, 1, item.rows_a())), lay.X - 1,
                    )
                add(
                    self.one_b, item.at((high,), 0, lay.X),
                    self.core, (0, *item.at((high, l), 0, lay.X, item.rows_b())), lay.L - 1,
                )

            over_high(one)
        if number == 2:

            def two(high):
                add(self.two_a, item.at((high,), 0), self.one_a, (0, *item.at((high, l), 0)), lay.L - 1)
                add(self.two_b, item.at((high,), 0), self.one_b, (0, *item.at((high,), x)), lay.X - 1)

            over_high(two)
        if number == 3:
            for rows, mine, others in (
                (item.rows_a(), self.two_a, self.top_a), (item.rows_b(), self.two_b, self.top_b),
            ):
                total = mine[(0, *item.at((h,), 0))].astype(f32)
                for other in range(lay.H - 1):
                    total = total + others[(other, *item.at((), 0))].astype(f32)
                total = total.reshape(item.J, item.half, item.c)
                for j in range(item.J):
                    self.write(j, rows, total[j])

    def close(self):
        self.lane.close()

    @staticmethod
    def sends(lay):
        return max(lay.C - 1, lay.X + lay.L - 2, 2 * (lay.H - 1))

    @staticmethod
    def count(lay):
        return (lay.C - 1) + 2 * (lay.X + lay.L - 2) + 2 * (lay.H - 1)


class Total:
    def __init__(self, lay, near, far, sems):
        self.lay, self.near, self.far = lay, near, far
        self.lane = sems.lane(self.sends(lay))

    def over_mp(self, value):
        dp, mp = lax.axis_index("dp"), lax.axis_index("mp")
        self.near[mp] = value
        self.flying = self.lane.send([
            (self.near.at[mp], self.near.at[mp], (dp, (mp + k) % self.lay.mp)) for k in range(1, self.lay.mp)
        ])

    def over_dp(self):
        dp, mp = lax.axis_index("dp"), lax.axis_index("mp")
        arrive(self.flying)
        total = self.near[0]
        for other in range(1, self.lay.mp):
            total = total + self.near[other]
        self.far[dp] = total
        self.flying = self.lane.send([
            (self.far.at[dp], self.far.at[dp], ((dp + k) % self.lay.dp, mp)) for k in range(1, self.lay.dp)
        ])

    def result(self):
        arrive(self.flying)
        total = self.far[0]
        for other in range(1, self.lay.dp):
            total = total + self.far[other]
        return total

    def close(self):
        self.lane.close()

    @staticmethod
    def sends(lay):
        return max(lay.mp, lay.dp) - 1

    @staticmethod
    def count(lay):
        return lay.mp - 1 + lay.dp - 1


def greet(lay):
    barrier = pltpu.get_barrier_semaphore()
    dp, mp = lax.axis_index("dp"), lax.axis_index("mp")
    for k in range(1, lay.mp):
        pl.semaphore_signal(barrier, inc=1, device_id=(dp, (mp + k) % lay.mp), device_id_type=MESH)
    for k in range(1, lay.dp):
        pl.semaphore_signal(barrier, inc=1, device_id=((dp + k) % lay.dp, mp), device_id_type=MESH)


def await_all(lay):
    pl.semaphore_wait(pltpu.get_barrier_semaphore(), lay.mp + lay.dp - 2)


def spread_rows(row):
    return jnp.concatenate([row[:, at : at + 128] for at in range(0, row.shape[1], 128)], axis=0)


def joined_row(rows):
    return jnp.concatenate([rows[at : at + 1] for at in range(rows.shape[0])], axis=1)


def diagonal_column(row, count):
    same = iota((count, count), 0) == iota((count, count), 1)
    return jnp.sum(jnp.where(same, jnp.broadcast_to(row, (count, count)), 0.0), axis=1, keepdims=True)


def spot(width):
    at = (lax.axis_index("dp") * lax.axis_size("mp") + lax.axis_index("mp")) * width
    return (iota((width, WIDTH), 1) == iota((width, WIDTH), 0) + at).astype(bf16)


def packing(r, c):
    return 128 // c if c < 128 and (r * c // 128) % 16 == 0 else 1


def step_kernel(
    lay, gathers, scatter_items, total_tokens,
    tokens_ref, cotangent_ref, segment_ref, gains_in, mixer_hbm, feed_hbm, sorter_hbm,
    out_hbm, grad_hbm, *refs,
):
    sums_hbm, scratch = refs[:4], list(refs[4:])

    def pop(count):
        taken = scratch[:count]
        del scratch[:count]
        return taken

    shards, weights_full, grads_full = pop(5), pop(5), pop(5)
    kv_ref, sorter_full, woq_ref, feed_a_ref, feed_b_ref = weights_full
    dfeed_a_ref, dfeed_b_ref, dwoq_ref, dkv_ref, dsorter_full = grads_full
    x_ref, cot_ref, out_ref, grad_ref = pop(4)
    (
        sorter_ref, first_ref, q_ref, k_ref, v_ref, sk_ref, sv_ref, place_k_ref, place_v_ref,
        att_ref, mixed_ref, means_ref, sink_ref, logs_ref, segrow_ref, spread_ref, gain_grad_ref,
        second_ref, act_ref, pre_ref, total_ref, second_grad_ref,
    ) = pop(22)
    dk_ref, dv_ref = total_ref, second_grad_ref
    near_a, far_a, near_b, far_b, send_sems, recv_sems, copy_sems = pop(7)
    sems = Sems(send_sems, recv_sems)
    fetch_x = pltpu.make_async_copy(tokens_ref, x_ref, copy_sems.at[0])
    fetch_cot = pltpu.make_async_copy(cotangent_ref, cot_ref, copy_sems.at[1])
    mixer_in, feed_in, sorter_in = pop(3)
    fetches = [
        pltpu.make_async_copy(source, target, copy_sems.at[5 + k])
        for k, (source, target) in enumerate(
            ((mixer_hbm, mixer_in), (sorter_hbm, sorter_in), (feed_hbm, feed_in))
        )
    ]
    begin(fetches)
    fetch_x.start()
    fetch_cot.start()
    mp = lax.axis_index("mp")
    greet(lay)
    gather = [
        Gather(item, shard, full, sems, k < 4)
        for k, (item, shard, full) in enumerate(zip(gathers, shards, weights_full))
    ]
    early = tuple(gather[:2])
    gather_woq, gather_a, gather_b = gather[2:]
    scatters = []
    feed_sum, mixer_sum, sorter_sum, small_out = sums = pop(4)
    pack = packing(*sorter_sum.shape)

    def write_to(out, places, lane, lanes):
        def write(j, rows, value):
            place = places[j]
            if len(out.shape) == 3:
                out[rows, place, lane : lane + lanes] = value
                return
            tiles = feed_tiles if out is feed_sum else lanes // 128
            group = len(mixer_order) if out is mixer_sum else 2
            for tile in range(lanes // 128):
                start = rows.start * tiles * group + (lane // 128 + tile) * group + place
                out[pl.ds(start, rows.stop - rows.start, stride=tiles * group), :] = value[:, tile * 128 : (tile + 1) * 128]

        return write

    def write_sorter(j, rows, value):
        deep, c = sorter_sum.shape[0] // pack, sorter_sum.shape[1]
        for k in range(pack):
            sorter_sum[k * deep + rows.start : k * deep + rows.stop, :] = value[:, k * c : (k + 1) * c]

    mixer_order = (3, 0, 1, 2)
    half_width = scatter_items[0].c
    feed_tiles = 2 * half_width // 128
    writers = (
        write_to(feed_sum, (0, 1), 0, half_width),
        write_to(feed_sum, (0, 1), half_width, half_width),
        write_to(mixer_sum, mixer_order[:2], 0, scatter_items[2].c),
        write_to(mixer_sum, mixer_order[2:], 0, scatter_items[2].c),
        write_sorter,
    )
    for item, full, write in zip(scatter_items, grads_full, writers):
        scatters.append(Scatter(item, full, pop(7), write, sems))
    write_sums = [
        pltpu.make_async_copy(buffer, target, copy_sems.at[8 + k])
        for k, (buffer, target) in enumerate(zip(sums, sums_hbm))
    ]
    scatter_a, scatter_b, scatter_woq, scatter_kv, scatter_sorter = scatters
    total_a = Total(lay, near_a, far_a, sems)
    total_b = Total(lay, near_b, far_b, sems)

    def each(group, name, *args):
        for member in group:
            getattr(member, name)(*args)

    width = gains_in.shape[1]
    lane = iota((BLOCKS, SEQ_LEN), 1)
    row = segment_ref[pl.ds(mp, 1), :].astype(f32)
    picked = jnp.where(lane // BLOCK == iota((BLOCKS, SEQ_LEN), 0), jnp.broadcast_to(row, (BLOCKS, SEQ_LEN)), 0.0)
    seg = picked[:, :PAIRS]
    for at in range(PAIRS, SEQ_LEN, PAIRS):
        seg = seg + picked[:, at : at + PAIRS]
    tiling = (iota((PAIRS, PAIRS), 0) % BLOCK == iota((PAIRS, PAIRS), 1) % BLOCK).astype(bf16)
    seg = exact_dot(seg, tiling)
    segrow_ref[...] = seg
    real_col = (seg[:, 0:1] > 0).astype(f32)
    count = jnp.broadcast_to(jnp.sum(real_col, axis=0, keepdims=True), (8, 128))
    placed = exact_dot(gains_in[...], spot(width))
    small = jnp.concatenate([spread_rows(placed[0:1]), spread_rows(placed[1:2]), count], axis=0)
    for fetch in fetches:
        fetch.wait()
    for j, source in enumerate((1, 2)):
        shards[0][j] = mixer_in[:, source, :].astype(bf16)
    deep = sorter_in.shape[0] // pack
    sorter_shard = sorter_in[...].astype(bf16)
    shards[1][0] = jnp.concatenate([sorter_shard[k * deep : (k + 1) * deep] for k in range(pack)], axis=1)
    for j, source in enumerate((3, 0)):
        shards[2][j] = mixer_in[:, source, :].astype(bf16)
    for j in range(2):
        shards[3][j] = feed_in[:, j, :half_width].astype(bf16)
        shards[4][j] = feed_in[:, j, half_width:].astype(bf16)
    each(gather, "place")
    lane_block = iota((BLOCKS, LOGITS), 1) % BLOCKS
    real_row = jnp.sum(jnp.where(iota((BLOCKS, LOGITS), 0) == lane_block, real_col, 0.0), axis=0, keepdims=True)
    allowed = permitted(real_col, real_row)
    await_all(lay)
    each(early, "stage", 0)
    total_a.over_mp(small)
    gather_woq.stage(0)
    gather_b.stage(0)
    fetch_x.wait()

    def norm_rows(tile, carry):
        rows = pl.ds(pl.multiple_of(tile * ROWS, ROWS), ROWS)
        total_ref[rows, :] = normalize(x_ref[rows, :].astype(f32))[0]
        return carry

    lax.fori_loop(0, TILES, norm_rows, 0)
    total_a.over_dp()
    each(early, "landed")
    each(early, "stage", 1)
    gather_a.stage(0)
    each(early, "landed")
    each(early, "stage", 2)
    gather_woq.landed()
    gather_woq.stage(1)
    summed = total_a.result()
    gain_first = joined_row(summed[0:4])
    gain_second = joined_row(summed[4:8])
    entropy_weight = penalty_weight * total_tokens / (summed[8:9, 0:1] * HEADS)

    def norm_first(tile, carry):
        rows = pl.ds(pl.multiple_of(tile * ROWS, ROWS), ROWS)
        first_ref[rows, :] = (total_ref[rows, :] * gain_first).astype(bf16)
        return carry

    lax.fori_loop(0, TILES, norm_first, 0)
    member = (iota((BLOCKS, SEQ_LEN), 0) == iota((BLOCKS, SEQ_LEN), 1) // BLOCK).astype(bf16)
    means = (mm(member, first_ref[...]) / BLOCK).astype(bf16)
    means_ref[...] = means
    each(early, "landed")
    each(early, "stage", 3)
    gather_woq.landed()
    gather_woq.stage(2)
    gather_a.landed()
    gather_a.stage(1)
    gather_b.landed()
    gather_b.stage(1)
    each(early, "landed")

    def weight(ref, j, cols=slice(None)):
        if len(ref.shape) == 6:
            parts = [ref[j, :, :, part].reshape(WIDTH, ref.shape[-1]) for part in range(lay.mp)]
            return jnp.concatenate(parts, axis=1)
        tile = ref[j, :, :, :, cols]
        return tile.reshape(WIDTH, tile.shape[-1])

    r, c = sorter_in.shape

    def sorter_places():
        for high in range(lay.H):
            for low in range(lay.L):
                for part in range(lay.mp):
                    base = (high * lay.L + low) * r
                    if pack == 1:
                        index = (0, high, low, part)
                    else:
                        index = (0, high, low, slice(None), slice(part * 128, (part + 1) * 128))
                    rows = [slice(base + k * deep, base + (k + 1) * deep) for k in range(pack)]
                    yield index, rows, slice(part * c, (part + 1) * c)

    for index, rows, cols in sorter_places():
        tile = sorter_full[index]
        for k in range(pack):
            sorter_ref[rows[k], cols] = tile[:, k * c : (k + 1) * c]
    logits = mm(means, sorter_ref[...])
    for tile in range(TILES):
        rows = slice(tile * ROWS, (tile + 1) * ROWS)
        k_ref[rows, :] = mm(first_ref[rows, :], weight(kv_ref, 0)).astype(bf16)
        v_ref[rows, :] = mm(first_ref[rows, :], weight(kv_ref, 1)).astype(bf16)

    place_k_ref[...] = by_place(k_ref[...])
    place_v_ref[...] = by_place(v_ref[...])

    def store(index, value):
        sink_ref[index] = value

    logs, weights = sinkhorn(logits, allowed, group_matrix(), store)
    logs_ref[...] = logs
    probs = weights.astype(bf16)
    gather_a.landed()
    gather_a.stage(2)
    gather_woq.landed()
    gather_woq.stage(3)
    first_head = iota((SPAN, 2 * PAIR), 1) % PAIR < HEAD_DIM

    def rearrange(matrices, keys, values, finish_pair):
        for pair in range(HEADS // 2):
            lanes = slice(pair * PAIR, (pair + 1) * PAIR)
            one, two = matrices(2 * pair), matrices(2 * pair + 1)
            outs = []
            for part in range(SEQ_LEN // SPAN):
                rows = slice(part * SPAN, (part + 1) * SPAN)
                both = jnp.concatenate([keys[rows, lanes], values[rows, lanes]], axis=1)
                outs.append(jnp.where(first_head, mm(one, both), mm(two, both)))
            out = jnp.concatenate(outs, axis=0)
            finish_pair(lanes, out[:, :PAIR], out[:, PAIR:])

    def forth(head):
        return repeated(probs[:, head * BLOCKS : (head + 1) * BLOCKS])

    def keep_sorted(lanes, keys, values):
        sk_ref[:, lanes] = by_place(keys.astype(bf16))
        sv_ref[:, lanes] = by_place(values.astype(bf16))

    rearrange(forth, place_k_ref, place_v_ref, keep_sorted)
    gather_woq.landed()

    def project_queries(tile, carry):
        rows = pl.ds(pl.multiple_of(tile * ROWS, ROWS), ROWS)
        q_ref[rows, :] = mm(first_ref[rows, :], weight(woq_ref, 1)).astype(bf16)
        return carry

    lax.fori_loop(0, TILES, project_queries, 0)

    def block_rows(block):
        return pl.ds(pl.multiple_of(block * BLOCK, BLOCK), BLOCK)

    def operands(block, group):
        rows = block_rows(block)
        lanes = slice(group * LANES, (group + 1) * LANES)
        keys = jnp.concatenate([k_ref[rows, lanes], sk_ref[rows, lanes]], axis=0)
        values = jnp.concatenate([v_ref[rows, lanes], sv_ref[rows, lanes]], axis=0)
        return keys, values

    def attend(step, carry):
        for block in [step * UNROLL + k for k in range(UNROLL)]:
            rows = block_rows(block)
            row = segrow_ref[pl.ds(block, 1), :]
            near = diagonal_column(row[:, :BLOCK], BLOCK) == row
            far = jnp.broadcast_to(row > 0, (BLOCK, PAIRS))
            mask = jnp.concatenate([near, far], axis=0)
            for group in range(GROUPS):
                lanes = slice(group * LANES, (group + 1) * LANES)
                keys, values = operands(block, group)
                scores = mm(keys, by_pack(q_ref[rows, lanes]), 1, 1) * (HEAD_DIM ** -0.5)
                scores = jnp.where(mask, scores, excluded_fill)
                shifted = jnp.exp(scores - jnp.max(scores, axis=0, keepdims=True))
                attention = shifted * (1.0 / jnp.sum(shifted, axis=0, keepdims=True))
                att_ref[block, group] = attention
                mixed_ref[rows, lanes] = own_heads(mm(attention.astype(bf16), values, 0, 0)).astype(bf16)
        return carry

    steps = BLOCKS // UNROLL
    lax.fori_loop(0, steps, attend, 0)
    gather_a.landed()
    gather_a.stage(3)
    gather_b.landed()
    gather_b.stage(2)
    fetch_cot.wait()
    gain_grad_ref[...] = jnp.zeros_like(gain_grad_ref)

    def keep(ref, j, cols, value):
        if len(ref.shape) == 6:
            for part in range(lay.mp):
                piece = value[:, part * ref.shape[-1] : (part + 1) * ref.shape[-1]]
                ref[j, :, :, part] = piece.astype(bf16).reshape(lay.H, lay.L, WIDTH // lay.dp, ref.shape[-1])
            return
        ref[j, :, :, :, cols] = value.astype(bf16).reshape(lay.H, lay.L, WIDTH // lay.dp, value.shape[1])

    def open_rows(tile, carry):
        rows = pl.ds(pl.multiple_of(tile * ROWS, ROWS), ROWS)
        middle = x_ref[rows, :].astype(f32) + mm(mixed_ref[rows, :], weight(woq_ref, 0), 1, 1)
        grad_ref[rows, :] = middle
        normed, _ = normalize(middle)
        second_ref[rows, :] = (normed * gain_second).astype(bf16)
        return carry

    def feed_rows(feed_ref, rows, total, second_grad):
        second, cot = second_ref[rows, :], cot_ref[rows, :]
        for part in range(feed_ref.shape[-1] // WIDTH):
            cols = slice(part * WIDTH, (part + 1) * WIDTH)
            up, down = weight(feed_ref, 0, cols), weight(feed_ref, 1, cols)
            pre = mm(second, up)
            act = jnp.maximum(pre, 0.0).astype(bf16)
            act_ref[rows, cols] = act
            total = total + mm(act, down, 1, 1)
            pre_grad = jnp.where(pre > 0, mm(cot, down), 0.0).astype(bf16)
            pre_ref[rows, cols] = pre_grad
            partial = mm(pre_grad, up, 1, 1)
            second_grad = partial if second_grad is None else second_grad + partial
        return total, second_grad

    def feed_a(tile, carry):
        rows = pl.ds(pl.multiple_of(tile * ROWS, ROWS), ROWS)
        total, second_grad = feed_rows(feed_a_ref, rows, grad_ref[rows, :], None)
        total_ref[rows, :] = total
        second_grad_ref[rows, :] = second_grad
        return carry

    def feed_b(tile, carry):
        rows = pl.ds(pl.multiple_of(tile * ROWS, ROWS), ROWS)
        total, second_grad = feed_rows(feed_b_ref, rows, total_ref[rows, :], second_grad_ref[rows, :])
        out_ref[rows, :] = total.astype(bf16)
        normed, inverse = normalize(grad_ref[rows, :])
        grad_ref[rows, :] = cot_ref[rows, :].astype(f32) + norm_back(second_grad, normed, inverse, gain_second)
        gain_grad_ref[8:16, :] += jnp.sum((second_grad * normed).reshape(ROWS // 8, 8, WIDTH), axis=0)
        return carry

    def feed_weights(dfeed_ref):
        keep(dfeed_ref, 0, slice(None), mm(second_ref[...], pre_ref[...], 0, 0))
        keep(dfeed_ref, 1, slice(None), mm(cot_ref[...], act_ref[...], 0, 0))

    lax.fori_loop(0, TILES, open_rows, 0)
    gather_a.landed()
    lax.fori_loop(0, TILES, feed_a, 0)
    gather_b.landed()
    gather_b.stage(3)
    feed_weights(dfeed_a_ref)
    scatter_a.stage(0)
    gather_b.landed()
    lax.fori_loop(0, TILES // 2, feed_b, 0)
    scatter_a.fold(0)
    scatter_a.stage(1)
    lax.fori_loop(TILES // 2, TILES, feed_b, 0)
    write_out = pltpu.make_async_copy(out_ref, out_hbm, copy_sems.at[2])
    write_out.start()
    feed_weights(dfeed_b_ref)
    scatter_b.stage(0)
    keep(dwoq_ref, 0, slice(None), mm(grad_ref[...].astype(bf16), mixed_ref[...], 0, 0))

    def start(tile, carry):
        rows = pl.ds(pl.multiple_of(tile * ROWS, ROWS), ROWS)
        mixed_ref[rows, :] = mm(grad_ref[rows, :].astype(bf16), weight(woq_ref, 0)).astype(bf16)
        return carry

    lax.fori_loop(0, TILES, start, 0)
    scatter_a.fold(1)
    scatter_a.stage(2)
    scatter_b.fold(0)
    scatter_b.stage(1)

    def attend_back(step, carry):
        units = [(step * UNROLL + k, group) for k in range(UNROLL) for group in range(GROUPS)]

        def mixed_pack(block, group):
            return by_pack(mixed_ref[block_rows(block), group * LANES : (group + 1) * LANES])

        for block, group in units:
            rows, at = block_rows(block), group * LANES
            keys, values = operands(block, group)
            attention = att_ref[block, group]
            prob_grad = mm(values, mixed_pack(block, group), 1, 1)
            inner = jnp.sum(attention * prob_grad, axis=0, keepdims=True)
            score_grad = (attention * (prob_grad - inner) * (HEAD_DIM ** -0.5)).astype(bf16)
            pre_ref[rows, WIDTH + at : WIDTH + at + PAIRS] = score_grad[:BLOCK]
            pre_ref[rows, WIDTH + at + PAIRS : WIDTH + at + 2 * PAIRS] = score_grad[BLOCK:]
            pre_ref[rows, at : at + LANES] = own_heads(mm(score_grad, keys, 0, 0)).astype(bf16)
        for block, group in units:
            rows, at = block_rows(block), group * LANES
            lanes = slice(at, at + LANES)
            score_grad = jnp.concatenate(
                [pre_ref[rows, WIDTH + at : WIDTH + at + PAIRS], pre_ref[rows, WIDTH + at + PAIRS : WIDTH + at + 2 * PAIRS]],
                axis=0,
            )
            key_grad = mm(score_grad, by_pack(q_ref[rows, lanes]))
            value_grad = mm(att_ref[block, group].astype(bf16), mixed_pack(block, group))
            dk_ref[rows, lanes] = key_grad[:BLOCK]
            dv_ref[rows, lanes] = value_grad[:BLOCK]
            act_ref[rows, lanes] = key_grad[BLOCK:].astype(bf16)
            act_ref[rows, WIDTH + at : WIDTH + at + LANES] = value_grad[BLOCK:].astype(bf16)
        return carry

    lax.fori_loop(0, steps, attend_back, 0)
    scatter_a.fold(2)
    scatter_a.stage(3)
    first = first_ref[...]
    q_ref[...] = pre_ref[:, :WIDTH]
    keep(dwoq_ref, 1, slice(None), mm(first, q_ref[...], 0, 0))
    scatter_woq.stage(0)
    weights = sink_ref[2 * SINK_ITERS - 1]
    same_head = iota((LOGITS, LOGITS), 0) // BLOCKS == iota((LOGITS, LOGITS), 1) // BLOCKS
    turned = jnp.where(same_head, jnp.concatenate([weights] * HEADS, axis=0), 0.0).T

    def back(head):
        rows = slice(head * BLOCKS, (head + 1) * BLOCKS)
        return repeated(turned[rows, rows].astype(bf16))

    sk_ref[...] = by_place(act_ref[:, :WIDTH])
    sv_ref[...] = by_place(act_ref[:, WIDTH:])

    def add_pair(lanes, keys, values):
        k_ref[:, lanes] = (dk_ref[:, lanes] + by_place(keys)).astype(bf16)
        v_ref[:, lanes] = (dv_ref[:, lanes] + by_place(values)).astype(bf16)

    rearrange(back, sk_ref, sv_ref, add_pair)
    scatter_b.fold(1)
    scatter_b.stage(2)
    scatter_woq.fold(0)
    scatter_woq.stage(1)
    dkv = mm(first, jnp.concatenate([k_ref[...], v_ref[...]], axis=1), 0, 0)
    keep(dkv_ref, 0, slice(None), dkv[:, :WIDTH])
    keep(dkv_ref, 1, slice(None), dkv[:, WIDTH:])
    scatter_kv.stage(0)
    lane_head = iota((SPAN, PAIR), 1) // HEAD_DIM
    diagonal = iota((SPAN, SPAN), 0) // BLOCKS == iota((SPAN, SPAN), 1) // BLOCKS
    folded = []
    for pair in range(HEADS // 2):
        lanes = slice(pair * PAIR, (pair + 1) * PAIR)
        parts = [slice(part * SPAN, (part + 1) * SPAN) for part in range(SEQ_LEN // SPAN)]
        right = [ref[rows, lanes] for rows in parts for ref in (place_k_ref, place_v_ref)]
        left = [ref[rows, lanes] for rows in parts for ref in (sk_ref, sv_ref)]
        for head in range(2):
            mine = [jnp.where(lane_head == head, tile, jnp.zeros_like(tile)) for tile in left]
            square = mm(jnp.concatenate(mine, axis=1), jnp.concatenate(right, axis=1), 1, 1)
            square = jnp.where(diagonal, square, 0.0)
            total = square[:BLOCKS]
            for place in range(1, STACK):
                total = total + square[place * BLOCKS : (place + 1) * BLOCKS]
            folded.append(total)
    copies = (iota((BLOCKS, LOGITS), 0) == iota((BLOCKS, LOGITS), 1) % BLOCKS).astype(bf16)
    stacked = exact_dot(jnp.concatenate(folded, axis=0), copies.T)
    wide = jnp.where(same_head, exact_dot(stacked, copies), 0.0)
    probs_grad = wide[:BLOCKS]
    for head in range(1, HEADS):
        probs_grad = probs_grad + wide[head * BLOCKS : (head + 1) * BLOCKS]
    logs = logs_ref[...]
    pull = jnp.where(real_col > 0, entropy_weight * (logs + 1.0), 0.0)
    scatter_kv.fold(0)
    scatter_kv.stage(1)
    grad = sinkhorn_back(weights * (probs_grad - pull), group_matrix(), lambda index: sink_ref[index])
    logit_grad = jnp.where(allowed, grad / softness_factor, 0.0).astype(bf16)
    sorter_grad = mm(means_ref[...], logit_grad, 0, 0).astype(bf16)
    for index, rows, cols in sorter_places():
        pieces = [sorter_grad[rows[k], cols] for k in range(pack)]
        dsorter_full[index] = jnp.concatenate(pieces, axis=1) if pack > 1 else pieces[0]
    scatter_sorter.stage(0)
    scatter_b.fold(2)
    scatter_b.stage(3)
    spread_ref[...] = mm(logit_grad, sorter_ref[...], 1, 1) / BLOCK
    here = ROWS // BLOCK

    def finish(tile, carry):
        rows = pl.ds(pl.multiple_of(tile * ROWS, ROWS), ROWS)
        spread = spread_ref[pl.ds(pl.multiple_of(tile * here, here), here), :]
        spread = jnp.broadcast_to(spread[:, None, :], (here, BLOCK, WIDTH)).reshape(ROWS, WIDTH)
        first_grad = (
            mm(q_ref[rows, :], weight(woq_ref, 1), 1, 1)
            + mm(k_ref[rows, :], weight(kv_ref, 0), 1, 1)
            + mm(v_ref[rows, :], weight(kv_ref, 1), 1, 1)
            + spread
        )
        normed, inverse = normalize(x_ref[rows, :].astype(f32))
        grad_ref[rows, :] += norm_back(first_grad, normed, inverse, gain_first)
        gain_grad_ref[0:8, :] += jnp.sum((first_grad * normed).reshape(ROWS // 8, 8, WIDTH), axis=0)
        return carry

    writes = []

    def write_rows(part):
        rows = slice(part * SEQ_LEN // 2, (part + 1) * SEQ_LEN // 2)
        copy = pltpu.make_async_copy(grad_ref.at[rows], grad_hbm.at[rows], copy_sems.at[3 + part])
        copy.start()
        writes.append(copy)

    lax.fori_loop(0, TILES // 2, finish, 0)
    write_rows(0)
    scatter_woq.fold(1)
    scatter_woq.stage(2)
    scatter_sorter.fold(0)
    scatter_sorter.stage(1)
    lax.fori_loop(TILES // 2, TILES, finish, 0)
    write_rows(1)
    entropy = -jnp.sum(jnp.where(real_col > 0, weights * logs, 0.0), axis=0, keepdims=True)
    entropy = jnp.broadcast_to(entropy[:, :128] + entropy[:, 128:], (8, 128))
    total_b.over_mp(jnp.concatenate([
        spread_rows(jnp.sum(gain_grad_ref[0:8, :], axis=0, keepdims=True)),
        spread_rows(jnp.sum(gain_grad_ref[8:16, :], axis=0, keepdims=True)),
        entropy,
    ], axis=0))
    scatter_kv.fold(1)
    scatter_kv.stage(2)
    scatter_woq.fold(2)
    scatter_woq.stage(3)
    scatter_sorter.fold(1)
    scatter_sorter.stage(2)
    total_b.over_dp()
    scatter_kv.fold(2)
    scatter_kv.stage(3)
    scatter_sorter.fold(2)
    scatter_sorter.stage(3)
    scatter_a.fold(3)
    scatter_b.fold(3)
    write_sums[0].start()
    small_out[0:16, :] = total_b.result()
    small_out[16:24, :] = summed[8:16]
    write_sums[3].start()
    scatter_woq.fold(3)
    write_out.wait()
    for copy in writes:
        copy.wait()
    each(tuple(gather) + (scatter_a, scatter_b, total_a, total_b), "close")
    scatter_kv.fold(3)
    write_sums[1].start()
    scatter_sorter.fold(3)
    write_sums[2].start()
    each((scatter_woq, scatter_kv, scatter_sorter), "close")
    for copy in write_sums:
        copy.wait()


def update_kernel(lay, step_ref, *refs):
    sources, targets, penalty_out, inputs, results = refs[:18], refs[18:32], refs[32], refs[33:51], refs[51:63]
    in_sems, out_sems, row_sems = refs[63:]
    bring = [pltpu.make_async_copy(source, inputs[k], in_sems.at[k]) for k, source in enumerate(sources) if k > 1]
    send = [
        pltpu.make_async_copy(buffer, targets[2 + k], out_sems.at[2 + k]) for k, buffer in enumerate(results)
    ]
    bring_rows, send_rows = [], []
    for part in range(ROW_PARTS):
        for which in range(2):
            rows = slice(part * SEQ_LEN // ROW_PARTS, (part + 1) * SEQ_LEN // ROW_PARTS)
            sem = row_sems.at[part, which]
            bring_rows.append(pltpu.make_async_copy(sources[which].at[rows], inputs[which].at[rows], sem.at[0]))
            send_rows.append(pltpu.make_async_copy(inputs[which].at[rows], targets[which].at[rows], sem.at[1]))
    begin(bring_rows[:2] + bring + bring_rows[2:])
    feed_sum, mixer_sum, sorter_sum, sums = inputs[2:6]
    masters = inputs[6:]
    step_value = jnp.full((1, 128), step_ref[0], jnp.int32).astype(f32)
    scale_first = 1.0 / (1.0 - jnp.exp(step_value * math.log(beta_first)))[:, 0:1]
    scale_second = 1.0 / (1.0 - jnp.exp(step_value * math.log(beta_second)))[:, 0:1]

    def adamw(which, grad, rate):
        master, moment, second = [ref[...] for ref in masters[3 * which : 3 * which + 3]]
        moment_new = beta_first * moment + (1.0 - beta_first) * grad
        second_new = beta_second * second + (1.0 - beta_second) * grad * grad
        change = (moment_new * scale_first) / (jnp.sqrt(second_new * scale_second) + adam_eps)
        outs = results[3 * which : 3 * which + 3]
        outs[0][...] = moment_new
        outs[1][...] = second_new
        outs[2][...] = master - rate * (change + weight_decay * master)
        begin(send[3 * which : 3 * which + 3])

    for copy, onward in zip(bring_rows[:2], send_rows[:2]):
        copy.wait()
        onward.start()
    for copy in bring:
        copy.wait()
    adamw(1, feed_sum[...], rate_feed)
    adamw(0, mixer_sum[...], rate_mixer)
    adamw(2, sorter_sum[...], rate_sorter)
    for copy, onward in zip(bring_rows[2:], send_rows[2:]):
        copy.wait()
        onward.start()
    rows = jnp.concatenate([joined_row(sums[0:4, :]), joined_row(sums[4:8, :])], axis=0)
    own = spot(masters[9].shape[1])
    adamw(3, sum(mm(part, own, 1, 1) for part in three_parts(rows)), rate_gains)
    entropy = jnp.sum(sums[8:9, :], axis=1, keepdims=True)
    penalty_out[...] = jnp.broadcast_to(entropy / (sums[16:17, 0:1] * HEADS), (1, 128))
    for copy in send + send_rows:
        copy.wait()


def flat_rows(array):
    if array.ndim != 3 or array.shape[2] % 128:
        return array
    rows, parts, width = array.shape
    return array.reshape(rows, parts, width // 128, 128).transpose(0, 2, 1, 3).reshape(-1, 128)


def unflat_rows(flat, like):
    if flat.shape == like.shape:
        return flat
    rows, parts, width = like.shape
    return flat.reshape(rows, width // 128, parts, 128).transpose(0, 2, 1, 3).reshape(like.shape)


def shape(dims, dtype):
    return jax.ShapeDtypeStruct(dims, dtype)


LIMIT = 65400 * 1024
TOK = (SEQ_LEN, WIDTH)


def run_step(lay, total_tokens, tokens, cotangent, segment_ids, gains, mixer, feed, sorter):
    r, c, half = mixer.shape[0], mixer.shape[2], feed.shape[2] // 2
    pack = packing(*sorter.shape)
    sorter_item = Item(lay, 1, sorter.shape[0] // pack, sorter.shape[1] * pack)
    feed_item, pair_item = Item(lay, 2, r, half), Item(lay, 2, r, c)
    gathers = (pair_item, sorter_item, pair_item, feed_item, feed_item)
    scatters = (feed_item, feed_item, pair_item, pair_item, sorter_item)
    sums = [shape(jax.eval_shape(flat_rows, array).shape, f32) for array in (feed, mixer, sorter)]
    sums.append(shape((24, 128), f32))
    vm = pltpu.VMEM
    recvs = 5 * (Gather.count(lay) + Scatter.count(lay)) + 2 * Total.count(lay)
    sends = 5 * (Gather.sends(lay) + Scatter.sends(lay)) + 2 * Total.sends(lay)
    scratch = (
        [vm(item.shard(), bf16) for item in gathers]
        + [vm(item.full(), bf16) for item in gathers + scatters]
        + [vm(TOK, bf16), vm(TOK, bf16), vm(TOK, bf16), vm(TOK, f32)]
        + [vm((WIDTH, LOGITS), bf16)]
        + [vm(TOK, bf16)] * 8
        + [
            vm((BLOCKS, GROUPS, 2 * BLOCK, PAIRS), f32), vm(TOK, bf16), vm((BLOCKS, WIDTH), bf16),
            vm((2 * SINK_ITERS, BLOCKS, LOGITS), f32), vm((BLOCKS, LOGITS), f32),
            vm((BLOCKS, PAIRS), f32), vm((BLOCKS, WIDTH), f32), vm((16, WIDTH), f32),
            vm(TOK, bf16), vm((SEQ_LEN, HIDDEN // 2), bf16), vm((SEQ_LEN, HIDDEN // 2), bf16),
        ]
        + [vm(TOK, f32)] * 2
        + [vm((lay.mp, 16, 128), f32), vm((lay.dp, 16, 128), f32)] * 2
        + [pltpu.SemaphoreType.DMA((sends,)), pltpu.SemaphoreType.DMA((recvs,))]
        + [pltpu.SemaphoreType.DMA((14,))]
        + [vm(mixer.shape, f32), vm(feed.shape, f32), vm(sorter.shape, f32)]
        + [vm(total.shape, f32) for total in sums]
    )
    for item in scatters:
        scratch += Scatter.buffers(item)
    inside = pl.BlockSpec(memory_space=pltpu.VMEM)
    outside = pl.BlockSpec(memory_space=pl.ANY)
    return pl.pallas_call(
        functools.partial(step_kernel, lay, gathers, scatters, total_tokens),
        out_shape=[shape(TOK, bf16), shape(TOK, f32)]
        + sums,
        in_specs=[outside] * 2 + [inside] * 2 + [outside] * 3,
        out_specs=[outside] * 6,
        scratch_shapes=scratch,
        compiler_params=pltpu.CompilerParams(collective_id=0, has_side_effects=True, vmem_limit_bytes=LIMIT),
        name="step",
    )(tokens, cotangent, segment_ids, gains, mixer, feed, sorter)


def run_update(lay, step_count, block_output, token_grad, sums, states):
    outside = pl.BlockSpec(memory_space=pl.ANY)
    arrays = (block_output, token_grad, *sums, *states)
    moved = [shape(array.shape, array.dtype) for array in (block_output, token_grad, *states)]
    *moved, penalty = pl.pallas_call(
        functools.partial(update_kernel, lay),
        out_shape=moved + [shape((1, 128), f32)],
        in_specs=[pl.BlockSpec(memory_space=pltpu.SMEM)] + [outside] * len(arrays),
        out_specs=[outside] * len(moved) + [pl.BlockSpec(memory_space=pltpu.VMEM)],
        scratch_shapes=[pltpu.VMEM(array.shape, array.dtype) for array in arrays]
        + [pltpu.VMEM(state.shape, f32) for state in states]
        + [pltpu.SemaphoreType.DMA((len(arrays),)), pltpu.SemaphoreType.DMA((len(moved),))]
        + [pltpu.SemaphoreType.DMA((ROW_PARTS, 2, 2))],
        compiler_params=pltpu.CompilerParams(vmem_limit_bytes=LIMIT),
        name="update",
    )(step_count, *arrays)
    return moved[0], moved[1], penalty, moved[2:]


rate_mixer = 0.2
rate_feed = 0.1
rate_sorter = 0.6
rate_gains = 1.0
beta_first = 0.9
beta_second = 0.95
adam_eps = 1e-08
weight_decay = 0.1


def local(
    lay,
    tokens,
    segment_ids,
    cotangent,
    step_count,
    mixer_weights,
    mixer_moment,
    mixer_second,
    feed_weights,
    feed_moment,
    feed_second,
    sorter_weights,
    sorter_moment,
    sorter_second,
    norm_gains,
    gain_moment,
    gain_second,
):
    total_tokens = float(lay.dp * segment_ids.shape[0] * SEQ_LEN)
    block_output, token_grad, *sums = run_step(
        lay, total_tokens, tokens, cotangent, segment_ids, norm_gains, mixer_weights, feed_weights, sorter_weights
    )
    states = (
        mixer_weights, mixer_moment, mixer_second, feed_weights, feed_moment, feed_second,
        sorter_weights, sorter_moment, sorter_second, norm_gains, gain_moment, gain_second,
    )
    flat = [flat_rows(state) for state in states]
    block_output, token_grad, penalty, flat = run_update(lay, step_count, block_output, token_grad, sums, flat)
    states = [unflat_rows(new, state) for new, state in zip(flat, states)]
    return (block_output, token_grad, penalty[0, :1], *states)


def solution(mesh):
    return jax.shard_map(
        functools.partial(local, Layout(mesh.shape["dp"], mesh.shape["mp"])),
        mesh=mesh,
        in_specs=(
            P(("dp", "mp"), None),
            P("dp", None),
            P(("dp", "mp"), None),
            P(),
            P("dp", None, "mp"),
            P("dp", None, "mp"),
            P("dp", None, "mp"),
            P("dp", None, "mp"),
            P("dp", None, "mp"),
            P("dp", None, "mp"),
            P("dp", "mp"),
            P("dp", "mp"),
            P("dp", "mp"),
            P(None, ("dp", "mp")),
            P(None, ("dp", "mp")),
            P(None, ("dp", "mp")),
        ),
        out_specs=(
            P(("dp", "mp"), None),
            P(("dp", "mp"), None),
            P(),
            P("dp", None, "mp"),
            P("dp", None, "mp"),
            P("dp", None, "mp"),
            P("dp", None, "mp"),
            P("dp", None, "mp"),
            P("dp", None, "mp"),
            P("dp", "mp"),
            P("dp", "mp"),
            P("dp", "mp"),
            P(None, ("dp", "mp")),
            P(None, ("dp", "mp")),
            P(None, ("dp", "mp")),
        ),
        check_vma=False,
    )
```

```python
import functools
import math
import jax
import jax.numpy as jnp
from jax import lax
from jax.sharding import PartitionSpec as P
from jax.experimental import pallas as pl
from jax.experimental.pallas import tpu as pltpu

WIDTH = 512
HEADS = 8
HEAD_DIM = 64
HIDDEN = 2048
BLOCK = 32
SINK_ITERS = 8
SEQ_LEN = 1024
BLOCKS = 32
LOGITS = HEADS * BLOCKS
ROWS = 512
TILES = SEQ_LEN // ROWS
PACK = 4
GROUPS = HEADS // PACK
LANES = PACK * HEAD_DIM
PAIRS = PACK * BLOCK
PAIR = 2 * HEAD_DIM
UNROLL = 32
ROW_PARTS = 2

norm_eps = 1e-05
softness_factor = 0.75
excluded_fill = -1000000000.0
penalty_weight = 0.1
bf16 = jnp.bfloat16
f32 = jnp.float32


def mm(a, b, ca=1, cb=0):
    return lax.dot_general(a, b, (((ca,), (cb,)), ((), ())), preferred_element_type=f32)


def iota(shape, dim):
    return lax.broadcasted_iota(jnp.int32, shape, dim)


def normalize(rows):
    centred = rows - jnp.mean(rows, axis=-1, keepdims=True)
    inverse = lax.rsqrt(jnp.mean(centred * centred, axis=-1, keepdims=True) + norm_eps)
    return centred * inverse, inverse


def norm_back(grad_out, normed, inverse, gain):
    scaled = grad_out * gain
    return inverse * (
        scaled
        - jnp.mean(scaled, axis=-1, keepdims=True)
        - normed * jnp.mean(scaled * normed, axis=-1, keepdims=True)
    )


def three_parts(value):
    high = value.astype(bf16)
    rest = value - high.astype(f32)
    mid = rest.astype(bf16)
    low = (rest - mid.astype(f32)).astype(bf16)
    return high, mid, low


def group_matrix():
    return (iota((LOGITS, LOGITS), 0) // BLOCKS == iota((LOGITS, LOGITS), 1) // BLOCKS).astype(bf16)


def exact_dot(value, matrix):
    rows = value.shape[0]
    out = mm(jnp.concatenate(three_parts(value), axis=0), matrix)
    return out[:rows] + out[rows : 2 * rows] + out[2 * rows :]


def head_max(value):
    lane_head = iota(value.shape, 1) // BLOCKS
    out = jnp.zeros_like(value)
    for head in range(HEADS):
        here = lane_head == head
        top = jnp.max(jnp.where(here, value, -jnp.inf), axis=1, keepdims=True)
        out = jnp.where(here, top, out)
    return out


def permitted(real_col, real_row):
    col = iota((BLOCKS, LOGITS), 1) % BLOCKS
    return ((real_col * real_row) > 0) | (iota((BLOCKS, LOGITS), 0) == col)


def sinkhorn(logits, allowed, groups, store):
    logs = jnp.where(allowed, logits / softness_factor, excluded_fill)
    top = head_max(logs)
    logs = logs - (top + jnp.log(exact_dot(jnp.exp(logs - top), groups)))
    store(0, jnp.exp(logs))
    top = jnp.max(logs, axis=0, keepdims=True)
    logs = logs - (top + jnp.log(jnp.sum(jnp.exp(logs - top), axis=0, keepdims=True)))
    weights = jnp.exp(logs)
    store(1, weights)
    for sweep in range(1, SINK_ITERS):
        logs = logs - jnp.log(exact_dot(weights, groups))
        weights = jnp.exp(logs)
        store(2 * sweep, weights)
        logs = logs - jnp.log(jnp.sum(weights, axis=0, keepdims=True))
        weights = jnp.exp(logs)
        store(2 * sweep + 1, weights)
    return logs, weights


def sinkhorn_back(grad, groups, load):
    for sweep in reversed(range(SINK_ITERS)):
        grad = grad - load(2 * sweep + 1) * jnp.sum(grad, axis=0, keepdims=True)
        grad = grad - load(2 * sweep) * exact_dot(grad, groups)
    return grad


def by_pack(tile):
    rows = jnp.concatenate([tile] * PACK, axis=0)
    keep = iota((PAIRS, LANES), 0) // BLOCK == iota((PAIRS, LANES), 1) // HEAD_DIM
    return jnp.where(keep, rows, jnp.zeros_like(rows))


def own_heads(product):
    lane_head = iota((BLOCK, LANES), 1) // HEAD_DIM
    out = product[:BLOCK]
    for head in range(1, PACK):
        out = jnp.where(lane_head == head, product[head * BLOCK : (head + 1) * BLOCK], out)
    return out


STACK = 8
SPAN = STACK * BLOCKS


def by_place(rows):
    lanes = rows.shape[1]
    return jnp.swapaxes(rows.reshape(BLOCKS, BLOCK, lanes), 0, 1).reshape(SEQ_LEN, lanes)


def repeated(matrix):
    wide = jnp.concatenate([matrix] * STACK, axis=1)
    wide = jnp.concatenate([wide] * STACK, axis=0)
    keep = iota((SPAN, SPAN), 0) // BLOCKS == iota((SPAN, SPAN), 1) // BLOCKS
    return jnp.where(keep, wide, jnp.zeros_like(wide))


MESH = pl.DeviceIdType.MESH


class Layout:
    def __init__(self, mesh_dp, mesh_mp):
        self.dp, self.mp = mesh_dp, mesh_mp
        self.C = 2 if mesh_mp % 2 == 0 else 1
        self.X = mesh_mp // self.C
        self.L = 2 if mesh_dp % 2 == 0 else 1
        self.H = mesh_dp // self.L

    def here(self):
        dp, mp = lax.axis_index("dp"), lax.axis_index("mp")
        return dp // self.L, dp % self.L, mp // self.C, mp % self.C


class Item:
    def __init__(self, lay, J, r, c):
        self.lay, self.J, self.r, self.c = lay, J, r, c
        self.direct = c % 128 == 0
        self.half = r // 2

    def shard(self):
        return (self.J, self.r, self.c)

    def dims(self, *lead, rows=None, wide=None):
        rows = self.r if rows is None else rows
        wide = self.lay.mp if wide is None else wide
        if self.direct:
            return (self.J, *lead, rows, wide * self.c)
        return (self.J, *lead, wide, rows, self.c)

    def full(self):
        return self.dims(self.lay.H, self.lay.L)

    def at(self, lead, first, count=1, rows=slice(None)):
        if self.direct:
            start = first * self.c if isinstance(first, int) else pl.multiple_of(first * self.c, 128)
            return (slice(None), *lead, rows, pl.ds(start, count * self.c))
        return (slice(None), *lead, first if count == 1 else pl.ds(first, count), rows, slice(None))

    def rows_a(self):
        return slice(0, self.half)

    def rows_b(self):
        return slice(self.half, self.r)


ALLR = slice(None)


class Sems:
    def __init__(self, send, recv):
        self.send, self.recv = send, recv
        self.sends, self.recvs = 0, 0

    def lane(self, count):
        return Lane(self, count)


class Lane:
    def __init__(self, sems, count):
        self.sems, self.first, self.waiting = sems, sems.sends, []
        sems.sends += count

    def send(self, copies):
        self.close()
        for k, (src, dst, device) in enumerate(copies):
            self.waiting.append(
                pltpu.make_async_remote_copy(
                    src_ref=src,
                    dst_ref=dst,
                    send_sem=self.sems.send.at[self.first + k],
                    recv_sem=self.sems.recv.at[self.sems.recvs + k],
                    device_id=device,
                    device_id_type=MESH,
                )
            )
        self.sems.recvs += len(copies)
        return begin(list(self.waiting))

    def close(self):
        for copy in self.waiting:
            copy.wait_send()
        self.waiting = []


def begin(copies):
    for copy in copies:
        copy.start()
    return copies


def arrive(copies):
    for copy in copies:
        copy.wait_recv()


class Gather:
    def __init__(self, item, shard, full, sems, high_first=True):
        self.item, self.shard, self.full, self.high_first = item, shard, full, high_first
        self.lane = sems.lane(self.sends(item.lay))

    def stage(self, number):
        item, lay, full = self.item, self.item.lay, self.full
        h, l, x, c = lay.here()
        copies = []

        def to(hh, ll, xx, cc):
            return (hh * lay.L + ll, xx * lay.C + cc)

        def same(index, device):
            copies.append((full.at[index], full.at[index], device))

        mine = c * lay.X + x
        if number == 0 and not self.high_first:
            for rows, index, devices in (
                (item.rows_a(), item.at((h, l), mine, 1, item.rows_a()), [to(h, (l + k) % lay.L, x, c) for k in range(1, lay.L)]),
                (item.rows_b(), item.at((h, l), mine, 1, item.rows_b()), [to(h, l, (x + k) % lay.X, c) for k in range(1, lay.X)]),
            ):
                copies += [(self.shard.at[:, rows], full.at[index], device) for device in devices]
        if number == 1 and not self.high_first:
            for k in range(1, lay.H):
                device = to((h + k) % lay.H, l, x, c)
                same(item.at((h, ALLR), mine, 1, item.rows_a()), device)
                same(item.at((h, l), c * lay.X, lay.X, item.rows_b()), device)
        if number == 0 and self.high_first:
            for k in range(1, lay.H):
                copies.append((self.shard, full.at[item.at((h, l), mine)], to((h + k) % lay.H, l, x, c)))
        if number == 1 and self.high_first:
            for k in range(1, lay.L):
                same(item.at((ALLR, l), mine, 1, item.rows_a()), to(h, (l + k) % lay.L, x, c))
            for k in range(1, lay.X):
                same(item.at((ALLR, l), mine, 1, item.rows_b()), to(h, l, (x + k) % lay.X, c))
        if number == 2:
            for k in range(1, lay.X):
                same(item.at((ALLR, ALLR), mine, 1, item.rows_a()), to(h, l, (x + k) % lay.X, c))
            for k in range(1, lay.L):
                same(item.at((ALLR, l), c * lay.X, lay.X, item.rows_b()), to(h, (l + k) % lay.L, x, c))
        if number == 3:
            for k in range(1, lay.C):
                same(item.at((ALLR, ALLR), c * lay.X, lay.X), to(h, l, x, (c + k) % lay.C))
        self.flying = self.lane.send(copies)

    def place(self):
        h, l, x, c = self.item.lay.here()
        self.full[self.item.at((h, l), c * self.item.lay.X + x)] = self.shard[...]

    def landed(self):
        arrive(self.flying)

    def close(self):
        self.lane.close()

    @staticmethod
    def sends(lay):
        return max(2 * (lay.H - 1), lay.L + lay.X - 2, lay.C - 1)

    @staticmethod
    def count(lay):
        return 2 * (lay.H - 1) + 2 * (lay.L + lay.X - 2) + (lay.C - 1)


class Scatter:
    def __init__(self, item, full, buffers, write, sems, high_last=True):
        self.item, self.full, self.write, self.high_last = item, full, write, high_last
        self.lane = sems.lane(self.sends(item.lay))
        self.core, self.one_a, self.one_b, self.two_a, self.two_b, self.top_a, self.top_b = buffers

    @staticmethod
    def buffers(item, high_last=True):
        lay = item.lay
        half = item.half
        if not high_last:
            return Scatter.buffers(item)[:3] + [
                pltpu.VMEM((lay.H - 1, *item.dims(lay.L, rows=half, wide=1)), bf16),
                pltpu.VMEM((lay.H - 1, *item.dims(rows=half, wide=lay.X)), bf16),
                pltpu.VMEM((lay.L - 1, *item.dims(rows=half, wide=1)), bf16),
                pltpu.VMEM((lay.X - 1, *item.dims(rows=half, wide=1)), bf16),
            ]
        return [
            pltpu.VMEM((lay.C - 1, *item.dims(lay.H, lay.L, wide=lay.X)), bf16),
            pltpu.VMEM((lay.X - 1, *item.dims(lay.H, lay.L, rows=half, wide=1)), bf16),
            pltpu.VMEM((lay.L - 1, *item.dims(lay.H, rows=half, wide=lay.X)), bf16),
            pltpu.VMEM((lay.L - 1, *item.dims(lay.H, rows=half, wide=1)), bf16),
            pltpu.VMEM((lay.X - 1, *item.dims(lay.H, rows=half, wide=1)), bf16),
            pltpu.VMEM((lay.H - 1, *item.dims(rows=half, wide=1)), bf16),
            pltpu.VMEM((lay.H - 1, *item.dims(rows=half, wide=1)), bf16),
        ]

    def stage(self, number):
        item, lay = self.item, self.item.lay
        h, l, x, c = lay.here()
        copies = []

        def to(hh, ll, xx, cc):
            return (hh * lay.L + ll, xx * lay.C + cc)

        def send(src, src_index, dst, dst_index, device):
            copies.append((src.at[src_index], dst.at[dst_index], device))

        if number == 0:
            for k in range(1, lay.C):
                cc = (c + k) % lay.C
                send(
                    self.full, item.at((ALLR, ALLR), cc * lay.X, lay.X),
                    self.core, (k - 1, *item.at((ALLR, ALLR), 0, lay.X)),
                    to(h, l, x, cc),
                )
        if number == 1:
            for k in range(1, lay.X):
                xx = (x + k) % lay.X
                send(
                    self.core, (0, *item.at((ALLR, ALLR), xx, 1, item.rows_a())),
                    self.one_a, (k - 1, *item.at((ALLR, ALLR), 0)),
                    to(h, l, xx, c),
                )
            for k in range(1, lay.L):
                ll = (l + k) % lay.L
                send(
                    self.core, (0, *item.at((ALLR, ll), 0, lay.X, item.rows_b())),
                    self.one_b, (k - 1, *item.at((ALLR,), 0, lay.X)),
                    to(h, ll, x, c),
                )
        if number == 2 and not self.high_last:
            for k in range(1, lay.H):
                hh = (h + k) % lay.H
                send(
                    self.one_a, (0, *item.at((hh, ALLR), 0)),
                    self.two_a, (k - 1, *item.at((ALLR,), 0)),
                    to(hh, l, x, c),
                )
                send(
                    self.one_b, (0, *item.at((hh,), 0, lay.X)),
                    self.two_b, (k - 1, *item.at((), 0, lay.X)),
                    to(hh, l, x, c),
                )
        if number == 3 and not self.high_last:
            for k in range(1, lay.L):
                ll = (l + k) % lay.L
                send(
                    self.two_a, (0, *item.at((ll,), 0)),
                    self.top_a, (k - 1, *item.at((), 0)),
                    to(h, ll, x, c),
                )
            for k in range(1, lay.X):
                xx = (x + k) % lay.X
                send(
                    self.two_b, (0, *item.at((), xx)),
                    self.top_b, (k - 1, *item.at((), 0)),
                    to(h, l, xx, c),
                )
        if number == 2 and self.high_last:
            for k in range(1, lay.L):
                ll = (l + k) % lay.L
                send(
                    self.one_a, (0, *item.at((ALLR, ll), 0)),
                    self.two_a, (k - 1, *item.at((ALLR,), 0)),
                    to(h, ll, x, c),
                )
            for k in range(1, lay.X):
                xx = (x + k) % lay.X
                send(
                    self.one_b, (0, *item.at((ALLR,), xx)),
                    self.two_b, (k - 1, *item.at((ALLR,), 0)),
                    to(h, l, xx, c),
                )
        if number == 3 and self.high_last:
            for k in range(1, lay.H):
                hh = (h + k) % lay.H
                for src, dst in ((self.two_a, self.top_a), (self.two_b, self.top_b)):
                    send(src, (0, *item.at((hh,), 0)), dst, (k - 1, *item.at((), 0)), to(hh, l, x, c))
        self.flying = self.lane.send(copies)

    def fold(self, number):
        item, lay = self.item, self.item.lay
        h, l, x, c = lay.here()
        arrive(self.flying)

        def over_high(body):
            def step(high, carry):
                body(high)
                return carry

            lax.fori_loop(0, lay.H, step, 0)

        def add(target, index, source, source_index, extra):
            total = source[source_index].astype(f32) + target[(0, *index)].astype(f32)
            for other in range(1, extra):
                total = total + target[(other, *index)].astype(f32)
            target[(0, *index)] = total.astype(bf16)

        if number == 0:

            def core(high):
                for low in range(lay.L):
                    add(
                        self.core, item.at((high, low), 0, lay.X),
                        self.full, item.at((high, low), c * lay.X, lay.X), lay.C - 1,
                    )

            over_high(core)
        if number == 1:

            def one(high):
                for low in range(lay.L):
                    add(
                        self.one_a, item.at((high, low), 0),
                        self.core, (0, *item.at((high, low), x, 1, item.rows_a())), lay.X - 1,
                    )
                add(
                    self.one_b, item.at((high,), 0, lay.X),
                    self.core, (0, *item.at((high, l), 0, lay.X, item.rows_b())), lay.L - 1,
                )

            over_high(one)
        if number == 2 and not self.high_last:
            add(self.two_a, item.at((ALLR,), 0), self.one_a, (0, *item.at((h, ALLR), 0)), lay.H - 1)
            add(self.two_b, item.at((), 0, lay.X), self.one_b, (0, *item.at((h,), 0, lay.X)), lay.H - 1)
        if number == 2 and self.high_last:

            def two(high):
                add(self.two_a, item.at((high,), 0), self.one_a, (0, *item.at((high, l), 0)), lay.L - 1)
                add(self.two_b, item.at((high,), 0), self.one_b, (0, *item.at((high,), x)), lay.X - 1)

            over_high(two)
        if number == 3:
            own_a, own_b = item.at((h,), 0), item.at((h,), 0)
            if not self.high_last:
                own_a, own_b = item.at((l,), 0), item.at((), x)
            for rows, mine, own, others in (
                (item.rows_a(), self.two_a, own_a, self.top_a), (item.rows_b(), self.two_b, own_b, self.top_b),
            ):
                total = mine[(0, *own)].astype(f32)
                for other in range(others.shape[0]):
                    total = total + others[(other, *item.at((), 0))].astype(f32)
                total = total.reshape(item.J, item.half, item.c)
                for j in range(item.J):
                    self.write(j, rows, total[j])

    def close(self):
        self.lane.close()

    @staticmethod
    def sends(lay):
        return max(lay.C - 1, lay.X + lay.L - 2, 2 * (lay.H - 1))

    @staticmethod
    def count(lay):
        return (lay.C - 1) + 2 * (lay.X + lay.L - 2) + 2 * (lay.H - 1)


class Total:
    def __init__(self, lay, near, far, sems):
        self.lay, self.near, self.far = lay, near, far
        self.lane = sems.lane(self.sends(lay))

    def over_mp(self, value):
        dp, mp = lax.axis_index("dp"), lax.axis_index("mp")
        self.near[mp] = value
        self.flying = self.lane.send([
            (self.near.at[mp], self.near.at[mp], (dp, (mp + k) % self.lay.mp)) for k in range(1, self.lay.mp)
        ])

    def over_dp(self):
        dp, mp = lax.axis_index("dp"), lax.axis_index("mp")
        arrive(self.flying)
        total = self.near[0]
        for other in range(1, self.lay.mp):
            total = total + self.near[other]
        self.far[dp] = total
        self.flying = self.lane.send([
            (self.far.at[dp], self.far.at[dp], ((dp + k) % self.lay.dp, mp)) for k in range(1, self.lay.dp)
        ])

    def result(self):
        arrive(self.flying)
        total = self.far[0]
        for other in range(1, self.lay.dp):
            total = total + self.far[other]
        return total

    def close(self):
        self.lane.close()

    @staticmethod
    def sends(lay):
        return max(lay.mp, lay.dp) - 1

    @staticmethod
    def count(lay):
        return lay.mp - 1 + lay.dp - 1


def greet(lay):
    barrier = pltpu.get_barrier_semaphore()
    dp, mp = lax.axis_index("dp"), lax.axis_index("mp")
    for k in range(1, lay.mp):
        pl.semaphore_signal(barrier, inc=1, device_id=(dp, (mp + k) % lay.mp), device_id_type=MESH)
    for k in range(1, lay.dp):
        pl.semaphore_signal(barrier, inc=1, device_id=((dp + k) % lay.dp, mp), device_id_type=MESH)


def await_all(lay):
    pl.semaphore_wait(pltpu.get_barrier_semaphore(), lay.mp + lay.dp - 2)


def spread_rows(row):
    return jnp.concatenate([row[:, at : at + 128] for at in range(0, row.shape[1], 128)], axis=0)


def joined_row(rows):
    return jnp.concatenate([rows[at : at + 1] for at in range(rows.shape[0])], axis=1)


def diagonal_column(row, count):
    same = iota((count, count), 0) == iota((count, count), 1)
    return jnp.sum(jnp.where(same, jnp.broadcast_to(row, (count, count)), 0.0), axis=1, keepdims=True)


def spot(width):
    at = (lax.axis_index("dp") * lax.axis_size("mp") + lax.axis_index("mp")) * width
    return (iota((width, WIDTH), 1) == iota((width, WIDTH), 0) + at).astype(bf16)


def packing(r, c):
    return 128 // c if c < 128 and (r * c // 128) % 16 == 0 else 1


def step_kernel(
    lay, gathers, scatter_items, total_tokens,
    tokens_ref, cotangent_ref, segment_ref, gains_in, mixer_hbm, feed_hbm, sorter_hbm,
    out_hbm, grad_hbm, *refs,
):
    sums_hbm, scratch = refs[:4], list(refs[4:])

    def pop(count):
        taken = scratch[:count]
        del scratch[:count]
        return taken

    shards, weights_full, grads_full = pop(5), pop(5), pop(6)
    kv_ref, sorter_full, woq_ref, feed_a_ref, feed_b_ref = weights_full
    dfeed_a_ref, dfeed_b_ref, dwo_ref, dq_ref, dkv_ref, dsorter_full = grads_full
    x_ref, cot_ref, out_ref, grad_ref = pop(4)
    (
        sorter_ref, first_ref, q_ref, k_ref, v_ref, sk_ref, sv_ref, place_k_ref, place_v_ref,
        att_ref, mixed_ref, means_ref, sink_ref, logs_ref, segrow_ref, spread_ref, gain_grad_ref,
        second_ref, act_ref, pre_ref, total_ref, second_grad_ref,
    ) = pop(22)
    dk_ref, dv_ref = total_ref, second_grad_ref
    near_a, far_a, near_b, far_b, send_sems, recv_sems, copy_sems = pop(7)
    sems = Sems(send_sems, recv_sems)
    fetch_x = pltpu.make_async_copy(tokens_ref, x_ref, copy_sems.at[0])
    fetch_cot = pltpu.make_async_copy(cotangent_ref, cot_ref, copy_sems.at[1])
    mixer_in, feed_in, sorter_in = pop(3)
    fetches = [
        pltpu.make_async_copy(source, target, copy_sems.at[5 + k])
        for k, (source, target) in enumerate(
            ((mixer_hbm, mixer_in), (sorter_hbm, sorter_in), (feed_hbm, feed_in))
        )
    ]
    begin(fetches)
    fetch_x.start()
    fetch_cot.start()
    mp = lax.axis_index("mp")
    greet(lay)
    gather = [
        Gather(item, shard, full, sems, k < 4)
        for k, (item, shard, full) in enumerate(zip(gathers, shards, weights_full))
    ]
    early = (gather[0], gather[1])
    gather_woq, gather_a, gather_b = gather[2:]
    scatters = []
    feed_sum, mixer_sum, sorter_sum, small_out = sums = pop(4)
    pack = packing(*sorter_sum.shape)

    def write_to(out, places, lane, lanes):
        def write(j, rows, value):
            place = places[j]
            if len(out.shape) == 3:
                out[rows, place, lane : lane + lanes] = value
                return
            tiles = feed_tiles if out is feed_sum else lanes // 128
            group = len(mixer_order) if out is mixer_sum else 2
            for tile in range(lanes // 128):
                start = rows.start * tiles * group + (lane // 128 + tile) * group + place
                out[pl.ds(start, rows.stop - rows.start, stride=tiles * group), :] = value[:, tile * 128 : (tile + 1) * 128]

        return write

    def write_sorter(j, rows, value):
        deep, c = sorter_sum.shape[0] // pack, sorter_sum.shape[1]
        for k in range(pack):
            sorter_sum[k * deep + rows.start : k * deep + rows.stop, :] = value[:, k * c : (k + 1) * c]

    mixer_order = (3, 0, 1, 2)
    half_width = scatter_items[0].c
    feed_tiles = 2 * half_width // 128
    writers = (
        write_to(feed_sum, (0, 1), 0, half_width),
        write_to(feed_sum, (0, 1), half_width, half_width),
        write_to(mixer_sum, mixer_order[:1], 0, scatter_items[2].c),
        write_to(mixer_sum, mixer_order[1:2], 0, scatter_items[2].c),
        write_to(mixer_sum, mixer_order[2:], 0, scatter_items[2].c),
        write_sorter,
    )
    for k, (item, full, write) in enumerate(zip(scatter_items, grads_full, writers)):
        scatters.append(Scatter(item, full, pop(7), write, sems, k > 0))
    write_sums = [
        pltpu.make_async_copy(buffer, target, copy_sems.at[8 + k])
        for k, (buffer, target) in enumerate(zip(sums, sums_hbm))
    ]
    scatter_a, scatter_b, scatter_wo, scatter_q, scatter_kv, scatter_sorter = scatters
    total_a = Total(lay, near_a, far_a, sems)
    total_b = Total(lay, near_b, far_b, sems)

    def each(group, name, *args):
        for member in group:
            getattr(member, name)(*args)

    width = gains_in.shape[1]
    lane = iota((BLOCKS, SEQ_LEN), 1)
    row = segment_ref[pl.ds(mp, 1), :].astype(f32)
    picked = jnp.where(lane // BLOCK == iota((BLOCKS, SEQ_LEN), 0), jnp.broadcast_to(row, (BLOCKS, SEQ_LEN)), 0.0)
    seg = picked[:, :PAIRS]
    for at in range(PAIRS, SEQ_LEN, PAIRS):
        seg = seg + picked[:, at : at + PAIRS]
    tiling = (iota((PAIRS, PAIRS), 0) % BLOCK == iota((PAIRS, PAIRS), 1) % BLOCK).astype(bf16)
    seg = exact_dot(seg, tiling)
    segrow_ref[...] = seg
    real_col = (seg[:, 0:1] > 0).astype(f32)
    count = jnp.broadcast_to(jnp.sum(real_col, axis=0, keepdims=True), (8, 128))
    placed = exact_dot(gains_in[...], spot(width))
    small = jnp.concatenate([spread_rows(placed[0:1]), spread_rows(placed[1:2]), count], axis=0)
    for fetch in fetches:
        fetch.wait()
    for j, source in enumerate((1, 2)):
        shards[0][j] = mixer_in[:, source, :].astype(bf16)
    deep = sorter_in.shape[0] // pack
    sorter_shard = sorter_in[...].astype(bf16)
    shards[1][0] = jnp.concatenate([sorter_shard[k * deep : (k + 1) * deep] for k in range(pack)], axis=1)
    for j, source in enumerate((3, 0)):
        shards[2][j] = mixer_in[:, source, :].astype(bf16)
    for j in range(2):
        shards[3][j] = feed_in[:, j, :half_width].astype(bf16)
        shards[4][j] = feed_in[:, j, half_width:].astype(bf16)
    each(gather, "place")
    lane_block = iota((BLOCKS, LOGITS), 1) % BLOCKS
    real_row = jnp.sum(jnp.where(iota((BLOCKS, LOGITS), 0) == lane_block, real_col, 0.0), axis=0, keepdims=True)
    allowed = permitted(real_col, real_row)
    await_all(lay)
    each(early, "stage", 0)
    total_a.over_mp(small)
    gather_woq.stage(0)
    gather_b.stage(0)
    fetch_x.wait()

    def norm_rows(tile, carry):
        rows = pl.ds(pl.multiple_of(tile * ROWS, ROWS), ROWS)
        total_ref[rows, :] = normalize(x_ref[rows, :].astype(f32))[0]
        return carry

    lax.fori_loop(0, TILES, norm_rows, 0)
    total_a.over_dp()
    each(early, "landed")
    each(early, "stage", 1)
    gather_a.stage(0)
    each(early, "landed")
    each(early, "stage", 2)
    gather_woq.landed()
    gather_woq.stage(1)
    summed = total_a.result()
    gain_first = joined_row(summed[0:4])
    gain_second = joined_row(summed[4:8])
    entropy_weight = penalty_weight * total_tokens / (summed[8:9, 0:1] * HEADS)

    def norm_first(tile, carry):
        rows = pl.ds(pl.multiple_of(tile * ROWS, ROWS), ROWS)
        first_ref[rows, :] = (total_ref[rows, :] * gain_first).astype(bf16)
        return carry

    lax.fori_loop(0, TILES, norm_first, 0)
    member = (iota((BLOCKS, SEQ_LEN), 0) == iota((BLOCKS, SEQ_LEN), 1) // BLOCK).astype(bf16)
    means = (mm(member, first_ref[...]) / BLOCK).astype(bf16)
    means_ref[...] = means
    each(early, "landed")
    each(early, "stage", 3)
    gather_woq.landed()
    gather_woq.stage(2)
    gather_a.landed()
    gather_a.stage(1)
    gather_b.landed()
    gather_b.stage(1)
    early[1].landed()

    def weight(ref, j, cols=slice(None)):
        if len(ref.shape) == 6:
            parts = [ref[j, :, :, part].reshape(WIDTH, ref.shape[-1]) for part in range(lay.mp)]
            return jnp.concatenate(parts, axis=1)
        tile = ref[j, :, :, :, cols]
        return tile.reshape(WIDTH, tile.shape[-1])

    r, c = sorter_in.shape

    def sorter_places():
        for high in range(lay.H):
            for low in range(lay.L):
                for part in range(lay.mp):
                    base = (high * lay.L + low) * r
                    if pack == 1:
                        index = (0, high, low, part)
                    else:
                        index = (0, high, low, slice(None), slice(part * 128, (part + 1) * 128))
                    rows = [slice(base + k * deep, base + (k + 1) * deep) for k in range(pack)]
                    yield index, rows, slice(part * c, (part + 1) * c)

    for index, rows, cols in sorter_places():
        tile = sorter_full[index]
        for k in range(pack):
            sorter_ref[rows[k], cols] = tile[:, k * c : (k + 1) * c]
    logits = mm(means, sorter_ref[...])
    def store(index, value):
        sink_ref[index] = value

    logs, weights = sinkhorn(logits, allowed, group_matrix(), store)
    logs_ref[...] = logs
    probs = weights.astype(bf16)
    early[0].landed()
    for tile in range(TILES):
        rows = slice(tile * ROWS, (tile + 1) * ROWS)
        k_ref[rows, :] = mm(first_ref[rows, :], weight(kv_ref, 0)).astype(bf16)
        v_ref[rows, :] = mm(first_ref[rows, :], weight(kv_ref, 1)).astype(bf16)

    place_k_ref[...] = by_place(k_ref[...])
    place_v_ref[...] = by_place(v_ref[...])
    gather_a.landed()
    gather_a.stage(2)
    gather_woq.landed()
    gather_woq.stage(3)
    first_head = iota((SPAN, 2 * PAIR), 1) % PAIR < HEAD_DIM

    def rearrange(matrices, keys, values, finish_pair):
        for pair in range(HEADS // 2):
            lanes = slice(pair * PAIR, (pair + 1) * PAIR)
            one, two = matrices(2 * pair), matrices(2 * pair + 1)
            outs = []
            for part in range(SEQ_LEN // SPAN):
                rows = slice(part * SPAN, (part + 1) * SPAN)
                both = jnp.concatenate([keys[rows, lanes], values[rows, lanes]], axis=1)
                outs.append(jnp.where(first_head, mm(one, both), mm(two, both)))
            out = jnp.concatenate(outs, axis=0)
            finish_pair(lanes, out[:, :PAIR], out[:, PAIR:])

    def forth(head):
        return repeated(probs[:, head * BLOCKS : (head + 1) * BLOCKS])

    def keep_sorted(lanes, keys, values):
        sk_ref[:, lanes] = by_place(keys.astype(bf16))
        sv_ref[:, lanes] = by_place(values.astype(bf16))

    rearrange(forth, place_k_ref, place_v_ref, keep_sorted)
    gather_woq.landed()

    def project_queries(tile, carry):
        rows = pl.ds(pl.multiple_of(tile * ROWS, ROWS), ROWS)
        q_ref[rows, :] = mm(first_ref[rows, :], weight(woq_ref, 1)).astype(bf16)
        return carry

    lax.fori_loop(0, TILES, project_queries, 0)

    def block_rows(block):
        return pl.ds(pl.multiple_of(block * BLOCK, BLOCK), BLOCK)

    def operands(block, group):
        rows = block_rows(block)
        lanes = slice(group * LANES, (group + 1) * LANES)
        keys = jnp.concatenate([k_ref[rows, lanes], sk_ref[rows, lanes]], axis=0)
        values = jnp.concatenate([v_ref[rows, lanes], sv_ref[rows, lanes]], axis=0)
        return keys, values

    def attend(step, carry):
        for block in [step * UNROLL + k for k in range(UNROLL)]:
            rows = block_rows(block)
            row = segrow_ref[pl.ds(block, 1), :]
            near = diagonal_column(row[:, :BLOCK], BLOCK) == row
            far = jnp.broadcast_to(row > 0, (BLOCK, PAIRS))
            mask = jnp.concatenate([near, far], axis=0)
            for group in range(GROUPS):
                lanes = slice(group * LANES, (group + 1) * LANES)
                keys, values = operands(block, group)
                scores = mm(keys, by_pack(q_ref[rows, lanes]), 1, 1) * (HEAD_DIM ** -0.5)
                scores = jnp.where(mask, scores, excluded_fill)
                shifted = jnp.exp(scores - jnp.max(scores, axis=0, keepdims=True))
                attention = shifted * (1.0 / jnp.sum(shifted, axis=0, keepdims=True))
                att_ref[block, group] = attention
                mixed_ref[rows, lanes] = own_heads(mm(attention.astype(bf16), values, 0, 0)).astype(bf16)
        return carry

    steps = BLOCKS // UNROLL
    lax.fori_loop(0, steps, attend, 0)
    gather_a.landed()
    gather_a.stage(3)
    gather_b.landed()
    gather_b.stage(2)
    fetch_cot.wait()
    gain_grad_ref[...] = jnp.zeros_like(gain_grad_ref)

    def keep(ref, j, cols, value):
        if len(ref.shape) == 6:
            for part in range(lay.mp):
                piece = value[:, part * ref.shape[-1] : (part + 1) * ref.shape[-1]]
                ref[j, :, :, part] = piece.astype(bf16).reshape(lay.H, lay.L, WIDTH // lay.dp, ref.shape[-1])
            return
        ref[j, :, :, :, cols] = value.astype(bf16).reshape(lay.H, lay.L, WIDTH // lay.dp, value.shape[1])

    def open_rows(tile, carry):
        rows = pl.ds(pl.multiple_of(tile * ROWS, ROWS), ROWS)
        middle = x_ref[rows, :].astype(f32) + mm(mixed_ref[rows, :], weight(woq_ref, 0), 1, 1)
        grad_ref[rows, :] = middle
        normed, _ = normalize(middle)
        second_ref[rows, :] = (normed * gain_second).astype(bf16)
        return carry

    def feed_rows(feed_ref, rows, total, second_grad):
        second, cot = second_ref[rows, :], cot_ref[rows, :]
        for part in range(feed_ref.shape[-1] // WIDTH):
            cols = slice(part * WIDTH, (part + 1) * WIDTH)
            up, down = weight(feed_ref, 0, cols), weight(feed_ref, 1, cols)
            pre = mm(second, up)
            act = jnp.maximum(pre, 0.0).astype(bf16)
            act_ref[rows, cols] = act
            total = total + mm(act, down, 1, 1)
            pre_grad = jnp.where(pre > 0, mm(cot, down), 0.0).astype(bf16)
            pre_ref[rows, cols] = pre_grad
            partial = mm(pre_grad, up, 1, 1)
            second_grad = partial if second_grad is None else second_grad + partial
        return total, second_grad

    def feed_a(tile, carry):
        rows = pl.ds(pl.multiple_of(tile * ROWS, ROWS), ROWS)
        total, second_grad = feed_rows(feed_a_ref, rows, grad_ref[rows, :], None)
        total_ref[rows, :] = total
        second_grad_ref[rows, :] = second_grad
        return carry

    def feed_b(tile, carry):
        rows = pl.ds(pl.multiple_of(tile * ROWS, ROWS), ROWS)
        total, second_grad = feed_rows(feed_b_ref, rows, total_ref[rows, :], second_grad_ref[rows, :])
        out_ref[rows, :] = total.astype(bf16)
        normed, inverse = normalize(grad_ref[rows, :])
        grad_ref[rows, :] = cot_ref[rows, :].astype(f32) + norm_back(second_grad, normed, inverse, gain_second)
        gain_grad_ref[8:16, :] += jnp.sum((second_grad * normed).reshape(ROWS // 8, 8, WIDTH), axis=0)
        return carry

    def feed_weights(dfeed_ref):
        keep(dfeed_ref, 0, slice(None), mm(second_ref[...], pre_ref[...], 0, 0))
        keep(dfeed_ref, 1, slice(None), mm(cot_ref[...], act_ref[...], 0, 0))

    lax.fori_loop(0, TILES, open_rows, 0)
    gather_a.landed()
    lax.fori_loop(0, TILES, feed_a, 0)
    gather_b.landed()
    gather_b.stage(3)
    feed_weights(dfeed_a_ref)
    scatter_a.stage(0)
    gather_b.landed()
    lax.fori_loop(0, TILES // 2, feed_b, 0)
    scatter_a.fold(0)
    scatter_a.stage(1)
    lax.fori_loop(TILES // 2, TILES, feed_b, 0)
    write_out = pltpu.make_async_copy(out_ref, out_hbm, copy_sems.at[2])
    write_out.start()
    feed_weights(dfeed_b_ref)
    scatter_b.stage(0)
    keep(dwo_ref, 0, slice(None), mm(grad_ref[...].astype(bf16), mixed_ref[...], 0, 0))

    scatter_wo.stage(0)

    def start(tile, carry):
        rows = pl.ds(pl.multiple_of(tile * ROWS, ROWS), ROWS)
        mixed_ref[rows, :] = mm(grad_ref[rows, :].astype(bf16), weight(woq_ref, 0)).astype(bf16)
        return carry

    lax.fori_loop(0, TILES, start, 0)
    scatter_a.fold(1)
    scatter_a.stage(2)
    scatter_b.fold(0)
    scatter_b.stage(1)
    scatter_wo.fold(0)
    scatter_wo.stage(1)

    def attend_back(step, carry):
        units = [(step * UNROLL + k, group) for k in range(UNROLL) for group in range(GROUPS)]

        def mixed_pack(block, group):
            return by_pack(mixed_ref[block_rows(block), group * LANES : (group + 1) * LANES])

        for block, group in units:
            rows, at = block_rows(block), group * LANES
            keys, values = operands(block, group)
            attention = att_ref[block, group]
            prob_grad = mm(values, mixed_pack(block, group), 1, 1)
            inner = jnp.sum(attention * prob_grad, axis=0, keepdims=True)
            score_grad = (attention * (prob_grad - inner) * (HEAD_DIM ** -0.5)).astype(bf16)
            pre_ref[rows, WIDTH + at : WIDTH + at + PAIRS] = score_grad[:BLOCK]
            pre_ref[rows, WIDTH + at + PAIRS : WIDTH + at + 2 * PAIRS] = score_grad[BLOCK:]
            pre_ref[rows, at : at + LANES] = own_heads(mm(score_grad, keys, 0, 0)).astype(bf16)
        for block, group in units:
            rows, at = block_rows(block), group * LANES
            lanes = slice(at, at + LANES)
            score_grad = jnp.concatenate(
                [pre_ref[rows, WIDTH + at : WIDTH + at + PAIRS], pre_ref[rows, WIDTH + at + PAIRS : WIDTH + at + 2 * PAIRS]],
                axis=0,
            )
            key_grad = mm(score_grad, by_pack(q_ref[rows, lanes]))
            value_grad = mm(att_ref[block, group].astype(bf16), mixed_pack(block, group))
            dk_ref[rows, lanes] = key_grad[:BLOCK]
            dv_ref[rows, lanes] = value_grad[:BLOCK]
            act_ref[rows, lanes] = key_grad[BLOCK:].astype(bf16)
            act_ref[rows, WIDTH + at : WIDTH + at + LANES] = value_grad[BLOCK:].astype(bf16)
        return carry

    lax.fori_loop(0, steps, attend_back, 0)
    first = first_ref[...]
    q_ref[...] = pre_ref[:, :WIDTH]
    keep(dq_ref, 0, slice(None), mm(first, q_ref[...], 0, 0))
    scatter_q.stage(0)
    weights = sink_ref[2 * SINK_ITERS - 1]
    same_head = iota((LOGITS, LOGITS), 0) // BLOCKS == iota((LOGITS, LOGITS), 1) // BLOCKS
    turned = jnp.where(same_head, jnp.concatenate([weights] * HEADS, axis=0), 0.0).T

    def back(head):
        rows = slice(head * BLOCKS, (head + 1) * BLOCKS)
        return repeated(turned[rows, rows].astype(bf16))

    sk_ref[...] = by_place(act_ref[:, :WIDTH])
    sv_ref[...] = by_place(act_ref[:, WIDTH:])

    def add_pair(lanes, keys, values):
        k_ref[:, lanes] = (dk_ref[:, lanes] + by_place(keys)).astype(bf16)
        v_ref[:, lanes] = (dv_ref[:, lanes] + by_place(values)).astype(bf16)

    rearrange(back, sk_ref, sv_ref, add_pair)
    scatter_b.fold(1)
    scatter_b.stage(2)
    scatter_q.fold(0)
    scatter_q.stage(1)
    dkv = mm(first, jnp.concatenate([k_ref[...], v_ref[...]], axis=1), 0, 0)
    keep(dkv_ref, 0, slice(None), dkv[:, :WIDTH])
    keep(dkv_ref, 1, slice(None), dkv[:, WIDTH:])
    scatter_kv.stage(0)
    scatter_wo.fold(1)
    scatter_wo.stage(2)
    lane_head = iota((SPAN, PAIR), 1) // HEAD_DIM
    diagonal = iota((SPAN, SPAN), 0) // BLOCKS == iota((SPAN, SPAN), 1) // BLOCKS
    folded = []
    for pair in range(HEADS // 2):
        lanes = slice(pair * PAIR, (pair + 1) * PAIR)
        parts = [slice(part * SPAN, (part + 1) * SPAN) for part in range(SEQ_LEN // SPAN)]
        right = [ref[rows, lanes] for rows in parts for ref in (place_k_ref, place_v_ref)]
        left = [ref[rows, lanes] for rows in parts for ref in (sk_ref, sv_ref)]
        for head in range(2):
            mine = [jnp.where(lane_head == head, tile, jnp.zeros_like(tile)) for tile in left]
            square = mm(jnp.concatenate(mine, axis=1), jnp.concatenate(right, axis=1), 1, 1)
            square = jnp.where(diagonal, square, 0.0)
            total = square[:BLOCKS]
            for place in range(1, STACK):
                total = total + square[place * BLOCKS : (place + 1) * BLOCKS]
            folded.append(total)
    copies = (iota((BLOCKS, LOGITS), 0) == iota((BLOCKS, LOGITS), 1) % BLOCKS).astype(bf16)
    stacked = exact_dot(jnp.concatenate(folded, axis=0), copies.T)
    wide = jnp.where(same_head, exact_dot(stacked, copies), 0.0)
    probs_grad = wide[:BLOCKS]
    for head in range(1, HEADS):
        probs_grad = probs_grad + wide[head * BLOCKS : (head + 1) * BLOCKS]
    logs = logs_ref[...]
    pull = jnp.where(real_col > 0, entropy_weight * (logs + 1.0), 0.0)
    scatter_kv.fold(0)
    scatter_kv.stage(1)
    grad = sinkhorn_back(weights * (probs_grad - pull), group_matrix(), lambda index: sink_ref[index])
    logit_grad = jnp.where(allowed, grad / softness_factor, 0.0).astype(bf16)
    sorter_grad = mm(means_ref[...], logit_grad, 0, 0).astype(bf16)
    for index, rows, cols in sorter_places():
        pieces = [sorter_grad[rows[k], cols] for k in range(pack)]
        dsorter_full[index] = jnp.concatenate(pieces, axis=1) if pack > 1 else pieces[0]
    scatter_sorter.stage(0)
    scatter_b.fold(2)
    scatter_b.stage(3)
    scatter_a.fold(2)
    scatter_a.stage(3)
    spread_ref[...] = mm(logit_grad, sorter_ref[...], 1, 1) / BLOCK
    here = ROWS // BLOCK

    def finish(tile, carry):
        rows = pl.ds(pl.multiple_of(tile * ROWS, ROWS), ROWS)
        spread = spread_ref[pl.ds(pl.multiple_of(tile * here, here), here), :]
        spread = jnp.broadcast_to(spread[:, None, :], (here, BLOCK, WIDTH)).reshape(ROWS, WIDTH)
        first_grad = (
            mm(q_ref[rows, :], weight(woq_ref, 1), 1, 1)
            + mm(k_ref[rows, :], weight(kv_ref, 0), 1, 1)
            + mm(v_ref[rows, :], weight(kv_ref, 1), 1, 1)
            + spread
        )
        normed, inverse = normalize(x_ref[rows, :].astype(f32))
        grad_ref[rows, :] += norm_back(first_grad, normed, inverse, gain_first)
        gain_grad_ref[0:8, :] += jnp.sum((first_grad * normed).reshape(ROWS // 8, 8, WIDTH), axis=0)
        return carry

    writes = []

    def write_rows(part):
        rows = slice(part * SEQ_LEN // 2, (part + 1) * SEQ_LEN // 2)
        copy = pltpu.make_async_copy(grad_ref.at[rows], grad_hbm.at[rows], copy_sems.at[3 + part])
        copy.start()
        writes.append(copy)

    lax.fori_loop(0, TILES // 2, finish, 0)
    write_rows(0)
    scatter_q.fold(1)
    scatter_q.stage(2)
    scatter_wo.fold(2)
    scatter_wo.stage(3)
    scatter_sorter.fold(0)
    scatter_sorter.stage(1)
    lax.fori_loop(TILES // 2, TILES, finish, 0)
    write_rows(1)
    entropy = -jnp.sum(jnp.where(real_col > 0, weights * logs, 0.0), axis=0, keepdims=True)
    entropy = jnp.broadcast_to(entropy[:, :128] + entropy[:, 128:], (8, 128))
    total_b.over_mp(jnp.concatenate([
        spread_rows(jnp.sum(gain_grad_ref[0:8, :], axis=0, keepdims=True)),
        spread_rows(jnp.sum(gain_grad_ref[8:16, :], axis=0, keepdims=True)),
        entropy,
    ], axis=0))
    scatter_kv.fold(1)
    scatter_kv.stage(2)
    scatter_q.fold(2)
    scatter_q.stage(3)
    scatter_sorter.fold(1)
    scatter_sorter.stage(2)
    total_b.over_dp()
    scatter_kv.fold(2)
    scatter_kv.stage(3)
    scatter_sorter.fold(2)
    scatter_sorter.stage(3)
    scatter_a.fold(3)
    scatter_b.fold(3)
    write_sums[0].start()
    small_out[0:16, :] = total_b.result()
    small_out[16:24, :] = summed[8:16]
    write_sums[3].start()
    scatter_wo.fold(3)
    scatter_q.fold(3)
    write_out.wait()
    for copy in writes:
        copy.wait()
    each(tuple(gather) + (scatter_a, scatter_b, scatter_wo, total_a, total_b), "close")
    scatter_kv.fold(3)
    write_sums[1].start()
    scatter_sorter.fold(3)
    write_sums[2].start()
    each((scatter_q, scatter_kv, scatter_sorter), "close")
    for copy in write_sums:
        copy.wait()


def update_kernel(lay, step_ref, *refs):
    sources, targets, penalty_out, inputs, results = refs[:18], refs[18:32], refs[32], refs[33:51], refs[51:63]
    in_sems, out_sems, row_sems = refs[63:]
    bring = [pltpu.make_async_copy(source, inputs[k], in_sems.at[k]) for k, source in enumerate(sources) if k > 1]
    send = [
        pltpu.make_async_copy(buffer, targets[2 + k], out_sems.at[2 + k]) for k, buffer in enumerate(results)
    ]
    bring_rows, send_rows = [], []
    for part in range(ROW_PARTS):
        for which in range(2):
            rows = slice(part * SEQ_LEN // ROW_PARTS, (part + 1) * SEQ_LEN // ROW_PARTS)
            sem = row_sems.at[part, which]
            bring_rows.append(pltpu.make_async_copy(sources[which].at[rows], inputs[which].at[rows], sem.at[0]))
            send_rows.append(pltpu.make_async_copy(inputs[which].at[rows], targets[which].at[rows], sem.at[1]))
    begin(bring_rows[:2] + bring + bring_rows[2:])
    feed_sum, mixer_sum, sorter_sum, sums = inputs[2:6]
    masters = inputs[6:]
    step_value = jnp.full((1, 128), step_ref[0], jnp.int32).astype(f32)
    scale_first = 1.0 / (1.0 - jnp.exp(step_value * math.log(beta_first)))[:, 0:1]
    scale_second = 1.0 / (1.0 - jnp.exp(step_value * math.log(beta_second)))[:, 0:1]

    def adamw(which, grad, rate):
        master, moment, second = [ref[...] for ref in masters[3 * which : 3 * which + 3]]
        moment_new = beta_first * moment + (1.0 - beta_first) * grad
        second_new = beta_second * second + (1.0 - beta_second) * grad * grad
        change = (moment_new * scale_first) / (jnp.sqrt(second_new * scale_second) + adam_eps)
        outs = results[3 * which : 3 * which + 3]
        outs[0][...] = moment_new
        outs[1][...] = second_new
        outs[2][...] = master - rate * (change + weight_decay * master)
        begin(send[3 * which : 3 * which + 3])

    for copy, onward in zip(bring_rows[:2], send_rows[:2]):
        copy.wait()
        onward.start()
    for copy in bring:
        copy.wait()
    adamw(1, feed_sum[...], rate_feed)
    adamw(0, mixer_sum[...], rate_mixer)
    adamw(2, sorter_sum[...], rate_sorter)
    for copy, onward in zip(bring_rows[2:], send_rows[2:]):
        copy.wait()
        onward.start()
    rows = jnp.concatenate([joined_row(sums[0:4, :]), joined_row(sums[4:8, :])], axis=0)
    own = spot(masters[9].shape[1])
    adamw(3, sum(mm(part, own, 1, 1) for part in three_parts(rows)), rate_gains)
    entropy = jnp.sum(sums[8:9, :], axis=1, keepdims=True)
    penalty_out[...] = jnp.broadcast_to(entropy / (sums[16:17, 0:1] * HEADS), (1, 128))
    for copy in send + send_rows:
        copy.wait()


def flat_rows(array):
    if array.ndim != 3 or array.shape[2] % 128:
        return array
    rows, parts, width = array.shape
    return array.reshape(rows, parts, width // 128, 128).transpose(0, 2, 1, 3).reshape(-1, 128)


def unflat_rows(flat, like):
    if flat.shape == like.shape:
        return flat
    rows, parts, width = like.shape
    return flat.reshape(rows, width // 128, parts, 128).transpose(0, 2, 1, 3).reshape(like.shape)


def shape(dims, dtype):
    return jax.ShapeDtypeStruct(dims, dtype)


LIMIT = 65400 * 1024
TOK = (SEQ_LEN, WIDTH)


def run_step(lay, total_tokens, tokens, cotangent, segment_ids, gains, mixer, feed, sorter):
    r, c, half = mixer.shape[0], mixer.shape[2], feed.shape[2] // 2
    pack = packing(*sorter.shape)
    sorter_item = Item(lay, 1, sorter.shape[0] // pack, sorter.shape[1] * pack)
    feed_item, pair_item, one_item = Item(lay, 2, r, half), Item(lay, 2, r, c), Item(lay, 1, r, c)
    gathers = (pair_item, sorter_item, pair_item, feed_item, feed_item)
    scatters = (feed_item, feed_item, one_item, one_item, pair_item, sorter_item)
    sums = [shape(jax.eval_shape(flat_rows, array).shape, f32) for array in (feed, mixer, sorter)]
    sums.append(shape((24, 128), f32))
    vm = pltpu.VMEM
    recvs = 5 * Gather.count(lay) + 6 * Scatter.count(lay) + 2 * Total.count(lay)
    sends = 5 * Gather.sends(lay) + 6 * Scatter.sends(lay) + 2 * Total.sends(lay)
    scratch = (
        [vm(item.shard(), bf16) for item in gathers]
        + [vm(item.full(), bf16) for item in gathers + scatters]
        + [vm(TOK, bf16), vm(TOK, bf16), vm(TOK, bf16), vm(TOK, f32)]
        + [vm((WIDTH, LOGITS), bf16)]
        + [vm(TOK, bf16)] * 8
        + [
            vm((BLOCKS, GROUPS, 2 * BLOCK, PAIRS), f32), vm(TOK, bf16), vm((BLOCKS, WIDTH), bf16),
            vm((2 * SINK_ITERS, BLOCKS, LOGITS), f32), vm((BLOCKS, LOGITS), f32),
            vm((BLOCKS, PAIRS), f32), vm((BLOCKS, WIDTH), f32), vm((16, WIDTH), f32),
            vm(TOK, bf16), vm((SEQ_LEN, HIDDEN // 2), bf16), vm((SEQ_LEN, HIDDEN // 2), bf16),
        ]
        + [vm(TOK, f32)] * 2
        + [vm((lay.mp, 16, 128), f32), vm((lay.dp, 16, 128), f32)] * 2
        + [pltpu.SemaphoreType.DMA((sends,)), pltpu.SemaphoreType.DMA((recvs,))]
        + [pltpu.SemaphoreType.DMA((14,))]
        + [vm(mixer.shape, f32), vm(feed.shape, f32), vm(sorter.shape, f32)]
        + [vm(total.shape, f32) for total in sums]
    )
    for k, item in enumerate(scatters):
        scratch += Scatter.buffers(item, k > 0)
    inside = pl.BlockSpec(memory_space=pltpu.VMEM)
    outside = pl.BlockSpec(memory_space=pl.ANY)
    return pl.pallas_call(
        functools.partial(step_kernel, lay, gathers, scatters, total_tokens),
        out_shape=[shape(TOK, bf16), shape(TOK, f32)]
        + sums,
        in_specs=[outside] * 2 + [inside] * 2 + [outside] * 3,
        out_specs=[outside] * 6,
        scratch_shapes=scratch,
        compiler_params=pltpu.CompilerParams(collective_id=0, has_side_effects=True, vmem_limit_bytes=LIMIT),
        name="step",
    )(tokens, cotangent, segment_ids, gains, mixer, feed, sorter)


def run_update(lay, step_count, block_output, token_grad, sums, states):
    outside = pl.BlockSpec(memory_space=pl.ANY)
    arrays = (block_output, token_grad, *sums, *states)
    moved = [shape(array.shape, array.dtype) for array in (block_output, token_grad, *states)]
    *moved, penalty = pl.pallas_call(
        functools.partial(update_kernel, lay),
        out_shape=moved + [shape((1, 128), f32)],
        in_specs=[pl.BlockSpec(memory_space=pltpu.SMEM)] + [outside] * len(arrays),
        out_specs=[outside] * len(moved) + [pl.BlockSpec(memory_space=pltpu.VMEM)],
        scratch_shapes=[pltpu.VMEM(array.shape, array.dtype) for array in arrays]
        + [pltpu.VMEM(state.shape, f32) for state in states]
        + [pltpu.SemaphoreType.DMA((len(arrays),)), pltpu.SemaphoreType.DMA((len(moved),))]
        + [pltpu.SemaphoreType.DMA((ROW_PARTS, 2, 2))],
        compiler_params=pltpu.CompilerParams(vmem_limit_bytes=LIMIT),
        name="update",
    )(step_count, *arrays)
    return moved[0], moved[1], penalty, moved[2:]


rate_mixer = 0.2
rate_feed = 0.1
rate_sorter = 0.6
rate_gains = 1.0
beta_first = 0.9
beta_second = 0.95
adam_eps = 1e-08
weight_decay = 0.1


def local(
    lay,
    tokens,
    segment_ids,
    cotangent,
    step_count,
    mixer_weights,
    mixer_moment,
    mixer_second,
    feed_weights,
    feed_moment,
    feed_second,
    sorter_weights,
    sorter_moment,
    sorter_second,
    norm_gains,
    gain_moment,
    gain_second,
):
    total_tokens = float(lay.dp * segment_ids.shape[0] * SEQ_LEN)
    block_output, token_grad, *sums = run_step(
        lay, total_tokens, tokens, cotangent, segment_ids, norm_gains, mixer_weights, feed_weights, sorter_weights
    )
    states = (
        mixer_weights, mixer_moment, mixer_second, feed_weights, feed_moment, feed_second,
        sorter_weights, sorter_moment, sorter_second, norm_gains, gain_moment, gain_second,
    )
    flat = [flat_rows(state) for state in states]
    block_output, token_grad, penalty, flat = run_update(lay, step_count, block_output, token_grad, sums, flat)
    states = [unflat_rows(new, state) for new, state in zip(flat, states)]
    return (block_output, token_grad, penalty[0, :1], *states)


def solution(mesh):
    return jax.shard_map(
        functools.partial(local, Layout(mesh.shape["dp"], mesh.shape["mp"])),
        mesh=mesh,
        in_specs=(
            P(("dp", "mp"), None),
            P("dp", None),
            P(("dp", "mp"), None),
            P(),
            P("dp", None, "mp"),
            P("dp", None, "mp"),
            P("dp", None, "mp"),
            P("dp", None, "mp"),
            P("dp", None, "mp"),
            P("dp", None, "mp"),
            P("dp", "mp"),
            P("dp", "mp"),
            P("dp", "mp"),
            P(None, ("dp", "mp")),
            P(None, ("dp", "mp")),
            P(None, ("dp", "mp")),
        ),
        out_specs=(
            P(("dp", "mp"), None),
            P(("dp", "mp"), None),
            P(),
            P("dp", None, "mp"),
            P("dp", None, "mp"),
            P("dp", None, "mp"),
            P("dp", None, "mp"),
            P("dp", None, "mp"),
            P("dp", None, "mp"),
            P("dp", "mp"),
            P("dp", "mp"),
            P("dp", "mp"),
            P(None, ("dp", "mp")),
            P(None, ("dp", "mp")),
            P(None, ("dp", "mp")),
        ),
        check_vma=False,
    )
```

```python
import functools
import math
import jax
import jax.numpy as jnp
from jax import lax
from jax.sharding import PartitionSpec as P
from jax.experimental import pallas as pl
from jax.experimental.pallas import tpu as pltpu

WIDTH = 512
HEADS = 8
HEAD_DIM = 64
HIDDEN = 2048
BLOCK = 32
SINK_ITERS = 8
SEQ_LEN = 1024
BLOCKS = 32
LOGITS = HEADS * BLOCKS
ROWS = 512
TILES = SEQ_LEN // ROWS
PACK = 4
GROUPS = HEADS // PACK
LANES = PACK * HEAD_DIM
PAIRS = PACK * BLOCK
PAIR = 2 * HEAD_DIM
UNROLL = 32
ROW_PARTS = 2

norm_eps = 1e-05
softness_factor = 0.75
excluded_fill = -1000000000.0
penalty_weight = 0.1
bf16 = jnp.bfloat16
f32 = jnp.float32


def mm(a, b, ca=1, cb=0):
    return lax.dot_general(a, b, (((ca,), (cb,)), ((), ())), preferred_element_type=f32)


def iota(shape, dim):
    return lax.broadcasted_iota(jnp.int32, shape, dim)


def normalize(rows):
    centred = rows - jnp.mean(rows, axis=-1, keepdims=True)
    inverse = lax.rsqrt(jnp.mean(centred * centred, axis=-1, keepdims=True) + norm_eps)
    return centred * inverse, inverse


def norm_back(grad_out, normed, inverse, gain):
    scaled = grad_out * gain
    return inverse * (
        scaled
        - jnp.mean(scaled, axis=-1, keepdims=True)
        - normed * jnp.mean(scaled * normed, axis=-1, keepdims=True)
    )


def three_parts(value):
    high = value.astype(bf16)
    rest = value - high.astype(f32)
    mid = rest.astype(bf16)
    low = (rest - mid.astype(f32)).astype(bf16)
    return high, mid, low


def group_matrix():
    return (iota((LOGITS, LOGITS), 0) // BLOCKS == iota((LOGITS, LOGITS), 1) // BLOCKS).astype(bf16)


def exact_dot(value, matrix):
    rows = value.shape[0]
    out = mm(jnp.concatenate(three_parts(value), axis=0), matrix)
    return out[:rows] + out[rows : 2 * rows] + out[2 * rows :]


def head_max(value):
    lane_head = iota(value.shape, 1) // BLOCKS
    out = jnp.zeros_like(value)
    for head in range(HEADS):
        here = lane_head == head
        top = jnp.max(jnp.where(here, value, -jnp.inf), axis=1, keepdims=True)
        out = jnp.where(here, top, out)
    return out


def permitted(real_col, real_row):
    col = iota((BLOCKS, LOGITS), 1) % BLOCKS
    return ((real_col * real_row) > 0) | (iota((BLOCKS, LOGITS), 0) == col)


def sinkhorn(logits, allowed, groups, store):
    logs = jnp.where(allowed, logits / softness_factor, excluded_fill)
    top = head_max(logs)
    logs = logs - (top + jnp.log(exact_dot(jnp.exp(logs - top), groups)))
    store(0, jnp.exp(logs))
    top = jnp.max(logs, axis=0, keepdims=True)
    logs = logs - (top + jnp.log(jnp.sum(jnp.exp(logs - top), axis=0, keepdims=True)))
    weights = jnp.exp(logs)
    store(1, weights)
    for sweep in range(1, SINK_ITERS):
        logs = logs - jnp.log(exact_dot(weights, groups))
        weights = jnp.exp(logs)
        store(2 * sweep, weights)
        logs = logs - jnp.log(jnp.sum(weights, axis=0, keepdims=True))
        weights = jnp.exp(logs)
        store(2 * sweep + 1, weights)
    return logs, weights


def sinkhorn_back(grad, groups, load):
    for sweep in reversed(range(SINK_ITERS)):
        grad = grad - load(2 * sweep + 1) * jnp.sum(grad, axis=0, keepdims=True)
        grad = grad - load(2 * sweep) * exact_dot(grad, groups)
    return grad


def by_pack(tile):
    rows = jnp.concatenate([tile] * PACK, axis=0)
    keep = iota((PAIRS, LANES), 0) // BLOCK == iota((PAIRS, LANES), 1) // HEAD_DIM
    return jnp.where(keep, rows, jnp.zeros_like(rows))


def own_heads(product):
    lane_head = iota((BLOCK, LANES), 1) // HEAD_DIM
    out = product[:BLOCK]
    for head in range(1, PACK):
        out = jnp.where(lane_head == head, product[head * BLOCK : (head + 1) * BLOCK], out)
    return out


STACK = 8
SPAN = STACK * BLOCKS


def by_place(rows):
    lanes = rows.shape[1]
    return jnp.swapaxes(rows.reshape(BLOCKS, BLOCK, lanes), 0, 1).reshape(SEQ_LEN, lanes)


def repeated(matrix):
    wide = jnp.concatenate([matrix] * STACK, axis=1)
    wide = jnp.concatenate([wide] * STACK, axis=0)
    keep = iota((SPAN, SPAN), 0) // BLOCKS == iota((SPAN, SPAN), 1) // BLOCKS
    return jnp.where(keep, wide, jnp.zeros_like(wide))


MESH = pl.DeviceIdType.MESH


class Layout:
    def __init__(self, mesh_dp, mesh_mp):
        self.dp, self.mp = mesh_dp, mesh_mp
        self.C = 2 if mesh_mp % 2 == 0 else 1
        self.X = mesh_mp // self.C
        self.L = 2 if mesh_dp % 2 == 0 else 1
        self.H = mesh_dp // self.L

    def here(self):
        dp, mp = lax.axis_index("dp"), lax.axis_index("mp")
        return dp // self.L, dp % self.L, mp // self.C, mp % self.C


class Item:
    def __init__(self, lay, J, r, c):
        self.lay, self.J, self.r, self.c = lay, J, r, c
        self.direct = c % 128 == 0
        self.half = r // 2

    def shard(self):
        return (self.J, self.r, self.c)

    def dims(self, *lead, rows=None, wide=None):
        rows = self.r if rows is None else rows
        wide = self.lay.mp if wide is None else wide
        if self.direct:
            return (self.J, *lead, rows, wide * self.c)
        return (self.J, *lead, wide, rows, self.c)

    def full(self):
        return self.dims(self.lay.H, self.lay.L)

    def at(self, lead, first, count=1, rows=slice(None)):
        if self.direct:
            start = first * self.c if isinstance(first, int) else pl.multiple_of(first * self.c, 128)
            return (slice(None), *lead, rows, pl.ds(start, count * self.c))
        return (slice(None), *lead, first if count == 1 else pl.ds(first, count), rows, slice(None))

    def rows_a(self):
        return slice(0, self.half)

    def rows_b(self):
        return slice(self.half, self.r)


ALLR = slice(None)


class Sems:
    def __init__(self, send, recv):
        self.send, self.recv = send, recv
        self.sends, self.recvs = 0, 0

    def lane(self, count):
        return Lane(self, count)


class Lane:
    def __init__(self, sems, count):
        self.sems, self.first, self.waiting = sems, sems.sends, []
        sems.sends += count

    def send(self, copies):
        self.close()
        for k, (src, dst, device) in enumerate(copies):
            self.waiting.append(
                pltpu.make_async_remote_copy(
                    src_ref=src,
                    dst_ref=dst,
                    send_sem=self.sems.send.at[self.first + k],
                    recv_sem=self.sems.recv.at[self.sems.recvs + k],
                    device_id=device,
                    device_id_type=MESH,
                )
            )
        self.sems.recvs += len(copies)
        return begin(list(self.waiting))

    def close(self):
        for copy in self.waiting:
            copy.wait_send()
        self.waiting = []


def begin(copies):
    for copy in copies:
        copy.start()
    return copies


def arrive(copies):
    for copy in copies:
        copy.wait_recv()


class Gather:
    def __init__(self, item, shard, full, sems, high_first=True):
        self.item, self.shard, self.full, self.high_first = item, shard, full, high_first
        self.lane = sems.lane(self.sends(item.lay, high_first))

    def stage(self, number):
        item, lay, full = self.item, self.item.lay, self.full
        h, l, x, c = lay.here()
        copies = []

        def to(hh, ll, xx, cc):
            return (hh * lay.L + ll, xx * lay.C + cc)

        def same(index, device):
            copies.append((full.at[index], full.at[index], device))

        mine = c * lay.X + x
        if number == 0 and not self.high_first:
            for rows, index, devices in (
                (item.rows_a(), item.at((h, l), mine, 1, item.rows_a()), [to(h, (l + k) % lay.L, x, c) for k in range(1, lay.L)]),
                (item.rows_b(), item.at((h, l), mine, 1, item.rows_b()), [to(h, l, (x + k) % lay.X, c) for k in range(1, lay.X)]),
            ):
                copies += [(self.shard.at[:, rows], full.at[index], device) for device in devices]
        if number == 1 and not self.high_first:
            for k in range(1, lay.H):
                device = to((h + k) % lay.H, l, x, c)
                same(item.at((h, ALLR), mine, 1, item.rows_a()), device)
                same(item.at((h, l), c * lay.X, lay.X, item.rows_b()), device)
        if number == 0 and self.high_first:
            for k in range(1, lay.H):
                copies.append((self.shard, full.at[item.at((h, l), mine)], to((h + k) % lay.H, l, x, c)))
        if number == 1 and self.high_first:
            for k in range(1, lay.L):
                same(item.at((ALLR, l), mine, 1, item.rows_a()), to(h, (l + k) % lay.L, x, c))
            for k in range(1, lay.X):
                same(item.at((ALLR, l), mine, 1, item.rows_b()), to(h, l, (x + k) % lay.X, c))
        if number == 2:
            for k in range(1, lay.X):
                same(item.at((ALLR, ALLR), mine, 1, item.rows_a()), to(h, l, (x + k) % lay.X, c))
            for k in range(1, lay.L):
                same(item.at((ALLR, l), c * lay.X, lay.X, item.rows_b()), to(h, (l + k) % lay.L, x, c))
        if number == 3:
            for k in range(1, lay.C):
                same(item.at((ALLR, ALLR), c * lay.X, lay.X), to(h, l, x, (c + k) % lay.C))
        self.flying = self.lane.send(copies)

    def place(self):
        h, l, x, c = self.item.lay.here()
        self.full[self.item.at((h, l), c * self.item.lay.X + x)] = self.shard[...]

    def landed(self):
        arrive(self.flying)

    def close(self):
        self.lane.close()

    @staticmethod
    def sends(lay, high_first):
        return max((lay.H - 1) * (1 if high_first else 2), lay.L + lay.X - 2, lay.C - 1)

    @staticmethod
    def count(lay, high_first):
        return (lay.H - 1) * (1 if high_first else 2) + 2 * (lay.L + lay.X - 2) + (lay.C - 1)


class Scatter:
    def __init__(self, item, full, buffers, write, sems, high_last=True):
        self.item, self.full, self.write, self.high_last = item, full, write, high_last
        self.lane = sems.lane(self.sends(item.lay))
        self.core, self.one_a, self.one_b, self.two_a, self.two_b, self.top_a, self.top_b = buffers

    @staticmethod
    def buffers(item, high_last=True):
        lay = item.lay
        half = item.half
        if not high_last:
            return Scatter.buffers(item)[:3] + [
                pltpu.VMEM((lay.H - 1, *item.dims(lay.L, rows=half, wide=1)), bf16),
                pltpu.VMEM((lay.H - 1, *item.dims(rows=half, wide=lay.X)), bf16),
                pltpu.VMEM((lay.L - 1, *item.dims(rows=half, wide=1)), bf16),
                pltpu.VMEM((lay.X - 1, *item.dims(rows=half, wide=1)), bf16),
            ]
        return [
            pltpu.VMEM((lay.C - 1, *item.dims(lay.H, lay.L, wide=lay.X)), bf16),
            pltpu.VMEM((lay.X - 1, *item.dims(lay.H, lay.L, rows=half, wide=1)), bf16),
            pltpu.VMEM((lay.L - 1, *item.dims(lay.H, rows=half, wide=lay.X)), bf16),
            pltpu.VMEM((lay.L - 1, *item.dims(lay.H, rows=half, wide=1)), bf16),
            pltpu.VMEM((lay.X - 1, *item.dims(lay.H, rows=half, wide=1)), bf16),
            pltpu.VMEM((lay.H - 1, *item.dims(rows=half, wide=1)), bf16),
            pltpu.VMEM((lay.H - 1, *item.dims(rows=half, wide=1)), bf16),
        ]

    def stage(self, number):
        item, lay = self.item, self.item.lay
        h, l, x, c = lay.here()
        copies = []

        def to(hh, ll, xx, cc):
            return (hh * lay.L + ll, xx * lay.C + cc)

        def send(src, src_index, dst, dst_index, device):
            copies.append((src.at[src_index], dst.at[dst_index], device))

        if number == 0:
            for k in range(1, lay.C):
                cc = (c + k) % lay.C
                send(
                    self.full, item.at((ALLR, ALLR), cc * lay.X, lay.X),
                    self.core, (k - 1, *item.at((ALLR, ALLR), 0, lay.X)),
                    to(h, l, x, cc),
                )
        if number == 1:
            for k in range(1, lay.X):
                xx = (x + k) % lay.X
                send(
                    self.core, (0, *item.at((ALLR, ALLR), xx, 1, item.rows_a())),
                    self.one_a, (k - 1, *item.at((ALLR, ALLR), 0)),
                    to(h, l, xx, c),
                )
            for k in range(1, lay.L):
                ll = (l + k) % lay.L
                send(
                    self.core, (0, *item.at((ALLR, ll), 0, lay.X, item.rows_b())),
                    self.one_b, (k - 1, *item.at((ALLR,), 0, lay.X)),
                    to(h, ll, x, c),
                )
        if number == 2 and not self.high_last:
            for k in range(1, lay.H):
                hh = (h + k) % lay.H
                send(
                    self.one_a, (0, *item.at((hh, ALLR), 0)),
                    self.two_a, (k - 1, *item.at((ALLR,), 0)),
                    to(hh, l, x, c),
                )
                send(
                    self.one_b, (0, *item.at((hh,), 0, lay.X)),
                    self.two_b, (k - 1, *item.at((), 0, lay.X)),
                    to(hh, l, x, c),
                )
        if number == 3 and not self.high_last:
            for k in range(1, lay.L):
                ll = (l + k) % lay.L
                send(
                    self.two_a, (0, *item.at((ll,), 0)),
                    self.top_a, (k - 1, *item.at((), 0)),
                    to(h, ll, x, c),
                )
            for k in range(1, lay.X):
                xx = (x + k) % lay.X
                send(
                    self.two_b, (0, *item.at((), xx)),
                    self.top_b, (k - 1, *item.at((), 0)),
                    to(h, l, xx, c),
                )
        if number == 2 and self.high_last:
            for k in range(1, lay.L):
                ll = (l + k) % lay.L
                send(
                    self.one_a, (0, *item.at((ALLR, ll), 0)),
                    self.two_a, (k - 1, *item.at((ALLR,), 0)),
                    to(h, ll, x, c),
                )
            for k in range(1, lay.X):
                xx = (x + k) % lay.X
                send(
                    self.one_b, (0, *item.at((ALLR,), xx)),
                    self.two_b, (k - 1, *item.at((ALLR,), 0)),
                    to(h, l, xx, c),
                )
        if number == 3 and self.high_last:
            for k in range(1, lay.H):
                hh = (h + k) % lay.H
                for src, dst in ((self.two_a, self.top_a), (self.two_b, self.top_b)):
                    send(src, (0, *item.at((hh,), 0)), dst, (k - 1, *item.at((), 0)), to(hh, l, x, c))
        self.flying = self.lane.send(copies)

    def fold(self, number):
        item, lay = self.item, self.item.lay
        h, l, x, c = lay.here()
        arrive(self.flying)

        def over_high(body):
            def step(high, carry):
                body(high)
                return carry

            lax.fori_loop(0, lay.H, step, 0)

        def add(target, index, source, source_index, extra):
            total = source[source_index].astype(f32) + target[(0, *index)].astype(f32)
            for other in range(1, extra):
                total = total + target[(other, *index)].astype(f32)
            target[(0, *index)] = total.astype(bf16)

        if number == 0:

            def core(high):
                for low in range(lay.L):
                    add(
                        self.core, item.at((high, low), 0, lay.X),
                        self.full, item.at((high, low), c * lay.X, lay.X), lay.C - 1,
                    )

            over_high(core)
        if number == 1:

            def one(high):
                for low in range(lay.L):
                    add(
                        self.one_a, item.at((high, low), 0),
                        self.core, (0, *item.at((high, low), x, 1, item.rows_a())), lay.X - 1,
                    )
                add(
                    self.one_b, item.at((high,), 0, lay.X),
                    self.core, (0, *item.at((high, l), 0, lay.X, item.rows_b())), lay.L - 1,
                )

            over_high(one)
        if number == 2 and not self.high_last:
            add(self.two_a, item.at((ALLR,), 0), self.one_a, (0, *item.at((h, ALLR), 0)), lay.H - 1)
            add(self.two_b, item.at((), 0, lay.X), self.one_b, (0, *item.at((h,), 0, lay.X)), lay.H - 1)
        if number == 2 and self.high_last:

            def two(high):
                add(self.two_a, item.at((high,), 0), self.one_a, (0, *item.at((high, l), 0)), lay.L - 1)
                add(self.two_b, item.at((high,), 0), self.one_b, (0, *item.at((high,), x)), lay.X - 1)

            over_high(two)
        if number == 3:
            own_a, own_b = item.at((h,), 0), item.at((h,), 0)
            if not self.high_last:
                own_a, own_b = item.at((l,), 0), item.at((), x)
            for rows, mine, own, others in (
                (item.rows_a(), self.two_a, own_a, self.top_a), (item.rows_b(), self.two_b, own_b, self.top_b),
            ):
                total = mine[(0, *own)].astype(f32)
                for other in range(others.shape[0]):
                    total = total + others[(other, *item.at((), 0))].astype(f32)
                total = total.reshape(item.J, item.half, item.c)
                for j in range(item.J):
                    self.write(j, rows, total[j])

    def close(self):
        self.lane.close()

    @staticmethod
    def sends(lay):
        return max(lay.C - 1, lay.X + lay.L - 2, 2 * (lay.H - 1))

    @staticmethod
    def count(lay):
        return (lay.C - 1) + 2 * (lay.X + lay.L - 2) + 2 * (lay.H - 1)


class Total:
    def __init__(self, lay, near, far, sems):
        self.lay, self.near, self.far = lay, near, far
        self.lane = sems.lane(self.sends(lay))

    def over_mp(self, value):
        dp, mp = lax.axis_index("dp"), lax.axis_index("mp")
        self.near[mp] = value
        self.flying = self.lane.send([
            (self.near.at[mp], self.near.at[mp], (dp, (mp + k) % self.lay.mp)) for k in range(1, self.lay.mp)
        ])

    def over_dp(self):
        dp, mp = lax.axis_index("dp"), lax.axis_index("mp")
        arrive(self.flying)
        total = self.near[0]
        for other in range(1, self.lay.mp):
            total = total + self.near[other]
        self.far[dp] = total
        self.flying = self.lane.send([
            (self.far.at[dp], self.far.at[dp], ((dp + k) % self.lay.dp, mp)) for k in range(1, self.lay.dp)
        ])

    def result(self):
        arrive(self.flying)
        total = self.far[0]
        for other in range(1, self.lay.dp):
            total = total + self.far[other]
        return total

    def close(self):
        self.lane.close()

    @staticmethod
    def sends(lay):
        return max(lay.mp, lay.dp) - 1

    @staticmethod
    def count(lay):
        return lay.mp - 1 + lay.dp - 1


def greet(lay):
    barrier = pltpu.get_barrier_semaphore()
    dp, mp = lax.axis_index("dp"), lax.axis_index("mp")
    for k in range(1, lay.mp):
        pl.semaphore_signal(barrier, inc=1, device_id=(dp, (mp + k) % lay.mp), device_id_type=MESH)
    for k in range(1, lay.dp):
        pl.semaphore_signal(barrier, inc=1, device_id=((dp + k) % lay.dp, mp), device_id_type=MESH)


def await_all(lay):
    pl.semaphore_wait(pltpu.get_barrier_semaphore(), lay.mp + lay.dp - 2)


def spread_rows(row):
    return jnp.concatenate([row[:, at : at + 128] for at in range(0, row.shape[1], 128)], axis=0)


def joined_row(rows):
    return jnp.concatenate([rows[at : at + 1] for at in range(rows.shape[0])], axis=1)


def diagonal_column(row, count):
    same = iota((count, count), 0) == iota((count, count), 1)
    return jnp.sum(jnp.where(same, jnp.broadcast_to(row, (count, count)), 0.0), axis=1, keepdims=True)


def spot(width):
    at = (lax.axis_index("dp") * lax.axis_size("mp") + lax.axis_index("mp")) * width
    return (iota((width, WIDTH), 1) == iota((width, WIDTH), 0) + at).astype(bf16)


def packing(r, c):
    return 128 // c if c < 128 and (r * c // 128) % 16 == 0 else 1


def step_kernel(
    lay, gathers, scatter_items, total_tokens,
    tokens_ref, cotangent_ref, segment_ref, gains_in, mixer_hbm, feed_hbm, sorter_hbm,
    out_hbm, grad_hbm, *refs,
):
    sums_hbm, scratch = refs[:4], list(refs[4:])

    def pop(count):
        taken = scratch[:count]
        del scratch[:count]
        return taken

    shards, weights_full, grads_full = pop(5), pop(5), pop(6)
    kv_ref, sorter_full, woq_ref, feed_a_ref, feed_b_ref = weights_full
    dfeed_a_ref, dfeed_b_ref, dwo_ref, dq_ref, dkv_ref, dsorter_full = grads_full
    x_ref, cot_ref, out_ref, grad_ref = pop(4)
    (
        sorter_ref, first_ref, q_ref, k_ref, v_ref, sk_ref, sv_ref, place_k_ref, place_v_ref,
        att_ref, mixed_ref, means_ref, sink_ref, logs_ref, segrow_ref, spread_ref, gain_grad_ref,
        second_ref, act_ref, pre_ref, total_ref, second_grad_ref,
    ) = pop(22)
    dk_ref, dv_ref = total_ref, second_grad_ref
    near_a, far_a, near_b, far_b, send_sems, recv_sems, copy_sems = pop(7)
    sems = Sems(send_sems, recv_sems)
    fetch_x = pltpu.make_async_copy(tokens_ref, x_ref, copy_sems.at[0])
    fetch_cot = pltpu.make_async_copy(cotangent_ref, cot_ref, copy_sems.at[1])
    mixer_in, feed_in, sorter_in = pop(3)
    fetches = [
        pltpu.make_async_copy(source, target, copy_sems.at[5 + k])
        for k, (source, target) in enumerate(
            ((mixer_hbm, mixer_in), (sorter_hbm, sorter_in), (feed_hbm, feed_in))
        )
    ]
    begin(fetches)
    fetch_x.start()
    fetch_cot.start()
    mp = lax.axis_index("mp")
    greet(lay)
    gather = [
        Gather(item, shard, full, sems, k < 4)
        for k, (item, shard, full) in enumerate(zip(gathers, shards, weights_full))
    ]
    early = (gather[0], gather[1])
    gather_woq, gather_a, gather_b = gather[2:]
    scatters = []
    feed_sum, mixer_sum, sorter_sum, small_out = sums = pop(4)
    pack = packing(*sorter_sum.shape)

    def write_to(out, places, lane, lanes):
        def write(j, rows, value):
            place = places[j]
            if len(out.shape) == 3:
                out[rows, place, lane : lane + lanes] = value
                return
            tiles = feed_tiles if out is feed_sum else lanes // 128
            group = len(mixer_order) if out is mixer_sum else 2
            for tile in range(lanes // 128):
                start = rows.start * tiles * group + (lane // 128 + tile) * group + place
                out[pl.ds(start, rows.stop - rows.start, stride=tiles * group), :] = value[:, tile * 128 : (tile + 1) * 128]

        return write

    def write_sorter(j, rows, value):
        deep, c = sorter_sum.shape[0] // pack, sorter_sum.shape[1]
        for k in range(pack):
            sorter_sum[k * deep + rows.start : k * deep + rows.stop, :] = value[:, k * c : (k + 1) * c]

    mixer_order = (3, 0, 1, 2)
    half_width = scatter_items[0].c
    feed_tiles = 2 * half_width // 128
    writers = (
        write_to(feed_sum, (0, 1), 0, half_width),
        write_to(feed_sum, (0, 1), half_width, half_width),
        write_to(mixer_sum, mixer_order[:1], 0, scatter_items[2].c),
        write_to(mixer_sum, mixer_order[1:2], 0, scatter_items[2].c),
        write_to(mixer_sum, mixer_order[2:], 0, scatter_items[2].c),
        write_sorter,
    )
    for k, (item, full, write) in enumerate(zip(scatter_items, grads_full, writers)):
        scatters.append(Scatter(item, full, pop(7), write, sems, k > 0))
    write_sums = [
        pltpu.make_async_copy(buffer, target, copy_sems.at[8 + k])
        for k, (buffer, target) in enumerate(zip(sums, sums_hbm))
    ]
    scatter_a, scatter_b, scatter_wo, scatter_q, scatter_kv, scatter_sorter = scatters
    total_a = Total(lay, near_a, far_a, sems)
    total_b = Total(lay, near_b, far_b, sems)

    def each(group, name, *args):
        for member in group:
            getattr(member, name)(*args)

    width = gains_in.shape[1]
    lane = iota((BLOCKS, SEQ_LEN), 1)
    row = segment_ref[pl.ds(mp, 1), :].astype(f32)
    picked = jnp.where(lane // BLOCK == iota((BLOCKS, SEQ_LEN), 0), jnp.broadcast_to(row, (BLOCKS, SEQ_LEN)), 0.0)
    seg = picked[:, :PAIRS]
    for at in range(PAIRS, SEQ_LEN, PAIRS):
        seg = seg + picked[:, at : at + PAIRS]
    tiling = (iota((PAIRS, PAIRS), 0) % BLOCK == iota((PAIRS, PAIRS), 1) % BLOCK).astype(bf16)
    seg = exact_dot(seg, tiling)
    segrow_ref[...] = seg
    real_col = (seg[:, 0:1] > 0).astype(f32)
    count = jnp.broadcast_to(jnp.sum(real_col, axis=0, keepdims=True), (8, 128))
    placed = exact_dot(gains_in[...], spot(width))
    small = jnp.concatenate([spread_rows(placed[0:1]), spread_rows(placed[1:2]), count], axis=0)
    for fetch in fetches:
        fetch.wait()
    for j, source in enumerate((1, 2)):
        shards[0][j] = mixer_in[:, source, :].astype(bf16)
    deep = sorter_in.shape[0] // pack
    sorter_shard = sorter_in[...].astype(bf16)
    shards[1][0] = jnp.concatenate([sorter_shard[k * deep : (k + 1) * deep] for k in range(pack)], axis=1)
    for j, source in enumerate((3, 0)):
        shards[2][j] = mixer_in[:, source, :].astype(bf16)
    for j in range(2):
        shards[3][j] = feed_in[:, j, :half_width].astype(bf16)
        shards[4][j] = feed_in[:, j, half_width:].astype(bf16)
    each(gather, "place")
    lane_block = iota((BLOCKS, LOGITS), 1) % BLOCKS
    real_row = jnp.sum(jnp.where(iota((BLOCKS, LOGITS), 0) == lane_block, real_col, 0.0), axis=0, keepdims=True)
    allowed = permitted(real_col, real_row)
    await_all(lay)
    each(early, "stage", 0)
    total_a.over_mp(small)
    gather_woq.stage(0)
    gather_b.stage(0)
    fetch_x.wait()

    def norm_rows(tile, carry):
        rows = pl.ds(pl.multiple_of(tile * ROWS, ROWS), ROWS)
        total_ref[rows, :] = normalize(x_ref[rows, :].astype(f32))[0]
        return carry

    lax.fori_loop(0, TILES, norm_rows, 0)
    total_a.over_dp()
    each(early, "landed")
    each(early, "stage", 1)
    gather_a.stage(0)
    each(early, "landed")
    each(early, "stage", 2)
    gather_woq.landed()
    gather_woq.stage(1)
    summed = total_a.result()
    gain_first = joined_row(summed[0:4])
    gain_second = joined_row(summed[4:8])
    entropy_weight = penalty_weight * total_tokens / (summed[8:9, 0:1] * HEADS)

    def norm_first(tile, carry):
        rows = pl.ds(pl.multiple_of(tile * ROWS, ROWS), ROWS)
        first_ref[rows, :] = (total_ref[rows, :] * gain_first).astype(bf16)
        return carry

    lax.fori_loop(0, TILES, norm_first, 0)
    member = (iota((BLOCKS, SEQ_LEN), 0) == iota((BLOCKS, SEQ_LEN), 1) // BLOCK).astype(bf16)
    means = (mm(member, first_ref[...]) / BLOCK).astype(bf16)
    means_ref[...] = means
    each(early, "landed")
    each(early, "stage", 3)
    gather_woq.landed()
    gather_woq.stage(2)
    gather_a.landed()
    gather_a.stage(1)
    gather_b.landed()
    gather_b.stage(1)
    early[1].landed()

    def weight(ref, j, cols=slice(None)):
        if len(ref.shape) == 6:
            parts = [ref[j, :, :, part].reshape(WIDTH, ref.shape[-1]) for part in range(lay.mp)]
            return jnp.concatenate(parts, axis=1)
        tile = ref[j, :, :, :, cols]
        return tile.reshape(WIDTH, tile.shape[-1])

    r, c = sorter_in.shape

    def sorter_places():
        for high in range(lay.H):
            for low in range(lay.L):
                for part in range(lay.mp):
                    base = (high * lay.L + low) * r
                    if pack == 1:
                        index = (0, high, low, part)
                    else:
                        index = (0, high, low, slice(None), slice(part * 128, (part + 1) * 128))
                    rows = [slice(base + k * deep, base + (k + 1) * deep) for k in range(pack)]
                    yield index, rows, slice(part * c, (part + 1) * c)

    for index, rows, cols in sorter_places():
        tile = sorter_full[index]
        for k in range(pack):
            sorter_ref[rows[k], cols] = tile[:, k * c : (k + 1) * c]
    logits = mm(means, sorter_ref[...])
    def store(index, value):
        sink_ref[index] = value

    logs, weights = sinkhorn(logits, allowed, group_matrix(), store)
    logs_ref[...] = logs
    probs = weights.astype(bf16)
    early[0].landed()
    for tile in range(TILES):
        rows = slice(tile * ROWS, (tile + 1) * ROWS)
        k_ref[rows, :] = mm(first_ref[rows, :], weight(kv_ref, 0)).astype(bf16)
        v_ref[rows, :] = mm(first_ref[rows, :], weight(kv_ref, 1)).astype(bf16)

    place_k_ref[...] = by_place(k_ref[...])
    place_v_ref[...] = by_place(v_ref[...])
    gather_a.landed()
    gather_a.stage(2)
    gather_woq.landed()
    gather_woq.stage(3)
    first_head = iota((SPAN, 2 * PAIR), 1) % PAIR < HEAD_DIM

    def rearrange(matrices, keys, values, finish_pair):
        for pair in range(HEADS // 2):
            lanes = slice(pair * PAIR, (pair + 1) * PAIR)
            one, two = matrices(2 * pair), matrices(2 * pair + 1)
            outs = []
            for part in range(SEQ_LEN // SPAN):
                rows = slice(part * SPAN, (part + 1) * SPAN)
                both = jnp.concatenate([keys[rows, lanes], values[rows, lanes]], axis=1)
                outs.append(jnp.where(first_head, mm(one, both), mm(two, both)))
            out = jnp.concatenate(outs, axis=0)
            finish_pair(lanes, out[:, :PAIR], out[:, PAIR:])

    def forth(head):
        return repeated(probs[:, head * BLOCKS : (head + 1) * BLOCKS])

    def keep_sorted(lanes, keys, values):
        sk_ref[:, lanes] = by_place(keys.astype(bf16))
        sv_ref[:, lanes] = by_place(values.astype(bf16))

    rearrange(forth, place_k_ref, place_v_ref, keep_sorted)
    gather_woq.landed()

    def project_queries(tile, carry):
        rows = pl.ds(pl.multiple_of(tile * ROWS, ROWS), ROWS)
        q_ref[rows, :] = mm(first_ref[rows, :], weight(woq_ref, 1)).astype(bf16)
        return carry

    lax.fori_loop(0, TILES, project_queries, 0)

    def block_rows(block):
        return pl.ds(pl.multiple_of(block * BLOCK, BLOCK), BLOCK)

    def operands(block, group):
        rows = block_rows(block)
        lanes = slice(group * LANES, (group + 1) * LANES)
        keys = jnp.concatenate([k_ref[rows, lanes], sk_ref[rows, lanes]], axis=0)
        values = jnp.concatenate([v_ref[rows, lanes], sv_ref[rows, lanes]], axis=0)
        return keys, values

    def attend(step, carry):
        for block in [step * UNROLL + k for k in range(UNROLL)]:
            rows = block_rows(block)
            row = segrow_ref[pl.ds(block, 1), :]
            near = diagonal_column(row[:, :BLOCK], BLOCK) == row
            far = jnp.broadcast_to(row > 0, (BLOCK, PAIRS))
            mask = jnp.concatenate([near, far], axis=0)
            for group in range(GROUPS):
                lanes = slice(group * LANES, (group + 1) * LANES)
                keys, values = operands(block, group)
                scores = mm(keys, by_pack(q_ref[rows, lanes]), 1, 1) * (HEAD_DIM ** -0.5)
                scores = jnp.where(mask, scores, excluded_fill)
                shifted = jnp.exp(scores - jnp.max(scores, axis=0, keepdims=True))
                attention = shifted * (1.0 / jnp.sum(shifted, axis=0, keepdims=True))
                att_ref[block, group] = attention
                mixed_ref[rows, lanes] = own_heads(mm(attention.astype(bf16), values, 0, 0)).astype(bf16)
        return carry

    steps = BLOCKS // UNROLL
    lax.fori_loop(0, steps, attend, 0)
    gather_a.landed()
    gather_a.stage(3)
    gather_b.landed()
    gather_b.stage(2)
    fetch_cot.wait()
    gain_grad_ref[...] = jnp.zeros_like(gain_grad_ref)

    def keep(ref, j, cols, value):
        if len(ref.shape) == 6:
            for part in range(lay.mp):
                piece = value[:, part * ref.shape[-1] : (part + 1) * ref.shape[-1]]
                ref[j, :, :, part] = piece.astype(bf16).reshape(lay.H, lay.L, WIDTH // lay.dp, ref.shape[-1])
            return
        ref[j, :, :, :, cols] = value.astype(bf16).reshape(lay.H, lay.L, WIDTH // lay.dp, value.shape[1])

    def open_rows(tile, carry):
        rows = pl.ds(pl.multiple_of(tile * ROWS, ROWS), ROWS)
        middle = x_ref[rows, :].astype(f32) + mm(mixed_ref[rows, :], weight(woq_ref, 0), 1, 1)
        grad_ref[rows, :] = middle
        normed, _ = normalize(middle)
        second_ref[rows, :] = (normed * gain_second).astype(bf16)
        return carry

    def feed_rows(feed_ref, rows, total, second_grad):
        second, cot = second_ref[rows, :], cot_ref[rows, :]
        for part in range(feed_ref.shape[-1] // WIDTH):
            cols = slice(part * WIDTH, (part + 1) * WIDTH)
            up, down = weight(feed_ref, 0, cols), weight(feed_ref, 1, cols)
            pre = mm(second, up)
            act = jnp.maximum(pre, 0.0).astype(bf16)
            act_ref[rows, cols] = act
            total = total + mm(act, down, 1, 1)
            pre_grad = jnp.where(pre > 0, mm(cot, down), 0.0).astype(bf16)
            pre_ref[rows, cols] = pre_grad
            partial = mm(pre_grad, up, 1, 1)
            second_grad = partial if second_grad is None else second_grad + partial
        return total, second_grad

    def feed_a(tile, carry):
        rows = pl.ds(pl.multiple_of(tile * ROWS, ROWS), ROWS)
        total, second_grad = feed_rows(feed_a_ref, rows, grad_ref[rows, :], None)
        total_ref[rows, :] = total
        second_grad_ref[rows, :] = second_grad
        return carry

    def feed_b(tile, carry):
        rows = pl.ds(pl.multiple_of(tile * ROWS, ROWS), ROWS)
        total, second_grad = feed_rows(feed_b_ref, rows, total_ref[rows, :], second_grad_ref[rows, :])
        out_ref[rows, :] = total.astype(bf16)
        normed, inverse = normalize(grad_ref[rows, :])
        grad_ref[rows, :] = cot_ref[rows, :].astype(f32) + norm_back(second_grad, normed, inverse, gain_second)
        gain_grad_ref[8:16, :] += jnp.sum((second_grad * normed).reshape(ROWS // 8, 8, WIDTH), axis=0)
        return carry

    def feed_weights(dfeed_ref):
        keep(dfeed_ref, 0, slice(None), mm(second_ref[...], pre_ref[...], 0, 0))
        keep(dfeed_ref, 1, slice(None), mm(cot_ref[...], act_ref[...], 0, 0))

    lax.fori_loop(0, TILES, open_rows, 0)
    gather_a.landed()
    lax.fori_loop(0, TILES, feed_a, 0)
    gather_b.landed()
    gather_b.stage(3)
    feed_weights(dfeed_a_ref)
    scatter_a.stage(0)
    gather_b.landed()
    lax.fori_loop(0, TILES // 2, feed_b, 0)
    scatter_a.fold(0)
    scatter_a.stage(1)
    lax.fori_loop(TILES // 2, TILES, feed_b, 0)
    write_out = pltpu.make_async_copy(out_ref, out_hbm, copy_sems.at[2])
    write_out.start()
    feed_weights(dfeed_b_ref)
    scatter_b.stage(0)
    keep(dwo_ref, 0, slice(None), mm(grad_ref[...].astype(bf16), mixed_ref[...], 0, 0))

    scatter_wo.stage(0)

    def start(tile, carry):
        rows = pl.ds(pl.multiple_of(tile * ROWS, ROWS), ROWS)
        mixed_ref[rows, :] = mm(grad_ref[rows, :].astype(bf16), weight(woq_ref, 0)).astype(bf16)
        return carry

    lax.fori_loop(0, TILES, start, 0)
    scatter_a.fold(1)
    scatter_a.stage(2)
    scatter_b.fold(0)
    scatter_b.stage(1)
    scatter_wo.fold(0)
    scatter_wo.stage(1)

    def attend_back(step, carry):
        units = [(step * UNROLL + k, group) for k in range(UNROLL) for group in range(GROUPS)]

        def mixed_pack(block, group):
            return by_pack(mixed_ref[block_rows(block), group * LANES : (group + 1) * LANES])

        for block, group in units:
            rows, at = block_rows(block), group * LANES
            keys, values = operands(block, group)
            attention = att_ref[block, group]
            prob_grad = mm(values, mixed_pack(block, group), 1, 1)
            inner = jnp.sum(attention * prob_grad, axis=0, keepdims=True)
            score_grad = (attention * (prob_grad - inner) * (HEAD_DIM ** -0.5)).astype(bf16)
            pre_ref[rows, WIDTH + at : WIDTH + at + PAIRS] = score_grad[:BLOCK]
            pre_ref[rows, WIDTH + at + PAIRS : WIDTH + at + 2 * PAIRS] = score_grad[BLOCK:]
            pre_ref[rows, at : at + LANES] = own_heads(mm(score_grad, keys, 0, 0)).astype(bf16)
        for block, group in units:
            rows, at = block_rows(block), group * LANES
            lanes = slice(at, at + LANES)
            score_grad = jnp.concatenate(
                [pre_ref[rows, WIDTH + at : WIDTH + at + PAIRS], pre_ref[rows, WIDTH + at + PAIRS : WIDTH + at + 2 * PAIRS]],
                axis=0,
            )
            key_grad = mm(score_grad, by_pack(q_ref[rows, lanes]))
            value_grad = mm(att_ref[block, group].astype(bf16), mixed_pack(block, group))
            dk_ref[rows, lanes] = key_grad[:BLOCK]
            dv_ref[rows, lanes] = value_grad[:BLOCK]
            act_ref[rows, lanes] = key_grad[BLOCK:].astype(bf16)
            act_ref[rows, WIDTH + at : WIDTH + at + LANES] = value_grad[BLOCK:].astype(bf16)
        return carry

    lax.fori_loop(0, steps, attend_back, 0)
    first = first_ref[...]
    q_ref[...] = pre_ref[:, :WIDTH]
    keep(dq_ref, 0, slice(None), mm(first, q_ref[...], 0, 0))
    scatter_q.stage(0)
    weights = sink_ref[2 * SINK_ITERS - 1]
    same_head = iota((LOGITS, LOGITS), 0) // BLOCKS == iota((LOGITS, LOGITS), 1) // BLOCKS
    turned = jnp.where(same_head, jnp.concatenate([weights] * HEADS, axis=0), 0.0).T

    def back(head):
        rows = slice(head * BLOCKS, (head + 1) * BLOCKS)
        return repeated(turned[rows, rows].astype(bf16))

    sk_ref[...] = by_place(act_ref[:, :WIDTH])
    sv_ref[...] = by_place(act_ref[:, WIDTH:])

    def add_pair(lanes, keys, values):
        k_ref[:, lanes] = (dk_ref[:, lanes] + by_place(keys)).astype(bf16)
        v_ref[:, lanes] = (dv_ref[:, lanes] + by_place(values)).astype(bf16)

    rearrange(back, sk_ref, sv_ref, add_pair)
    scatter_b.fold(1)
    scatter_b.stage(2)
    scatter_q.fold(0)
    scatter_q.stage(1)
    dkv = mm(first, jnp.concatenate([k_ref[...], v_ref[...]], axis=1), 0, 0)
    keep(dkv_ref, 0, slice(None), dkv[:, :WIDTH])
    keep(dkv_ref, 1, slice(None), dkv[:, WIDTH:])
    scatter_kv.stage(0)
    scatter_wo.fold(1)
    scatter_wo.stage(2)
    lane_head = iota((SPAN, PAIR), 1) // HEAD_DIM
    diagonal = iota((SPAN, SPAN), 0) // BLOCKS == iota((SPAN, SPAN), 1) // BLOCKS
    folded = []
    for pair in range(HEADS // 2):
        lanes = slice(pair * PAIR, (pair + 1) * PAIR)
        parts = [slice(part * SPAN, (part + 1) * SPAN) for part in range(SEQ_LEN // SPAN)]
        right = [ref[rows, lanes] for rows in parts for ref in (place_k_ref, place_v_ref)]
        left = [ref[rows, lanes] for rows in parts for ref in (sk_ref, sv_ref)]
        for head in range(2):
            mine = [jnp.where(lane_head == head, tile, jnp.zeros_like(tile)) for tile in left]
            square = mm(jnp.concatenate(mine, axis=1), jnp.concatenate(right, axis=1), 1, 1)
            square = jnp.where(diagonal, square, 0.0)
            total = square[:BLOCKS]
            for place in range(1, STACK):
                total = total + square[place * BLOCKS : (place + 1) * BLOCKS]
            folded.append(total)
    copies = (iota((BLOCKS, LOGITS), 0) == iota((BLOCKS, LOGITS), 1) % BLOCKS).astype(bf16)
    stacked = exact_dot(jnp.concatenate(folded, axis=0), copies.T)
    wide = jnp.where(same_head, exact_dot(stacked, copies), 0.0)
    probs_grad = wide[:BLOCKS]
    for head in range(1, HEADS):
        probs_grad = probs_grad + wide[head * BLOCKS : (head + 1) * BLOCKS]
    logs = logs_ref[...]
    pull = jnp.where(real_col > 0, entropy_weight * (logs + 1.0), 0.0)
    scatter_kv.fold(0)
    scatter_kv.stage(1)
    grad = sinkhorn_back(weights * (probs_grad - pull), group_matrix(), lambda index: sink_ref[index])
    logit_grad = jnp.where(allowed, grad / softness_factor, 0.0).astype(bf16)
    sorter_grad = mm(means_ref[...], logit_grad, 0, 0).astype(bf16)
    for index, rows, cols in sorter_places():
        pieces = [sorter_grad[rows[k], cols] for k in range(pack)]
        dsorter_full[index] = jnp.concatenate(pieces, axis=1) if pack > 1 else pieces[0]
    scatter_sorter.stage(0)
    scatter_b.fold(2)
    scatter_b.stage(3)
    scatter_a.fold(2)
    scatter_a.stage(3)
    spread_ref[...] = mm(logit_grad, sorter_ref[...], 1, 1) / BLOCK
    here = ROWS // BLOCK

    def finish(tile, carry):
        rows = pl.ds(pl.multiple_of(tile * ROWS, ROWS), ROWS)
        spread = spread_ref[pl.ds(pl.multiple_of(tile * here, here), here), :]
        spread = jnp.broadcast_to(spread[:, None, :], (here, BLOCK, WIDTH)).reshape(ROWS, WIDTH)
        first_grad = (
            mm(q_ref[rows, :], weight(woq_ref, 1), 1, 1)
            + mm(k_ref[rows, :], weight(kv_ref, 0), 1, 1)
            + mm(v_ref[rows, :], weight(kv_ref, 1), 1, 1)
            + spread
        )
        normed, inverse = normalize(x_ref[rows, :].astype(f32))
        grad_ref[rows, :] += norm_back(first_grad, normed, inverse, gain_first)
        gain_grad_ref[0:8, :] += jnp.sum((first_grad * normed).reshape(ROWS // 8, 8, WIDTH), axis=0)
        return carry

    writes = []

    def write_rows(part):
        rows = slice(part * SEQ_LEN // 2, (part + 1) * SEQ_LEN // 2)
        copy = pltpu.make_async_copy(grad_ref.at[rows], grad_hbm.at[rows], copy_sems.at[3 + part])
        copy.start()
        writes.append(copy)

    lax.fori_loop(0, TILES // 2, finish, 0)
    write_rows(0)
    scatter_q.fold(1)
    scatter_q.stage(2)
    scatter_wo.fold(2)
    scatter_wo.stage(3)
    scatter_sorter.fold(0)
    scatter_sorter.stage(1)
    lax.fori_loop(TILES // 2, TILES, finish, 0)
    write_rows(1)
    entropy = -jnp.sum(jnp.where(real_col > 0, weights * logs, 0.0), axis=0, keepdims=True)
    entropy = jnp.broadcast_to(entropy[:, :128] + entropy[:, 128:], (8, 128))
    total_b.over_mp(jnp.concatenate([
        spread_rows(jnp.sum(gain_grad_ref[0:8, :], axis=0, keepdims=True)),
        spread_rows(jnp.sum(gain_grad_ref[8:16, :], axis=0, keepdims=True)),
        entropy,
    ], axis=0))
    scatter_kv.fold(1)
    scatter_kv.stage(2)
    scatter_q.fold(2)
    scatter_q.stage(3)
    scatter_sorter.fold(1)
    scatter_sorter.stage(2)
    total_b.over_dp()
    scatter_kv.fold(2)
    scatter_kv.stage(3)
    scatter_sorter.fold(2)
    scatter_sorter.stage(3)
    scatter_a.fold(3)
    scatter_b.fold(3)
    write_sums[0].start()
    small_out[0:16, :] = total_b.result()
    small_out[16:24, :] = summed[8:16]
    write_sums[3].start()
    scatter_wo.fold(3)
    scatter_q.fold(3)
    write_out.wait()
    for copy in writes:
        copy.wait()
    each(tuple(gather) + (scatter_a, scatter_b, scatter_wo, total_a, total_b), "close")
    scatter_kv.fold(3)
    write_sums[1].start()
    scatter_sorter.fold(3)
    write_sums[2].start()
    each((scatter_q, scatter_kv, scatter_sorter), "close")
    for copy in write_sums:
        copy.wait()


def update_kernel(lay, step_ref, *refs):
    sources, targets, penalty_out, inputs, results = refs[:18], refs[18:32], refs[32], refs[33:51], refs[51:63]
    in_sems, out_sems, row_sems = refs[63:]
    bring = [pltpu.make_async_copy(source, inputs[k], in_sems.at[k]) for k, source in enumerate(sources) if k > 1]
    send = [
        pltpu.make_async_copy(buffer, targets[2 + k], out_sems.at[2 + k]) for k, buffer in enumerate(results)
    ]
    bring_rows, send_rows = [], []
    for part in range(ROW_PARTS):
        for which in range(2):
            rows = slice(part * SEQ_LEN // ROW_PARTS, (part + 1) * SEQ_LEN // ROW_PARTS)
            sem = row_sems.at[part, which]
            bring_rows.append(pltpu.make_async_copy(sources[which].at[rows], inputs[which].at[rows], sem.at[0]))
            send_rows.append(pltpu.make_async_copy(inputs[which].at[rows], targets[which].at[rows], sem.at[1]))
    begin(bring_rows[:2] + bring + bring_rows[2:])
    feed_sum, mixer_sum, sorter_sum, sums = inputs[2:6]
    masters = inputs[6:]
    step_value = jnp.full((1, 128), step_ref[0], jnp.int32).astype(f32)
    scale_first = 1.0 / (1.0 - jnp.exp(step_value * math.log(beta_first)))[:, 0:1]
    scale_second = 1.0 / (1.0 - jnp.exp(step_value * math.log(beta_second)))[:, 0:1]

    def adamw(which, grad, rate):
        master, moment, second = [ref[...] for ref in masters[3 * which : 3 * which + 3]]
        moment_new = beta_first * moment + (1.0 - beta_first) * grad
        second_new = beta_second * second + (1.0 - beta_second) * grad * grad
        change = (moment_new * scale_first) / (jnp.sqrt(second_new * scale_second) + adam_eps)
        outs = results[3 * which : 3 * which + 3]
        outs[0][...] = moment_new
        outs[1][...] = second_new
        outs[2][...] = master - rate * (change + weight_decay * master)
        begin(send[3 * which : 3 * which + 3])

    for copy, onward in zip(bring_rows[:2], send_rows[:2]):
        copy.wait()
        onward.start()
    for copy in bring:
        copy.wait()
    adamw(1, feed_sum[...], rate_feed)
    adamw(0, mixer_sum[...], rate_mixer)
    adamw(2, sorter_sum[...], rate_sorter)
    for copy, onward in zip(bring_rows[2:], send_rows[2:]):
        copy.wait()
        onward.start()
    rows = jnp.concatenate([joined_row(sums[0:4, :]), joined_row(sums[4:8, :])], axis=0)
    own = spot(masters[9].shape[1])
    adamw(3, sum(mm(part, own, 1, 1) for part in three_parts(rows)), rate_gains)
    entropy = jnp.sum(sums[8:9, :], axis=1, keepdims=True)
    penalty_out[...] = jnp.broadcast_to(entropy / (sums[16:17, 0:1] * HEADS), (1, 128))
    for copy in send + send_rows:
        copy.wait()


def flat_rows(array):
    if array.ndim != 3 or array.shape[2] % 128:
        return array
    rows, parts, width = array.shape
    return array.reshape(rows, parts, width // 128, 128).transpose(0, 2, 1, 3).reshape(-1, 128)


def unflat_rows(flat, like):
    if flat.shape == like.shape:
        return flat
    rows, parts, width = like.shape
    return flat.reshape(rows, width // 128, parts, 128).transpose(0, 2, 1, 3).reshape(like.shape)


def shape(dims, dtype):
    return jax.ShapeDtypeStruct(dims, dtype)


LIMIT = 65400 * 1024
TOK = (SEQ_LEN, WIDTH)


def run_step(lay, total_tokens, tokens, cotangent, segment_ids, gains, mixer, feed, sorter):
    r, c, half = mixer.shape[0], mixer.shape[2], feed.shape[2] // 2
    pack = packing(*sorter.shape)
    sorter_item = Item(lay, 1, sorter.shape[0] // pack, sorter.shape[1] * pack)
    feed_item, pair_item, one_item = Item(lay, 2, r, half), Item(lay, 2, r, c), Item(lay, 1, r, c)
    gathers = (pair_item, sorter_item, pair_item, feed_item, feed_item)
    scatters = (feed_item, feed_item, one_item, one_item, pair_item, sorter_item)
    sums = [shape(jax.eval_shape(flat_rows, array).shape, f32) for array in (feed, mixer, sorter)]
    sums.append(shape((24, 128), f32))
    vm = pltpu.VMEM
    recvs = 4 * Gather.count(lay, True) + Gather.count(lay, False) + 6 * Scatter.count(lay) + 2 * Total.count(lay)
    sends = 4 * Gather.sends(lay, True) + Gather.sends(lay, False) + 6 * Scatter.sends(lay) + 2 * Total.sends(lay)
    scratch = (
        [vm(item.shard(), bf16) for item in gathers]
        + [vm(item.full(), bf16) for item in gathers + scatters]
        + [vm(TOK, bf16), vm(TOK, bf16), vm(TOK, bf16), vm(TOK, f32)]
        + [vm((WIDTH, LOGITS), bf16)]
        + [vm(TOK, bf16)] * 8
        + [
            vm((BLOCKS, GROUPS, 2 * BLOCK, PAIRS), f32), vm(TOK, bf16), vm((BLOCKS, WIDTH), bf16),
            vm((2 * SINK_ITERS, BLOCKS, LOGITS), f32), vm((BLOCKS, LOGITS), f32),
            vm((BLOCKS, PAIRS), f32), vm((BLOCKS, WIDTH), f32), vm((16, WIDTH), f32),
            vm(TOK, bf16), vm((SEQ_LEN, HIDDEN // 2), bf16), vm((SEQ_LEN, HIDDEN // 2), bf16),
        ]
        + [vm(TOK, f32)] * 2
        + [vm((lay.mp, 16, 128), f32), vm((lay.dp, 16, 128), f32)] * 2
        + [pltpu.SemaphoreType.DMA((sends,)), pltpu.SemaphoreType.DMA((recvs,))]
        + [pltpu.SemaphoreType.DMA((14,))]
        + [vm(mixer.shape, f32), vm(feed.shape, f32), vm(sorter.shape, f32)]
        + [vm(total.shape, f32) for total in sums]
    )
    for k, item in enumerate(scatters):
        scratch += Scatter.buffers(item, k > 0)
    inside = pl.BlockSpec(memory_space=pltpu.VMEM)
    outside = pl.BlockSpec(memory_space=pl.ANY)
    return pl.pallas_call(
        functools.partial(step_kernel, lay, gathers, scatters, total_tokens),
        out_shape=[shape(TOK, bf16), shape(TOK, f32)]
        + sums,
        in_specs=[outside] * 2 + [inside] * 2 + [outside] * 3,
        out_specs=[outside] * 6,
        scratch_shapes=scratch,
        compiler_params=pltpu.CompilerParams(collective_id=0, has_side_effects=True, vmem_limit_bytes=LIMIT),
        name="step",
    )(tokens, cotangent, segment_ids, gains, mixer, feed, sorter)


def run_update(lay, step_count, block_output, token_grad, sums, states):
    outside = pl.BlockSpec(memory_space=pl.ANY)
    arrays = (block_output, token_grad, *sums, *states)
    moved = [shape(array.shape, array.dtype) for array in (block_output, token_grad, *states)]
    *moved, penalty = pl.pallas_call(
        functools.partial(update_kernel, lay),
        out_shape=moved + [shape((1, 128), f32)],
        in_specs=[pl.BlockSpec(memory_space=pltpu.SMEM)] + [outside] * len(arrays),
        out_specs=[outside] * len(moved) + [pl.BlockSpec(memory_space=pltpu.VMEM)],
        scratch_shapes=[pltpu.VMEM(array.shape, array.dtype) for array in arrays]
        + [pltpu.VMEM(state.shape, f32) for state in states]
        + [pltpu.SemaphoreType.DMA((len(arrays),)), pltpu.SemaphoreType.DMA((len(moved),))]
        + [pltpu.SemaphoreType.DMA((ROW_PARTS, 2, 2))],
        compiler_params=pltpu.CompilerParams(vmem_limit_bytes=LIMIT),
        name="update",
    )(step_count, *arrays)
    return moved[0], moved[1], penalty, moved[2:]


rate_mixer = 0.2
rate_feed = 0.1
rate_sorter = 0.6
rate_gains = 1.0
beta_first = 0.9
beta_second = 0.95
adam_eps = 1e-08
weight_decay = 0.1


def local(
    lay,
    tokens,
    segment_ids,
    cotangent,
    step_count,
    mixer_weights,
    mixer_moment,
    mixer_second,
    feed_weights,
    feed_moment,
    feed_second,
    sorter_weights,
    sorter_moment,
    sorter_second,
    norm_gains,
    gain_moment,
    gain_second,
):
    total_tokens = float(lay.dp * segment_ids.shape[0] * SEQ_LEN)
    block_output, token_grad, *sums = run_step(
        lay, total_tokens, tokens, cotangent, segment_ids, norm_gains, mixer_weights, feed_weights, sorter_weights
    )
    states = (
        mixer_weights, mixer_moment, mixer_second, feed_weights, feed_moment, feed_second,
        sorter_weights, sorter_moment, sorter_second, norm_gains, gain_moment, gain_second,
    )
    flat = [flat_rows(state) for state in states]
    block_output, token_grad, penalty, flat = run_update(lay, step_count, block_output, token_grad, sums, flat)
    states = [unflat_rows(new, state) for new, state in zip(flat, states)]
    return (block_output, token_grad, penalty[0, :1], *states)


def solution(mesh):
    return jax.shard_map(
        functools.partial(local, Layout(mesh.shape["dp"], mesh.shape["mp"])),
        mesh=mesh,
        in_specs=(
            P(("dp", "mp"), None),
            P("dp", None),
            P(("dp", "mp"), None),
            P(),
            P("dp", None, "mp"),
            P("dp", None, "mp"),
            P("dp", None, "mp"),
            P("dp", None, "mp"),
            P("dp", None, "mp"),
            P("dp", None, "mp"),
            P("dp", "mp"),
            P("dp", "mp"),
            P("dp", "mp"),
            P(None, ("dp", "mp")),
            P(None, ("dp", "mp")),
            P(None, ("dp", "mp")),
        ),
        out_specs=(
            P(("dp", "mp"), None),
            P(("dp", "mp"), None),
            P(),
            P("dp", None, "mp"),
            P("dp", None, "mp"),
            P("dp", None, "mp"),
            P("dp", None, "mp"),
            P("dp", None, "mp"),
            P("dp", None, "mp"),
            P("dp", "mp"),
            P("dp", "mp"),
            P("dp", "mp"),
            P(None, ("dp", "mp")),
            P(None, ("dp", "mp")),
            P(None, ("dp", "mp")),
        ),
        check_vma=False,
    )
```
